32 devices in a mesh: group: 1, tile: 8 (over z, core), dp: 4 (over y, x).
Axes of the slice: x: 2, y: 2, z: 4, core: 2. Of those that a mesh axis runs over, the one named last changes fastest.
Arguments:
- activations: bfloat16 [4, 8, 24, 24, 128], P(('group', 'dp'), 'tile'), may hold values from -6 to 6
- cotangent: bfloat16 [4, 8, 24, 24, 128], P(('group', 'dp'), 'tile'), may hold values from -1.5 to 1.5
- kernel: bfloat16 [1152, 128], P('group'), may hold values from -0.1875 to 0.1875
- turning: int32 [8], P('tile'), may hold values from 0 to 3
- orient: int32 [8, 4], P('tile'), may hold values from 0 to 7, as said below
- left_factor: float32 [1152, 1152], P(('group', 'tile')), may hold values from -0.15 to 5.15
- left_basis: float32 [1152, 1152], P(('group', 'tile'), 'dp'), may hold values from -0.026516504 to 1.0265165
- right_factor: float32 [128, 128], P('group'), may hold values from -4.26 to 49.26
- right_basis: float32 [128, 128], P('group'), may hold values from -0.079549513 to 1.0795495
- momentum: float32 [1152, 128], P(('group', 'dp')), may hold values from -1.5 to 1.5
- second_moment: float32 [1152, 128], P(('group', 'dp')), may hold values from 0.02 to 0.2
Outputs:
- output: bfloat16 [4, 8, 24, 24, 128], P(('group', 'dp'), 'tile')
- input_grad: bfloat16 [4, 8, 24, 24, 128], P(('group', 'dp'), 'tile')
- kernel_grad: float32 [1152, 128], P('group')
- left_factor_new: float32 [1152, 1152], P(('group', 'tile'))
- left_basis_new: float32 [1152, 1152], P(('group', 'tile'))
- right_factor_new: float32 [128, 128], P('group')
- right_basis_new: float32 [128, 128], P('group')
- momentum_new: float32 [1152, 128], P(('group', 'dp'))
- second_new: float32 [1152, 128], P(('group', 'dp'))
- update: float32 [1152, 128], P(('group', 'tile'))
The draws below stay inside these ranges and needn't reach their ends.
Inputs may be any that keep to these rules, and one draw needn't show every extreme that they name: 0 where edge e of tile t leaves the patch; otherwise orient[t, e] % 4 is the edge of neighbor[t, e] that heads back to t, and 4 is added where the two edges' cell orders run opposite ways.
All inputs are finite; a program needn't handle non-finite values.
Results may differ from the reference program's by a relative error of at most 0.0025.
Values may be sent and summed in bfloat16 or wider, within the bound.
A program may use at most 128 MiB of HBM per device.

```python
import math
import jax
import jax.numpy as jnp
from jax import lax

C = 128
TS = 24
FL = 1152
NTILES = 8
BATCH = 4
CELLS = 18432


def tile_turns(key):
    return jax.random.randint(jax.random.fold_in(key, 12), (NTILES,), 0, 4).astype(jnp.int32)


def draw_turning(key, part):
    return tile_turns(key)


def draw_orient(key, part):
    count = NTILES
    turning = tile_turns(key)
    tile_ids = jnp.arange(count, dtype=jnp.int32)
    row_of = tile_ids // 4
    col_of = tile_ids % 4
    edges = jnp.arange(4, dtype=jnp.int32)[None, :]
    heading = (edges + turning[:, None]) % 4
    row_step = jnp.where(heading == 0, -1, jnp.where(heading == 2, 1, 0)).astype(jnp.int32)
    col_step = jnp.where(heading == 1, 1, jnp.where(heading == 3, -1, 0)).astype(jnp.int32)
    next_row = row_of[:, None] + row_step
    next_col = col_of[:, None] + col_step
    inside = (next_row >= 0) & (next_row < count // 4) & (next_col >= 0) & (next_col < 4)
    target = jnp.clip(next_row, 0, count // 4 - 1) * 4 + jnp.clip(next_col, 0, 3)
    target_turn = turning[target]
    their_edge = (heading + 2 - target_turn) % 4
    mine_dir = (1 + edges % 2 + turning[:, None]) % 4
    their_dir = (1 + their_edge % 2 + target_turn) % 4
    flip_flag = (mine_dir != their_dir).astype(jnp.int32)
    return jnp.where(inside, their_edge + 4 * flip_flag, 0).astype(jnp.int32)


def raw_noise(key, count):
    return jax.random.truncated_normal(key, -3.0, 3.0, (count, count), jnp.float32)


def symmetric_noise(key, count):
    noise = raw_noise(jax.random.fold_in(key, 5), count)
    return (noise + noise.T) * 0.5


def draw_left_factor(key, part):
    diagonal = jax.random.uniform(jax.random.fold_in(key, 3), (FL,), jnp.float32, 3.5, 5.0)
    return symmetric_noise(key, FL) * 0.05 + jnp.diag(diagonal)


def draw_right_factor(key, part):
    diagonal = jax.random.uniform(jax.random.fold_in(key, 3), (C,), jnp.float32, 30.0, 45.0)
    return symmetric_noise(key, C) * 1.42 + jnp.diag(diagonal)


def draw_left_basis(key, part):
    noise = raw_noise(jax.random.fold_in(key, 7), FL)
    return noise * (0.3 / math.sqrt(FL)) + jnp.eye(FL, dtype=jnp.float32)


def draw_right_basis(key, part):
    noise = raw_noise(jax.random.fold_in(key, 7), C)
    return noise * (0.3 / math.sqrt(C)) + jnp.eye(C, dtype=jnp.float32)


def block_scale(key, dims, shards, smallest, high):
    loudness, own = 1.0, jax.random.fold_in(key, 6)
    for position, shards_of in shards:
        steps = jnp.exp(jax.random.uniform(jax.random.fold_in(own, position), (shards_of,), jnp.float32, smallest / len(shards), high / len(shards)))
        loudness = loudness * jnp.repeat(steps, dims[position] // shards_of).reshape([-1 if axis == position else 1 for axis in range(len(dims))])
    return loudness


def gaussian(stream_key, extent, scale, reach, shards=(), held_as=jnp.bfloat16):
    entries = scale * jax.random.normal(stream_key, extent, jnp.float32)
    if shards:
        entries = entries * block_scale(stream_key, extent, shards, -0.22, 0.18)
    return jnp.clip(entries, -reach, reach).astype(held_as)


def setup_inputs(seed: int = 0, part: int = 0) -> dict:
    arg_keys = jax.random.split(jax.random.key(seed), 12)
    part_splits = jax.random.split(jax.random.fold_in(arg_keys[11], part), 12)
    return {
        "activations": gaussian(part_splits[0], (BATCH, NTILES, TS, TS, C), 1.0, 6.0, ((0, 4), (1, 8))),
        "cotangent": gaussian(part_splits[1], (BATCH, NTILES, TS, TS, C), 0.25, 1.5, ((0, 4), (1, 8))),
        "kernel": gaussian(part_splits[2], (FL, C), FL ** -0.5, 0.1875),
        "turning": draw_turning(jax.random.fold_in(arg_keys[11], 71), part),
        "orient": draw_orient(jax.random.fold_in(arg_keys[11], 71), part),
        "left_factor": draw_left_factor(jax.random.fold_in(jax.random.fold_in(arg_keys[11], part), 71), part),
        "left_basis": draw_left_basis(jax.random.fold_in(jax.random.fold_in(arg_keys[11], part), 71), part),
        "right_factor": draw_right_factor(jax.random.fold_in(jax.random.fold_in(arg_keys[11], part), 71), part),
        "right_basis": draw_right_basis(jax.random.fold_in(jax.random.fold_in(arg_keys[11], part), 71), part),
        "momentum": gaussian(part_splits[9], (FL, C), 0.25, 1.5, ((0, 4),), jnp.float32),
        "second_moment": jnp.clip(jnp.exp(math.log(0.2) - 2.3025851 * jax.random.uniform(part_splits[10], (FL, C), jnp.float32) ** block_scale(part_splits[10], (FL, C), ((0, 4),), -0.2, 0.2)), 0.02, 0.2),
    }


highest = lax.Precision.HIGHEST

def patch_layout(turning):
    count = turning.shape[0]
    tile_ids = jnp.arange(count, dtype=jnp.int32)
    row_of = tile_ids // 4
    col_of = tile_ids % 4
    heading = (jnp.arange(4, dtype=jnp.int32)[None, :] + turning[:, None]) % 4
    row_step = jnp.where(heading == 0, -1, jnp.where(heading == 2, 1, 0)).astype(jnp.int32)
    col_step = jnp.where(heading == 1, 1, jnp.where(heading == 3, -1, 0)).astype(jnp.int32)
    next_row = row_of[:, None] + row_step
    next_col = col_of[:, None] + col_step
    inside = (next_row >= 0) & (next_row < count // 4) & (next_col >= 0) & (next_col < 4)
    target = jnp.clip(next_row, 0, count // 4 - 1) * 4 + jnp.clip(next_col, 0, 3)
    return jnp.where(inside, target, -1).astype(jnp.int32)

def edge_strips(values):
    return jnp.stack([values[..., 0, :, :], values[..., :, -1, :], values[..., -1, :, :], values[..., :, 0, :]], axis=0)

def cycle_strips(spread):
    return jnp.stack([spread[:, 0, 1:-1], spread[:, 1:-1, -1], spread[:, -1, 1:-1], spread[:, 1:-1, 0]], axis=0)

def assemble(tile_vals, borders):
    middle = jnp.concatenate([borders[3][:, :, None, :], tile_vals, borders[1][:, :, None, :]], axis=2)
    top_row = jnp.pad(borders[0], ((0, 0), (1, 1), (0, 0)))[:, None]
    bottom_row = jnp.pad(borders[2], ((0, 0), (1, 1), (0, 0)))[:, None]
    return jnp.concatenate([top_row, middle, bottom_row], axis=1)

def tap_patches(padded, side):
    pieces = [padded[:, row_off:row_off + side, col_off:col_off + side, :] for row_off in range(3) for col_off in range(3)]
    joined = jnp.concatenate(pieces, axis=-1)
    return joined.reshape(-1, joined.shape[-1])

def spread_back(flat_grads, kernel, sample_count, side):
    channels = kernel.shape[1]
    summed = jnp.zeros((sample_count, side + 2, side + 2, channels), jnp.float32)
    for tap_index in range(9):
        row_off, col_off = divmod(tap_index, 3)
        weight_tap = kernel[tap_index * channels:(tap_index + 1) * channels]
        contrib = lax.dot_general(flat_grads.astype(jnp.float32), weight_tap.astype(jnp.float32), (((1,), (1,)), ((), ())), preferred_element_type=jnp.float32)
        contrib = contrib.reshape(sample_count, side, side, channels)
        summed = summed + jnp.pad(contrib, ((0, 0), (row_off, 2 - row_off), (col_off, 2 - col_off), (0, 0)))
    return summed

def absorb_rims(interior, incoming):
    result = interior.at[..., 0, :, :].add(incoming[0])
    result = result.at[..., :, -1, :].add(incoming[1])
    result = result.at[..., -1, :, :].add(incoming[2])
    return result.at[..., :, 0, :].add(incoming[3])

def route(strips, source, facing, flipped, usable):
    picked = strips[source, facing]
    picked = jnp.where(flipped[:, :, None, None, None], picked[:, :, :, ::-1, :], picked)
    return jnp.where(usable[:, :, None, None, None], picked, jnp.zeros_like(picked))

def orthonormal(power):
    gram = jnp.dot(power.T, power, precision=highest)
    lower = jnp.linalg.cholesky(gram)
    return lax.linalg.triangular_solve(lower, power.T, left_side=True, lower=True).T

def reference(activations, cotangent, kernel, turning, orient, left_factor, left_basis, right_factor, right_basis, momentum, second_moment):
    neighbor = patch_layout(turning)
    usable = neighbor >= 0
    source = jnp.where(usable, neighbor, 0).astype(jnp.int32)
    facing = (orient % 4).astype(jnp.int32)
    flipped = orient >= 4
    by_tile = jnp.swapaxes(activations, 0, 1)
    grads_tile = jnp.swapaxes(cotangent, 0, 1)
    strips = jnp.moveaxis(edge_strips(by_tile), 0, 1)
    borders = route(strips, source, facing, flipped, usable)

    def one_tile(inputs):
        tile_vals, tile_grads, tile_borders = inputs
        padded = assemble(tile_vals, tile_borders)
        columns = tap_patches(padded, TS)
        flat_grads = tile_grads.reshape(-1, C)
        result = jnp.dot(columns.astype(jnp.float32), kernel.astype(jnp.float32), preferred_element_type=jnp.float32).astype(jnp.bfloat16).reshape(tile_vals.shape)
        spread = spread_back(flat_grads, kernel, tile_vals.shape[0], TS)
        rim_cells = cycle_strips(spread).astype(jnp.bfloat16)
        interior = spread[:, 1:-1, 1:-1]
        partial_grad = lax.dot_general(columns.astype(jnp.float32), flat_grads.astype(jnp.float32), (((0,), (0,)), ((), ())), preferred_element_type=jnp.float32)
        return (result, interior, rim_cells, partial_grad)
    outputs, interiors, rims, partials = lax.map(one_tile, (by_tile, grads_tile, borders))
    incoming = route(rims, source, facing, flipped, usable).astype(jnp.float32)
    input_grad = absorb_rims(interiors, jnp.moveaxis(incoming, 1, 0)).astype(jnp.bfloat16)
    grad = lax.optimization_barrier(jnp.sum(partials, axis=0)) * (1.0 / math.sqrt(CELLS))
    left_new = 0.95 * left_factor + 0.05 * jnp.dot(grad, grad.T, precision=highest)
    right_new = 0.95 * right_factor + 0.05 * jnp.dot(grad.T, grad, precision=highest)
    basis_new = orthonormal(jnp.dot(left_new, left_basis, precision=highest))
    right_basis_new = orthonormal(jnp.dot(right_new, right_basis, precision=highest))
    back = jnp.dot(left_basis, momentum, precision=highest)
    right_turn = jnp.dot(right_basis.T, right_basis_new, precision=highest)
    rotated = jnp.dot(jnp.dot(basis_new.T, back, precision=highest), right_turn, precision=highest)
    projected = jnp.dot(jnp.dot(basis_new.T, grad, precision=highest), right_basis_new, precision=highest)
    momentum_new = 0.9 * rotated + 0.1 * projected
    second_new = 0.95 * second_moment + 0.05 * projected * projected
    normalized = momentum_new / (jnp.sqrt(second_new) + 1e-08)
    update = jnp.dot(jnp.dot(basis_new, normalized, precision=highest), right_basis_new.T, precision=highest)
    return (jnp.swapaxes(outputs, 0, 1), jnp.swapaxes(input_grad, 0, 1), grad, left_new, basis_new, right_new, right_basis_new, momentum_new, second_new, update)
```

```python
import math

import jax
import jax.numpy as jnp
from jax import lax
from jax.experimental import pallas as pl
from jax.experimental.pallas import tpu as pltpu
from jax.sharding import PartitionSpec as P

highest = lax.Precision.HIGHEST
epsilon = 1e-08


def edge_strips(values):
    return jnp.stack(
        [values[..., 0, :, :], values[..., :, -1, :], values[..., -1, :, :], values[..., :, 0, :]],
        axis=0,
    )


def cycle_strips(spread):
    return jnp.stack(
        [spread[:, 0, 1:-1], spread[:, 1:-1, -1], spread[:, -1, 1:-1], spread[:, 1:-1, 0]], axis=0
    )


def assemble(tile_vals, borders):
    middle = jnp.concatenate(
        [borders[3][:, :, None, :], tile_vals, borders[1][:, :, None, :]], axis=2
    )
    top_row = jnp.pad(borders[0], ((0, 0), (1, 1), (0, 0)))[:, None]
    bottom_row = jnp.pad(borders[2], ((0, 0), (1, 1), (0, 0)))[:, None]
    return jnp.concatenate([top_row, middle, bottom_row], axis=1)


def tap_patches(padded, side):
    pieces = [
        padded[:, row_off : row_off + side, col_off : col_off + side, :]
        for row_off in range(3)
        for col_off in range(3)
    ]
    joined = jnp.concatenate(pieces, axis=-1)
    return joined.reshape(-1, joined.shape[-1])


def spread_back(flat_grads, kernel, sample_count, side):
    channels = kernel.shape[1]
    summed = jnp.zeros((sample_count, side + 2, side + 2, channels), jnp.float32)
    for tap_index in range(9):
        row_off, col_off = divmod(tap_index, 3)
        weight_tap = kernel[tap_index * channels : (tap_index + 1) * channels]
        contrib = lax.dot_general(
            flat_grads, weight_tap, (((1,), (1,)), ((), ())), preferred_element_type=jnp.float32
        )
        contrib = contrib.reshape(sample_count, side, side, channels)
        summed = summed + jnp.pad(
            contrib, ((0, 0), (row_off, 2 - row_off), (col_off, 2 - col_off), (0, 0))
        )
    return summed


def absorb_rims(interior, incoming):
    result = interior.at[..., 0, :, :].add(incoming[0])
    result = result.at[..., :, -1, :].add(incoming[1])
    result = result.at[..., -1, :, :].add(incoming[2])
    return result.at[..., :, 0, :].add(incoming[3])


def flip_edges(strips, flipped):
    return jnp.where(flipped[:, None, None, None], strips[:, :, ::-1, :], strips)


def pick_gathered(everything, near_tiles, facing, flipped, usable):
    flat = everything.reshape(everything.shape[0] * 4, -1)
    wanted = jnp.where(usable, near_tiles * 4 + facing, -1)
    selector = (lax.broadcasted_iota(jnp.int32, (4, flat.shape[0]), 1) == wanted[:, None]).astype(
        jnp.bfloat16
    )
    picked = jnp.dot(selector, flat, preferred_element_type=jnp.float32).astype(jnp.bfloat16)
    return flip_edges(picked.reshape((4,) + everything.shape[2:]), flipped)


LEAF = 128
SPAN = 384


def split(value):
    high = value.astype(jnp.bfloat16)
    return high, (value - high.astype(jnp.float32)).astype(jnp.bfloat16)


def split_wide(value):
    high = lax.reduce_precision(value, 8, 7)
    return high.astype(jnp.bfloat16), (value - high).astype(jnp.bfloat16)


def dot3(left, right, dims=(((1,), (0,)), ((), ()))):
    def one(a, b):
        return lax.dot_general(a, b, dims, preferred_element_type=jnp.float32)

    return one(left[0], right[0]) + (one(left[0], right[1]) + one(left[1], right[0]))


by_rows = (((1,), (1,)), ((), ()))


def leaf_inverse(block, m_ref, s_ref):
    row = lax.broadcasted_iota(jnp.int32, (LEAF, LEAF), 0)
    col = lax.broadcasted_iota(jnp.int32, (LEAF, LEAF), 1)
    on_diag = row == col
    unit = jnp.where(on_diag, 1.0, 0.0)
    kept = jnp.where(on_diag, block, 0.0)
    across = lax.rsqrt(jnp.sum(kept, axis=0, keepdims=True))
    down = lax.rsqrt(jnp.sum(kept, axis=1, keepdims=True))
    scaled = block * across * down
    m_ref[...] = jnp.where(on_diag, down, jnp.where(row > col, -scaled * across, 0.0))
    pair = split(block)
    rough = m_ref[...].astype(jnp.bfloat16)
    turned = jnp.dot(rough, pair[0], preferred_element_type=jnp.float32).astype(jnp.bfloat16)
    gap = lax.dot_general(turned, rough, by_rows, preferred_element_type=jnp.float32) - unit
    low = jnp.where(row > col, gap, jnp.where(on_diag, 0.5 * gap, 0.0)).astype(jnp.bfloat16)
    m_ref[...] -= jnp.dot(low, rough, preferred_element_type=jnp.float32)

    def more(carry):
        step, error = carry
        return (step < 12) & (error > 1e-4)

    def refine(carry):
        step, _ = carry
        guess = m_ref[...]
        guess_pair = split(guess)
        turned = dot3(guess_pair, pair)
        gap = dot3(split(turned), guess_pair, by_rows) - unit
        error = jnp.max(jnp.abs(gap))
        low = jnp.where(row > col, gap, jnp.where(on_diag, 0.5 * gap, 0.0))
        m_ref[...] = guess - dot3(split(low), guess_pair)
        return step + 1, error

    _, error = lax.while_loop(more, refine, (jnp.int32(0), jnp.float32(1.0)))

    @pl.when(jnp.logical_not(error <= 1e-4))
    def _():
        s_ref[...] = block
        m_ref[...] = unit

        def eliminate(j, carry):
            work = s_ref[...]
            line = s_ref[pl.ds(j, 1), :]
            lane = lax.broadcasted_iota(jnp.int32, (1, LEAF), 1)
            scale = lax.rsqrt(jnp.sum(jnp.where(lane == j, line, 0.0), axis=1, keepdims=True))
            column = jnp.sum(jnp.where(col == j, work, 0.0), axis=1, keepdims=True)
            side = lax.broadcasted_iota(jnp.int32, (LEAF, 1), 0)
            column = jnp.where(side > j, column * scale, 0.0)
            s_ref[...] = work - column * (line * scale)
            mine = m_ref[pl.ds(j, 1), :] * scale
            m_ref[...] = m_ref[...] - column * mine
            m_ref[pl.ds(j, 1), :] = mine
            return carry

        lax.fori_loop(0, LEAF, eliminate, 0)


def factor_kernel(
    gram_ref, side_ref, small_ref, y_ref, small_out_ref, a_ref, uh, ul, uth, utl, yh, yl, m_ref, s_ref
):
    width = gram_ref.shape[1]
    blocks = width // LEAF
    spans = width // SPAN
    leaf_inverse(small_ref[...], m_ref, s_ref)
    small_out_ref[...] = m_ref[...]
    a_ref[...] = gram_ref[...]
    y_ref[...] = side_ref[...]

    def block_step(k, carry):
        k0 = pl.multiple_of(k * LEAF, LEAF)
        leaf_inverse(a_ref[pl.ds(k0, LEAF), pl.ds(k0, LEAF)], m_ref, s_ref)
        inverse = split(m_ref[...])
        for span in range(spans):
            part = slice(span * SPAN, (span + 1) * SPAN)

            @pl.when((span + 1) * SPAN > k0 + LEAF)
            def _():
                value = dot3(inverse, split(a_ref[pl.ds(k0, LEAF), part]))
                uh[:, part], ul[:, part] = split(value)
                uth[part, :], utl[part, :] = split(value.T)

        value = dot3(inverse, split(y_ref[pl.ds(k0, LEAF), :]))
        y_ref[pl.ds(k0, LEAF), :] = value
        yh[...], yl[...] = split(value)

        def row_step(i, inner):
            i0 = pl.multiple_of(i * LEAF, LEAF)
            left = uth[pl.ds(i0, LEAF), :], utl[pl.ds(i0, LEAF), :]
            for span in range(spans):
                part = slice(span * SPAN, (span + 1) * SPAN)

                @pl.when((span + 1) * SPAN > i0)
                def _():
                    a_ref[pl.ds(i0, LEAF), part] -= dot3(left, (uh[:, part], ul[:, part]))

            y_ref[pl.ds(i0, LEAF), :] -= dot3(left, (yh[...], yl[...]))
            return inner

        lax.fori_loop(k + 1, blocks, row_step, 0)
        return carry

    lax.fori_loop(0, blocks, block_step, 0)


def factor_solve(gram, side, small):
    width, columns = side.shape
    vmem = pl.BlockSpec(memory_space=pltpu.VMEM)
    half = jnp.bfloat16
    return pl.pallas_call(
        factor_kernel,
        out_shape=(
            jax.ShapeDtypeStruct(side.shape, jnp.float32),
            jax.ShapeDtypeStruct(small.shape, jnp.float32),
        ),
        in_specs=[vmem] * 3,
        out_specs=(vmem, vmem),
        scratch_shapes=[
            pltpu.VMEM((width, width), jnp.float32),
            pltpu.VMEM((LEAF, width), half),
            pltpu.VMEM((LEAF, width), half),
            pltpu.VMEM((width, LEAF), half),
            pltpu.VMEM((width, LEAF), half),
            pltpu.VMEM((LEAF, columns), half),
            pltpu.VMEM((LEAF, columns), half),
            pltpu.VMEM((LEAF, LEAF), jnp.float32),
            pltpu.VMEM((LEAF, LEAF), jnp.float32),
        ],
        compiler_params=pltpu.CompilerParams(vmem_limit_bytes=40 * 1024 * 1024),
        name="factor_solve",
    )(gram, side, small)


high = lax.Precision.HIGH
tn = (((0,), (0,)), ((), ()))


def sum_kernel(dp_count, tiles, x_ref, out_ref, near, part, far, *sems):
    dp_index = lax.axis_index("dp")
    tile_index = lax.axis_index("tile")
    dp_peers = [lax.rem(dp_index + step, dp_count) for step in range(1, dp_count)]
    tile_peers = [lax.rem(tile_index + step, tiles) for step in range(1, tiles)]
    barrier = pltpu.get_barrier_semaphore()
    for axis, peers in (("dp", dp_peers), ("tile", tile_peers)):
        for peer in peers:
            pl.semaphore_signal(
                barrier, inc=1, device_id={axis: peer}, device_id_type=pl.DeviceIdType.MESH
            )
    pl.semaphore_wait(barrier, dp_count + tiles - 2)

    def exchange(axis, peers, source, target, send, receive):
        copies = [
            pltpu.make_async_remote_copy(
                src_ref=source(peer),
                dst_ref=target(slot),
                send_sem=send.at[slot],
                recv_sem=receive.at[slot],
                device_id={axis: peer},
                device_id_type=pl.DeviceIdType.MESH,
            )
            for slot, peer in enumerate(peers)
        ]
        for copy in copies:
            copy.start()
        for copy in copies:
            copy.wait()

    exchange("dp", dp_peers, lambda peer: x_ref.at[peer], lambda slot: near.at[slot], *sems[0:2])
    total = x_ref[dp_index]
    for slot in range(dp_count - 1):
        total = total + near[slot]
    part[...] = total
    exchange("tile", tile_peers, lambda peer: part.at[peer], lambda slot: far.at[slot], *sems[2:4])
    total = part[tile_index]
    for slot in range(tiles - 1):
        total = total + far[slot]
    out_ref[dp_index, tile_index] = total
    own = out_ref.at[dp_index, tile_index]
    exchange("tile", tile_peers, lambda peer: own, lambda slot: own, *sems[4:6])
    slab = out_ref.at[dp_index]
    exchange("dp", dp_peers, lambda peer: slab, lambda slot: slab, *sems[6:8])


def sum_everywhere(value):
    tiles = lax.axis_size("tile")
    dp_count = lax.axis_size("dp")
    rows, columns = value.shape
    if tiles < 2 or dp_count < 2 or rows % (tiles * dp_count):
        return lax.psum(value, ("tile", "dp"))
    piece = rows // (tiles * dp_count)
    vmem = pl.BlockSpec(memory_space=pltpu.VMEM)
    wide = (dp_count, tiles, piece, columns)
    counts = [dp_count - 1] * 2 + [tiles - 1] * 4 + [dp_count - 1] * 2
    out = pl.pallas_call(
        lambda *refs: sum_kernel(dp_count, tiles, *refs),
        out_shape=jax.ShapeDtypeStruct(wide, jnp.float32),
        in_specs=[vmem],
        out_specs=vmem,
        scratch_shapes=[
            pltpu.VMEM((dp_count - 1, tiles, piece, columns), jnp.float32),
            pltpu.VMEM((tiles, piece, columns), jnp.float32),
            pltpu.VMEM((tiles - 1, piece, columns), jnp.float32),
            *[pltpu.SemaphoreType.DMA((count,)) for count in counts],
        ],
        compiler_params=pltpu.CompilerParams(collective_id=0, has_side_effects=True),
        name="sum_everywhere",
    )(value.reshape(wide))
    return out.reshape(rows, columns)


def body_plain(
    activations,
    cotangent,
    kernel,
    turning,
    orient,
    left_factor,
    left_basis,
    right_factor,
    right_basis,
    momentum,
    second_moment,
):
    tiles = lax.axis_size("tile")
    dp_count = lax.axis_size("dp")
    tile_index = lax.axis_index("tile")
    dp_index = lax.axis_index("dp")
    tile_vals = activations[:, 0]
    tile_grads = cotangent[:, 0]
    sample_count = tile_vals.shape[0]
    side = tile_vals.shape[1]
    channels = tile_vals.shape[-1]
    own_turn = turning[0]
    facing = orient[0] % 4
    flipped = orient[0] >= 4
    heading = (jnp.arange(4, dtype=jnp.int32) + own_turn) % 4
    row_of = tile_index // 4
    col_of = tile_index % 4
    room = jnp.stack([row_of > 0, col_of < 3, row_of < tiles // 4 - 1, col_of > 0])
    usable = (
        jnp.sum(
            jnp.where(
                heading[:, None] == jnp.arange(4, dtype=jnp.int32)[None, :], room[None, :], False
            ),
            axis=1,
        )
        > 0
    )
    offsets = jnp.array([-4, 1, 4, -1], dtype=jnp.int32)
    near_tiles = tile_index + jnp.sum(
        jnp.where(heading[:, None] == jnp.arange(4, dtype=jnp.int32)[None, :], offsets[None, :], 0),
        axis=1,
    )
    strips = edge_strips(tile_vals)
    flat_grads = tile_grads.reshape(-1, channels)
    spread = spread_back(flat_grads, kernel, sample_count, side)
    rim_cells = cycle_strips(spread).astype(jnp.bfloat16)
    everything = lax.all_gather(
        jnp.concatenate([strips, rim_cells], axis=0)[None], "tile", axis=0, tiled=True
    )
    borders = pick_gathered(everything[:, :4], near_tiles, facing, flipped, usable)
    incoming = pick_gathered(everything[:, 4:], near_tiles, facing, flipped, usable)
    padded = assemble(tile_vals, borders)
    columns = tap_patches(padded, side)
    partial_grad = lax.dot_general(
        columns, flat_grads, (((0,), (0,)), ((), ())), preferred_element_type=jnp.float32
    )
    summed_grad = sum_everywhere(partial_grad)
    result = jnp.dot(columns, kernel, preferred_element_type=jnp.float32).astype(jnp.bfloat16)
    result = result.reshape(activations.shape)
    input_grad = absorb_rims(spread[:, 1:-1, 1:-1], incoming.astype(jnp.float32)).astype(
        jnp.bfloat16
    )
    input_grad = input_grad.reshape(cotangent.shape)
    cells = dp_count * sample_count * tiles * side * side
    grad = summed_grad * (1.0 / math.sqrt(cells))
    rows_per, width = left_factor.shape
    row_start = tile_index * rows_per
    moment_rows = momentum.shape[0]
    moment_start = dp_index * moment_rows
    grad_rows = lax.dynamic_slice_in_dim(grad, row_start, rows_per, 0)
    left_new = 0.95 * left_factor + 0.05 * lax.dot_general(
        grad_rows, grad, (((1,), (1,)), ((), ())), precision=high
    )
    basis_rows = lax.all_gather(left_basis, "dp", axis=1, tiled=True)
    basis = lax.all_gather(basis_rows.astype(jnp.bfloat16), "tile", axis=0, tiled=True)
    moments = lax.all_gather(
        jnp.concatenate([momentum, second_moment], axis=1), "dp", axis=0, tiled=True
    )
    all_momentum, all_second = moments[:, :channels], moments[:, channels:]
    back_rows = jnp.dot(basis_rows, all_momentum, precision=highest)
    own_row = row_start + lax.broadcasted_iota(jnp.int32, left_factor.shape, 0)
    own_col = lax.broadcasted_iota(jnp.int32, left_factor.shape, 1)
    diagonal = jnp.sum(jnp.where(own_row == own_col, left_factor, 0.0), axis=1, keepdims=True)
    rest = jnp.broadcast_to(split_wide(diagonal)[1], (rows_per, LEAF))
    factor = lax.all_gather(
        jnp.concatenate(
            [left_factor.astype(jnp.bfloat16), *split_wide(back_rows), rest], axis=1
        ),
        "tile",
        axis=0,
        tiled=True,
    )
    back = factor[:, width : width + channels].astype(jnp.float32) + factor[
        :, width + channels : width + 2 * channels
    ].astype(jnp.float32)
    rest = factor[:, width + 2 * channels : width + 2 * channels + 1]
    factor = factor[:, :width]
    mapped = 0.95 * (
        jnp.dot(factor, basis, preferred_element_type=jnp.float32)
        + rest.astype(jnp.float32) * basis.astype(jnp.float32)
    )
    mapped_gram = lax.dot_general(mapped, mapped, tn, precision=high)
    mapped_back = lax.dot_general(mapped, back, tn, precision=high)
    crossed = sum(
        lax.dot_general(term, basis, tn, preferred_element_type=jnp.float32) for term in split_wide(grad)
    )
    mapped_grad = lax.dot_general(mapped, grad, tn, precision=high)
    grad_gram = lax.dot_general(grad, grad, tn, precision=high)
    grad_back = lax.dot_general(grad, back, tn, precision=high)
    weight = 0.05 * mapped_grad + 0.00125 * lax.dot_general(crossed, grad_gram, tn, precision=high)
    gram = mapped_gram + lax.dot_general(
        jnp.concatenate([weight.T, crossed], axis=0),
        jnp.concatenate([crossed, weight.T], axis=0),
        tn,
        precision=high,
    )
    power_rows = lax.dynamic_slice_in_dim(mapped, row_start, rows_per, 0) + 0.05 * jnp.dot(
        grad_rows, crossed, precision=high
    )
    power_side = jnp.concatenate([mapped_back, mapped_grad], axis=1) + 0.05 * lax.dot_general(
        crossed, jnp.concatenate([grad_back, grad_gram], axis=1), tn, precision=high
    )
    right_new = 0.95 * right_factor + 0.05 * grad_gram
    right_power = jnp.dot(right_new, right_basis, precision=high)
    right_gram = lax.dot_general(right_power, right_power, tn, precision=high)
    solved, right_inverse = factor_solve(
        gram, jnp.concatenate([power_side, power_rows.T], axis=1), right_gram
    )
    turned_momentum = solved[:, :channels]
    turned_grad = solved[:, channels : 2 * channels]
    basis_new = solved[:, 2 * channels :].T
    right_basis_new = lax.dot_general(
        right_power, right_inverse, (((1,), (1,)), ((), ())), precision=high
    )
    right_turn = lax.dot_general(right_basis, right_basis_new, tn, precision=high)
    rotated = jnp.dot(turned_momentum, right_turn, precision=high)
    projected = jnp.dot(turned_grad, right_basis_new, precision=high)
    momentum_all = 0.9 * rotated + 0.1 * projected
    second_all = 0.95 * all_second + 0.05 * projected * projected
    normalized = momentum_all / (jnp.sqrt(second_all) + epsilon)
    momentum_new = lax.dynamic_slice_in_dim(momentum_all, moment_start, moment_rows, 0)
    second_new = lax.dynamic_slice_in_dim(second_all, moment_start, moment_rows, 0)
    update_rows = jnp.dot(basis_new, normalized, precision=high)
    update = lax.dot_general(
        update_rows, right_basis_new, (((1,), (1,)), ((), ())), precision=high
    )
    return (
        result,
        input_grad,
        grad,
        left_new,
        basis_new,
        right_new,
        right_basis_new,
        momentum_new,
        second_new,
        update,
    )


ZS = 4
CORES = 2
DPS = 4
LANES = 384


def to_device(source, target, send, receive, **device):
    return pltpu.make_async_remote_copy(
        src_ref=source,
        dst_ref=target,
        send_sem=send,
        recv_sem=receive,
        device_id=device,
        device_id_type=pl.DeviceIdType.MESH,
    )


def greet():
    t = lax.axis_index("tile")
    d = lax.axis_index("dp")
    barrier = pltpu.get_barrier_semaphore()
    tiles = ZS * CORES
    for step in range(1, tiles):
        pl.semaphore_signal(
            barrier,
            inc=1,
            device_id={"tile": lax.rem(t + step, tiles)},
            device_id_type=pl.DeviceIdType.MESH,
        )
    for step in range(1, DPS):
        pl.semaphore_signal(
            barrier,
            inc=1,
            device_id={"dp": lax.rem(d + step, DPS)},
            device_id_type=pl.DeviceIdType.MESH,
        )
    pl.semaphore_wait(barrier, tiles + DPS - 2)


class Edges:
    def __init__(self, source, target, send, receive):
        t = lax.axis_index("tile")
        row, col = t // 4, t % 4
        self.rooms = (row > 0, col < 3, row < 1, col > 0)
        self.target = target
        self.copies = []
        for h, step in enumerate((4, 1, 4, 7)):
            back = (h + 2) % 4
            peer = lax.rem(t + step, ZS * CORES)
            self.copies.append(
                to_device(source.at[h], target.at[back], send.at[h], receive.at[back], tile=peer)
            )

    def start(self):
        for h in range(4):

            @pl.when(self.rooms[h])
            def _():
                self.copies[h].start()

            @pl.when(jnp.logical_not(self.rooms[h]))
            def _():
                self.target[h] = jnp.zeros(self.target.shape[1:], self.target.dtype)

    def wait(self):
        for h in range(4):

            @pl.when(self.rooms[h])
            def _():
                self.copies[h].wait_send()
                self.copies[(h + 2) % 4].wait_recv()


def first_kernel(
    strips_ref,
    block_ref,
    back_ref,
    second_ref,
    borders_ref,
    basis_ref,
    piece_ref,
    seconds_ref,
    near,
    edge_send,
    edge_recv,
    z_send,
    z_recv,
    sib_send,
    sib_recv,
    back_send,
    back_recv,
    sec_send,
    sec_recv,
    pass_send,
    pass_recv,
):
    t = lax.axis_index("tile")
    d = lax.axis_index("dp")
    z, c = t // CORES, t % CORES
    sibling = t + 1 - 2 * c
    greet()
    edges = Edges(strips_ref, borders_ref, edge_send, edge_recv)
    edges.start()

    def z_copy(k):
        return to_device(
            block_ref, basis_ref.at[z, c], z_send.at[k - 1], z_recv.at[k - 1],
            tile=lax.rem(t + CORES * k, ZS * CORES),
        )

    def sib_copy(k):
        spot = lax.rem(z + ZS - k, ZS)
        source = block_ref if k == 0 else basis_ref.at[spot, c]
        return to_device(source, basis_ref.at[spot, c], sib_send.at[k], sib_recv.at[k], tile=sibling)

    def back_copy(j):
        peer = lax.rem(d + j, DPS)
        return to_device(
            back_ref.at[peer], near.at[j - 1], back_send.at[j - 1], back_recv.at[j - 1], dp=peer
        )

    def sec_copy(j):
        return to_device(
            second_ref.at[c], seconds_ref.at[d, c], sec_send.at[j - 1], sec_recv.at[j - 1],
            dp=lax.rem(d + j, DPS),
        )

    def pass_copy(j):
        spot = seconds_ref.at[lax.rem(d + DPS - j, DPS), c]
        return to_device(spot, spot, pass_send.at[j - 1], pass_recv.at[j - 1], tile=sibling)

    z_copies = [z_copy(k) for k in (1, 2, 3)]
    sib_copies = [sib_copy(k) for k in range(ZS)]
    back_copies = [back_copy(j) for j in (1, 2, 3)]
    sec_copies = [sec_copy(j) for j in (1, 2, 3)]
    pass_copies = [pass_copy(j) for j in (1, 2, 3)]
    for copy in z_copies + sib_copies[:1] + back_copies + sec_copies:
        copy.start()
    basis_ref[z, c] = block_ref[...]
    seconds_ref[d] = second_ref[...]
    for copy in back_copies:
        copy.wait_recv()
    total = back_ref[d]
    for slot in range(DPS - 1):
        total = total + near[slot]
    piece_ref[...] = total
    for j in range(DPS - 1):
        sec_copies[j].wait_recv()
        pass_copies[j].start()
    for k in range(1, ZS):
        z_copies[k - 1].wait_recv()
        sib_copies[k].start()
    edges.wait()
    for copy in back_copies + sec_copies + z_copies:
        copy.wait_send()
    for copy in sib_copies + pass_copies:
        copy.wait()


def first_exchange(strips, block, back, second):
    vmem = pl.BlockSpec(memory_space=pltpu.VMEM)
    rows = block.shape[0]
    half = second.shape[1:]
    piece = back.shape[1:]
    counts = [4, 4, 3, 3, 4, 4, 3, 3, 3, 3, 3, 3]
    return pl.pallas_call(
        first_kernel,
        out_shape=(
            jax.ShapeDtypeStruct(strips.shape, jnp.bfloat16),
            jax.ShapeDtypeStruct((ZS, CORES, rows, LANES), jnp.bfloat16),
            jax.ShapeDtypeStruct(piece, jnp.float32),
            jax.ShapeDtypeStruct((DPS, CORES) + half, jnp.float32),
        ),
        in_specs=[vmem] * 4,
        out_specs=(vmem,) * 4,
        scratch_shapes=[
            pltpu.VMEM((DPS - 1,) + piece, jnp.float32),
            *[pltpu.SemaphoreType.DMA((count,)) for count in counts],
        ],
        compiler_params=pltpu.CompilerParams(
            collective_id=0, has_side_effects=True, vmem_limit_bytes=40 * 1024 * 1024
        ),
        name="first_exchange",
    )(strips, block, back, second)


def second_kernel(
    grad_scale,
    partial_ref,
    piece_ref,
    mapped_ref,
    basis_ref,
    rims_ref,
    grad_ref,
    back_ref,
    all_ref,
    crossed_ref,
    incoming_ref,
    near,
    half,
    dp_in,
    pieces,
    z_in,
    spread_out,
    edge_send,
    edge_recv,
    half_send,
    half_recv,
    sum_send,
    sum_recv,
    zsum_send,
    zsum_recv,
    zall_send,
    zall_recv,
    dpall_send,
    dpall_recv,
    last_send,
    last_recv,
    mz_send,
    mz_recv,
    md_send,
    md_recv,
    ms_send,
    ms_recv,
    cd_send,
    cd_recv,
    cs_send,
    cs_recv,
):
    t = lax.axis_index("tile")
    d = lax.axis_index("dp")
    z, c = t // CORES, t % CORES
    other = 1 - c
    sibling = t + 1 - 2 * c
    z_peers = [lax.rem(t + CORES * k, ZS * CORES) for k in range(ZS)]
    z_from = [lax.rem(z + ZS - k, ZS) for k in range(ZS)]
    z_to = [lax.rem(z + k, ZS) for k in range(ZS)]
    d_to = [lax.rem(d + j, DPS) for j in range(DPS)]
    d_from = [lax.rem(d + DPS - j, DPS) for j in range(DPS)]
    rest = range(1, ZS)
    greet()

    swap = to_device(partial_ref.at[other], near, half_send, half_recv, tile=sibling)
    swap.start()
    edges = Edges(rims_ref, incoming_ref, edge_send, edge_recv)
    edges.start()
    m_z = [
        to_device(mapped_ref, all_ref.at[d, z, c], mz_send.at[k - 1], mz_recv.at[k - 1], tile=z_peers[k])
        for k in rest
    ]
    for copy in m_z:
        copy.start()
    all_ref[d, z, c] = mapped_ref[...]
    swap.wait_recv()
    half[...] = partial_ref[c] + near[...]

    sums = [
        to_device(half.at[d_to[j]], dp_in.at[j - 1], sum_send.at[j - 1], sum_recv.at[j - 1], dp=d_to[j])
        for j in rest
    ]
    for copy in sums:
        copy.start()

    def m_dp(j, k):
        spot = all_ref.at[d, z_from[k], c]
        source = mapped_ref if k == 0 else spot
        return to_device(source, spot, md_send.at[j - 1, k], md_recv.at[j - 1, k], dp=d_to[j])

    m_dps = [[m_dp(j, k) for j in rest] for k in range(ZS)]

    def m_sib(k):
        spot = all_ref.at[d, z_from[k], c]
        source = mapped_ref if k == 0 else spot
        return to_device(source, spot, ms_send.at[k], ms_recv.at[k], tile=sibling)

    m_sibs = [m_sib(k) for k in range(ZS)]
    for copy in m_dps[0] + m_sibs[:1]:
        copy.start()
    for copy in sums:
        copy.wait_recv()
    total = half[d]
    for slot in range(DPS - 1):
        total = total + dp_in[slot]
    piece = total.shape[0] // ZS
    for k in range(ZS):
        pieces[k] = total[k * piece : (k + 1) * piece]
    zsums = [
        to_device(pieces.at[z_to[k]], z_in.at[k - 1], zsum_send.at[k - 1], zsum_recv.at[k - 1], tile=z_peers[k])
        for k in rest
    ]
    for copy in zsums:
        copy.start()
    for copy in zsums:
        copy.wait_recv()
    total = pieces[z]
    for slot in range(ZS - 1):
        total = total + z_in[slot]
    spread_out[c, d, z, 0] = total
    spread_out[c, d, z, 1] = piece_ref[...]
    mine = spread_out.at[c, d, z]
    zalls = [
        to_device(mine, mine, zall_send.at[k - 1], zall_recv.at[k - 1], tile=z_peers[k]) for k in rest
    ]
    for copy in zalls:
        copy.start()
    for k in rest:
        m_z[k - 1].wait_recv()
    for copy in zalls:
        copy.wait_recv()
    slab = spread_out.at[c, d]
    dpalls = [
        to_device(slab, slab, dpall_send.at[j - 1], dpall_recv.at[j - 1], dp=d_to[j]) for j in rest
    ]
    for copy in dpalls:
        copy.start()
    for k in rest:
        for copy in m_dps[k]:
            copy.start()
        m_sibs[k].start()

    def last(j):
        spot = spread_out.at[c, d_from[j]]
        return to_device(spot, spot, last_send.at[j], last_recv.at[j], tile=sibling)

    lasts = [last(j) for j in range(DPS)]
    lasts[0].start()
    for j in rest:
        dpalls[j - 1].wait_recv()
        lasts[j].start()
    for copy in lasts:
        copy.wait_recv()
    for core in range(CORES):
        for dp in range(DPS):
            for line in range(ZS):
                at = ((core * DPS + dp) * ZS + line) * piece
                grad_ref[at : at + piece] = spread_out[core, dp, line, 0]
                to = ((line * CORES + core) * DPS + dp) * piece
                back_ref[to : to + piece] = spread_out[core, dp, line, 1]

    grad = grad_ref[...] * grad_scale
    grad_ref[...] = grad
    grad_hi, grad_lo = split(grad)
    columns = basis_ref[...].reshape(grad.shape[0], LANES)
    crossed = lax.dot_general(
        grad_hi, columns, tn, preferred_element_type=jnp.float32
    ) + lax.dot_general(grad_lo, columns, tn, preferred_element_type=jnp.float32)
    side = crossed.shape[0] // CORES
    crossed_ref[d, 0] = crossed[:side]
    crossed_ref[d, 1] = crossed[side:]
    own = crossed_ref.at[d, c]
    c_dps = [to_device(own, own, cd_send.at[j - 1], cd_recv.at[j - 1], dp=d_to[j]) for j in rest]
    for copy in c_dps:
        copy.start()

    def m_far(j):
        spot = all_ref.at[d_from[j], :, c]
        return to_device(spot, spot, ms_send.at[ZS + j - 1], ms_recv.at[ZS + j - 1], tile=sibling)

    m_fars = [m_far(j) for j in rest]
    for j in rest:
        for k in range(ZS):
            m_dps[k][j - 1].wait_recv()
        m_fars[j - 1].start()

    def c_sib(j):
        spot = crossed_ref.at[d_from[j], c]
        return to_device(spot, spot, cs_send.at[j - 1], cs_recv.at[j - 1], tile=sibling)

    c_sibs = [c_sib(j) for j in rest]
    for j in rest:
        c_dps[j - 1].wait_recv()
        c_sibs[j - 1].start()
    edges.wait()
    swap.wait_send()
    for copy in sums + zsums + zalls + dpalls + lasts + m_z + c_dps:
        copy.wait_send()
    for group in m_dps:
        for copy in group:
            copy.wait_send()
    for copy in m_sibs + m_fars + c_sibs:
        copy.wait()


def second_exchange(partial, piece, mapped, basis, rims, scale):
    vmem = pl.BlockSpec(memory_space=pltpu.VMEM)
    rows, channels = partial.shape
    block = rows // (CORES * DPS)
    dma = pltpu.SemaphoreType.DMA
    pair = [dma((3,)), dma((3,))]
    return pl.pallas_call(
        lambda *refs: second_kernel(scale, *refs),
        out_shape=(
            jax.ShapeDtypeStruct((rows, channels), jnp.float32),
            jax.ShapeDtypeStruct((rows, channels), jnp.float32),
            jax.ShapeDtypeStruct((DPS, ZS, CORES) + mapped.shape, jnp.bfloat16),
            jax.ShapeDtypeStruct((DPS, CORES, channels // CORES, LANES), jnp.float32),
            jax.ShapeDtypeStruct(rims.shape, jnp.bfloat16),
        ),
        in_specs=[vmem] * 5,
        out_specs=(vmem,) * 5,
        scratch_shapes=[
            pltpu.VMEM((DPS, block, channels), jnp.float32),
            pltpu.VMEM((DPS, block, channels), jnp.float32),
            pltpu.VMEM((DPS - 1, block, channels), jnp.float32),
            pltpu.VMEM((ZS, block // ZS, channels), jnp.float32),
            pltpu.VMEM((ZS - 1, block // ZS, channels), jnp.float32),
            pltpu.VMEM((CORES, DPS, ZS, 2, block // ZS, channels), jnp.float32),
            dma((4,)),
            dma((4,)),
            dma,
            dma,
            *(pair * 4),
            dma((4,)),
            dma((4,)),
            *pair,
            dma((3, 4)),
            dma((3, 4)),
            dma((7,)),
            dma((7,)),
            *(pair * 2),
        ],
        compiler_params=pltpu.CompilerParams(
            collective_id=1, has_side_effects=True, vmem_limit_bytes=48 * 1024 * 1024
        ),
        name="second_exchange",
    )(partial.reshape(CORES, DPS, block, channels), piece, mapped, basis, rims)


def by_direction(strips, turn):
    return lax.dynamic_slice_in_dim(jnp.concatenate([strips, strips], axis=0), turn, 4, 0)


def body_quick(
    activations,
    cotangent,
    kernel,
    turning,
    orient,
    left_factor,
    left_basis,
    right_factor,
    right_basis,
    momentum,
    second_moment,
):
    tiles, dp_count = ZS * CORES, DPS
    tile_index = lax.axis_index("tile")
    dp_index = lax.axis_index("dp")
    tile_vals = activations[:, 0]
    tile_grads = cotangent[:, 0]
    side = tile_vals.shape[1]
    channels = tile_vals.shape[-1]
    turn = turning[0]
    flipped = orient[0] >= 4
    rows_per, width = left_factor.shape
    part = left_basis.shape[1]
    row_start = tile_index * rows_per
    moment_rows = momentum.shape[0]
    moment_start = dp_index * moment_rows

    strips = by_direction(edge_strips(tile_vals)[:, 0], (4 - turn) % 4)
    block = jnp.pad(left_basis.astype(jnp.bfloat16), ((0, 0), (0, LANES - part)))
    back = jnp.dot(left_basis, momentum, precision=high)
    borders, basis, piece, seconds = first_exchange(
        strips,
        block,
        back.reshape(DPS, rows_per // DPS, channels),
        second_moment.reshape(CORES, moment_rows // CORES, channels),
    )
    all_second = seconds.reshape(width, channels)
    borders = flip_edges(by_direction(borders, turn)[:, None], flipped)
    padded = assemble(tile_vals, borders)
    columns = tap_patches(padded, side)
    flat_grads = tile_grads.reshape(-1, channels)
    partial_grad = lax.dot_general(
        columns, flat_grads, (((0,), (0,)), ((), ())), preferred_element_type=jnp.float32
    )
    spread = spread_back(flat_grads, kernel, 1, side)
    rims = by_direction(cycle_strips(spread).astype(jnp.bfloat16)[:, 0], (4 - turn) % 4)
    factor_hi, factor_lo = split_wide(left_factor)
    flat_basis = basis.reshape(width, LANES)
    mapped = 0.95 * (
        jnp.dot(factor_hi, flat_basis, preferred_element_type=jnp.float32)
        + jnp.dot(factor_lo, flat_basis, preferred_element_type=jnp.float32)
    )
    cells = dp_count * tiles * side * side
    grad, back, mapped, crossed, incoming = second_exchange(
        partial_grad, piece, mapped.astype(jnp.bfloat16), basis, rims, 1.0 / math.sqrt(cells)
    )
    result = jnp.dot(columns, kernel, preferred_element_type=jnp.float32).astype(jnp.bfloat16)
    result = result.reshape(activations.shape)
    incoming = flip_edges(by_direction(incoming, turn)[:, None], flipped)
    input_grad = absorb_rims(spread[:, 1:-1, 1:-1], incoming.astype(jnp.float32)).astype(
        jnp.bfloat16
    )
    input_grad = input_grad.reshape(cotangent.shape)
    grad_rows = lax.dynamic_slice_in_dim(grad, row_start, rows_per, 0)
    left_new = 0.95 * left_factor + 0.05 * lax.dot_general(
        grad_rows, grad, (((1,), (1,)), ((), ())), precision=high
    )
    mapped = mapped.reshape(DPS, width, LANES)
    mapped = jnp.concatenate([mapped[d, :, :part] for d in range(DPS)], axis=1)
    crossed = crossed.reshape(DPS, channels, LANES)
    crossed = jnp.concatenate([crossed[d, :, :part] for d in range(DPS)], axis=1)
    both = jnp.concatenate([back, grad], axis=1)
    mapped_gram = lax.dot_general(mapped, mapped, tn, preferred_element_type=jnp.float32)
    mapped_both = sum(
        lax.dot_general(mapped, term, tn, preferred_element_type=jnp.float32) for term in split_wide(both)
    )
    mapped_grad = mapped_both[:, channels:]
    grad_both = lax.dot_general(grad, both, tn, precision=high)
    grad_gram = grad_both[:, channels:]
    weight = 0.05 * mapped_grad + 0.00125 * lax.dot_general(crossed, grad_gram, tn, precision=high)
    gram = mapped_gram + lax.dot_general(
        jnp.concatenate([weight.T, crossed], axis=0),
        jnp.concatenate([crossed, weight.T], axis=0),
        tn,
        precision=high,
    )
    power_rows = lax.dynamic_slice_in_dim(mapped, row_start, rows_per, 0).astype(
        jnp.float32
    ) + 0.05 * jnp.dot(grad_rows, crossed, precision=high)
    power_side = mapped_both + 0.05 * lax.dot_general(crossed, grad_both, tn, precision=high)
    right_new = 0.95 * right_factor + 0.05 * grad_gram
    right_power = jnp.dot(right_new, right_basis, precision=high)
    right_gram = lax.dot_general(right_power, right_power, tn, precision=high)
    solved, right_inverse = factor_solve(
        gram, jnp.concatenate([power_side, power_rows.T], axis=1), right_gram
    )
    turned_momentum = solved[:, :channels]
    turned_grad = solved[:, channels : 2 * channels]
    basis_new = solved[:, 2 * channels :].T
    right_basis_new = lax.dot_general(
        right_power, right_inverse, (((1,), (1,)), ((), ())), precision=high
    )
    right_turn = lax.dot_general(right_basis, right_basis_new, tn, precision=high)
    rotated = jnp.dot(turned_momentum, right_turn, precision=high)
    projected = jnp.dot(turned_grad, right_basis_new, precision=high)
    momentum_all = 0.9 * rotated + 0.1 * projected
    second_all = 0.95 * all_second + 0.05 * projected * projected
    normalized = momentum_all / (jnp.sqrt(second_all) + epsilon)
    momentum_new = lax.dynamic_slice_in_dim(momentum_all, moment_start, moment_rows, 0)
    second_new = lax.dynamic_slice_in_dim(second_all, moment_start, moment_rows, 0)
    update_rows = jnp.dot(basis_new, normalized, precision=high)
    update = lax.dot_general(
        update_rows, right_basis_new, (((1,), (1,)), ((), ())), precision=high
    )
    return (
        result,
        input_grad,
        grad,
        left_new,
        basis_new,
        right_new,
        right_basis_new,
        momentum_new,
        second_new,
        update,
    )


def body(*args):
    tiles = lax.axis_size("tile")
    dp_count = lax.axis_size("dp")
    left_basis = args[6]
    samples = args[0].shape[0]
    if (tiles, dp_count, samples) == (ZS * CORES, DPS, 1) and left_basis.shape == (144, 288):
        return body_quick(*args)
    return body_plain(*args)


def solution(mesh):
    placed = (
        P(("group", "dp"), "tile", None, None, None),
        P(("group", "dp"), "tile", None, None, None),
        P("group", None),
        P("tile"),
        P("tile", None),
        P(("group", "tile"), None),
        P(("group", "tile"), "dp"),
        P("group", None),
        P("group", None),
        P(("group", "dp"), None),
        P(("group", "dp"), None),
    )
    return jax.shard_map(
        body,
        mesh=mesh,
        in_specs=placed,
        out_specs=(
            P(("group", "dp"), "tile", None, None, None),
            P(("group", "dp"), "tile", None, None, None),
            P("group", None),
            P(("group", "tile"), None),
            P(("group", "tile"), None),
            P("group", None),
            P("group", None),
            P(("group", "dp"), None),
            P(("group", "dp"), None),
            P(("group", "tile"), None),
        ),
        check_vma=False,
    )
```

```python
import math

import jax
import jax.numpy as jnp
from jax import lax
from jax.experimental import pallas as pl
from jax.experimental.pallas import tpu as pltpu
from jax.sharding import PartitionSpec as P

highest = lax.Precision.HIGHEST
epsilon = 1e-08


def edge_strips(values):
    return jnp.stack(
        [values[..., 0, :, :], values[..., :, -1, :], values[..., -1, :, :], values[..., :, 0, :]],
        axis=0,
    )


def cycle_strips(spread):
    return jnp.stack(
        [spread[:, 0, 1:-1], spread[:, 1:-1, -1], spread[:, -1, 1:-1], spread[:, 1:-1, 0]], axis=0
    )


def assemble(tile_vals, borders):
    middle = jnp.concatenate(
        [borders[3][:, :, None, :], tile_vals, borders[1][:, :, None, :]], axis=2
    )
    top_row = jnp.pad(borders[0], ((0, 0), (1, 1), (0, 0)))[:, None]
    bottom_row = jnp.pad(borders[2], ((0, 0), (1, 1), (0, 0)))[:, None]
    return jnp.concatenate([top_row, middle, bottom_row], axis=1)


def tap_patches(padded, side):
    pieces = [
        padded[:, row_off : row_off + side, col_off : col_off + side, :]
        for row_off in range(3)
        for col_off in range(3)
    ]
    joined = jnp.concatenate(pieces, axis=-1)
    return joined.reshape(-1, joined.shape[-1])


def spread_back(flat_grads, kernel, sample_count, side):
    channels = kernel.shape[1]
    summed = jnp.zeros((sample_count, side + 2, side + 2, channels), jnp.float32)
    for tap_index in range(9):
        row_off, col_off = divmod(tap_index, 3)
        weight_tap = kernel[tap_index * channels : (tap_index + 1) * channels]
        contrib = lax.dot_general(
            flat_grads, weight_tap, (((1,), (1,)), ((), ())), preferred_element_type=jnp.float32
        )
        contrib = contrib.reshape(sample_count, side, side, channels)
        summed = summed + jnp.pad(
            contrib, ((0, 0), (row_off, 2 - row_off), (col_off, 2 - col_off), (0, 0))
        )
    return summed


def absorb_rims(interior, incoming):
    result = interior.at[..., 0, :, :].add(incoming[0])
    result = result.at[..., :, -1, :].add(incoming[1])
    result = result.at[..., -1, :, :].add(incoming[2])
    return result.at[..., :, 0, :].add(incoming[3])


def flip_edges(strips, flipped):
    return jnp.where(flipped[:, None, None, None], strips[:, :, ::-1, :], strips)


def pick_gathered(everything, near_tiles, facing, flipped, usable):
    flat = everything.reshape(everything.shape[0] * 4, -1)
    wanted = jnp.where(usable, near_tiles * 4 + facing, -1)
    selector = (lax.broadcasted_iota(jnp.int32, (4, flat.shape[0]), 1) == wanted[:, None]).astype(
        jnp.bfloat16
    )
    picked = jnp.dot(selector, flat, preferred_element_type=jnp.float32).astype(jnp.bfloat16)
    return flip_edges(picked.reshape((4,) + everything.shape[2:]), flipped)


LEAF = 128
SPAN = 384


def split(value):
    high = value.astype(jnp.bfloat16)
    return high, (value - high.astype(jnp.float32)).astype(jnp.bfloat16)


def split_wide(value):
    high = lax.reduce_precision(value, 8, 7)
    return high.astype(jnp.bfloat16), (value - high).astype(jnp.bfloat16)


def dot3(left, right, dims=(((1,), (0,)), ((), ()))):
    def one(a, b):
        return lax.dot_general(a, b, dims, preferred_element_type=jnp.float32)

    return one(left[0], right[0]) + (one(left[0], right[1]) + one(left[1], right[0]))


by_rows = (((1,), (1,)), ((), ()))


def leaf_inverse(block, m_ref, s_ref):
    row = lax.broadcasted_iota(jnp.int32, (LEAF, LEAF), 0)
    col = lax.broadcasted_iota(jnp.int32, (LEAF, LEAF), 1)
    on_diag = row == col
    unit = jnp.where(on_diag, 1.0, 0.0)
    kept = jnp.where(on_diag, block, 0.0)
    across = lax.rsqrt(jnp.sum(kept, axis=0, keepdims=True))
    down = lax.rsqrt(jnp.sum(kept, axis=1, keepdims=True))
    scaled = block * across * down
    m_ref[...] = jnp.where(on_diag, down, jnp.where(row > col, -scaled * across, 0.0))
    pair = split(block)
    rough = m_ref[...].astype(jnp.bfloat16)
    turned = jnp.dot(rough, pair[0], preferred_element_type=jnp.float32).astype(jnp.bfloat16)
    gap = lax.dot_general(turned, rough, by_rows, preferred_element_type=jnp.float32) - unit
    low = jnp.where(row > col, gap, jnp.where(on_diag, 0.5 * gap, 0.0)).astype(jnp.bfloat16)
    m_ref[...] -= jnp.dot(low, rough, preferred_element_type=jnp.float32)

    def more(carry):
        step, error = carry
        return (step < 12) & (error > 1e-4)

    def refine(carry):
        step, _ = carry
        guess = m_ref[...]
        guess_pair = split(guess)
        turned = dot3(guess_pair, pair)
        gap = dot3(split(turned), guess_pair, by_rows) - unit
        error = jnp.max(jnp.abs(gap))
        low = jnp.where(row > col, gap, jnp.where(on_diag, 0.5 * gap, 0.0))
        m_ref[...] = guess - dot3(split(low), guess_pair)
        return step + 1, error

    _, error = lax.while_loop(more, refine, (jnp.int32(0), jnp.float32(1.0)))

    @pl.when(jnp.logical_not(error <= 1e-4))
    def _():
        s_ref[...] = block
        m_ref[...] = unit

        def eliminate(j, carry):
            work = s_ref[...]
            line = s_ref[pl.ds(j, 1), :]
            lane = lax.broadcasted_iota(jnp.int32, (1, LEAF), 1)
            scale = lax.rsqrt(jnp.sum(jnp.where(lane == j, line, 0.0), axis=1, keepdims=True))
            column = jnp.sum(jnp.where(col == j, work, 0.0), axis=1, keepdims=True)
            side = lax.broadcasted_iota(jnp.int32, (LEAF, 1), 0)
            column = jnp.where(side > j, column * scale, 0.0)
            s_ref[...] = work - column * (line * scale)
            mine = m_ref[pl.ds(j, 1), :] * scale
            m_ref[...] = m_ref[...] - column * mine
            m_ref[pl.ds(j, 1), :] = mine
            return carry

        lax.fori_loop(0, LEAF, eliminate, 0)


def factor_kernel(
    gram_ref, side_ref, small_ref, y_ref, small_out_ref, a_ref, uh, ul, uth, utl, yh, yl, m_ref, s_ref
):
    width = gram_ref.shape[1]
    blocks = width // LEAF
    spans = width // SPAN
    leaf_inverse(small_ref[...], m_ref, s_ref)
    small_out_ref[...] = m_ref[...]
    a_ref[...] = gram_ref[...]
    y_ref[...] = side_ref[...]

    def block_step(k, carry):
        k0 = pl.multiple_of(k * LEAF, LEAF)
        leaf_inverse(a_ref[pl.ds(k0, LEAF), pl.ds(k0, LEAF)], m_ref, s_ref)
        inverse = split(m_ref[...])
        for span in range(spans):
            part = slice(span * SPAN, (span + 1) * SPAN)

            @pl.when((span + 1) * SPAN > k0 + LEAF)
            def _():
                value = dot3(inverse, split(a_ref[pl.ds(k0, LEAF), part]))
                uh[:, part], ul[:, part] = split(value)
                uth[part, :], utl[part, :] = split(value.T)

        value = dot3(inverse, split(y_ref[pl.ds(k0, LEAF), :]))
        y_ref[pl.ds(k0, LEAF), :] = value
        yh[...], yl[...] = split(value)

        def row_step(i, inner):
            i0 = pl.multiple_of(i * LEAF, LEAF)
            left = uth[pl.ds(i0, LEAF), :], utl[pl.ds(i0, LEAF), :]
            for span in range(spans):
                part = slice(span * SPAN, (span + 1) * SPAN)

                @pl.when((span + 1) * SPAN > i0)
                def _():
                    a_ref[pl.ds(i0, LEAF), part] -= dot3(left, (uh[:, part], ul[:, part]))

            y_ref[pl.ds(i0, LEAF), :] -= dot3(left, (yh[...], yl[...]))
            return inner

        lax.fori_loop(k + 1, blocks, row_step, 0)
        return carry

    lax.fori_loop(0, blocks, block_step, 0)


def factor_solve(gram, side, small):
    width, columns = side.shape
    vmem = pl.BlockSpec(memory_space=pltpu.VMEM)
    half = jnp.bfloat16
    return pl.pallas_call(
        factor_kernel,
        out_shape=(
            jax.ShapeDtypeStruct(side.shape, jnp.float32),
            jax.ShapeDtypeStruct(small.shape, jnp.float32),
        ),
        in_specs=[vmem] * 3,
        out_specs=(vmem, vmem),
        scratch_shapes=[
            pltpu.VMEM((width, width), jnp.float32),
            pltpu.VMEM((LEAF, width), half),
            pltpu.VMEM((LEAF, width), half),
            pltpu.VMEM((width, LEAF), half),
            pltpu.VMEM((width, LEAF), half),
            pltpu.VMEM((LEAF, columns), half),
            pltpu.VMEM((LEAF, columns), half),
            pltpu.VMEM((LEAF, LEAF), jnp.float32),
            pltpu.VMEM((LEAF, LEAF), jnp.float32),
        ],
        compiler_params=pltpu.CompilerParams(vmem_limit_bytes=40 * 1024 * 1024),
        name="factor_solve",
    )(gram, side, small)


high = lax.Precision.HIGH
tn = (((0,), (0,)), ((), ()))


def sum_kernel(dp_count, tiles, x_ref, out_ref, near, part, far, *sems):
    dp_index = lax.axis_index("dp")
    tile_index = lax.axis_index("tile")
    dp_peers = [lax.rem(dp_index + step, dp_count) for step in range(1, dp_count)]
    tile_peers = [lax.rem(tile_index + step, tiles) for step in range(1, tiles)]
    barrier = pltpu.get_barrier_semaphore()
    for axis, peers in (("dp", dp_peers), ("tile", tile_peers)):
        for peer in peers:
            pl.semaphore_signal(
                barrier, inc=1, device_id={axis: peer}, device_id_type=pl.DeviceIdType.MESH
            )
    pl.semaphore_wait(barrier, dp_count + tiles - 2)

    def exchange(axis, peers, source, target, send, receive):
        copies = [
            pltpu.make_async_remote_copy(
                src_ref=source(peer),
                dst_ref=target(slot),
                send_sem=send.at[slot],
                recv_sem=receive.at[slot],
                device_id={axis: peer},
                device_id_type=pl.DeviceIdType.MESH,
            )
            for slot, peer in enumerate(peers)
        ]
        for copy in copies:
            copy.start()
        for copy in copies:
            copy.wait()

    exchange("dp", dp_peers, lambda peer: x_ref.at[peer], lambda slot: near.at[slot], *sems[0:2])
    total = x_ref[dp_index]
    for slot in range(dp_count - 1):
        total = total + near[slot]
    part[...] = total
    exchange("tile", tile_peers, lambda peer: part.at[peer], lambda slot: far.at[slot], *sems[2:4])
    total = part[tile_index]
    for slot in range(tiles - 1):
        total = total + far[slot]
    out_ref[dp_index, tile_index] = total
    own = out_ref.at[dp_index, tile_index]
    exchange("tile", tile_peers, lambda peer: own, lambda slot: own, *sems[4:6])
    slab = out_ref.at[dp_index]
    exchange("dp", dp_peers, lambda peer: slab, lambda slot: slab, *sems[6:8])


def sum_everywhere(value):
    tiles = lax.axis_size("tile")
    dp_count = lax.axis_size("dp")
    rows, columns = value.shape
    if tiles < 2 or dp_count < 2 or rows % (tiles * dp_count):
        return lax.psum(value, ("tile", "dp"))
    piece = rows // (tiles * dp_count)
    vmem = pl.BlockSpec(memory_space=pltpu.VMEM)
    wide = (dp_count, tiles, piece, columns)
    counts = [dp_count - 1] * 2 + [tiles - 1] * 4 + [dp_count - 1] * 2
    out = pl.pallas_call(
        lambda *refs: sum_kernel(dp_count, tiles, *refs),
        out_shape=jax.ShapeDtypeStruct(wide, jnp.float32),
        in_specs=[vmem],
        out_specs=vmem,
        scratch_shapes=[
            pltpu.VMEM((dp_count - 1, tiles, piece, columns), jnp.float32),
            pltpu.VMEM((tiles, piece, columns), jnp.float32),
            pltpu.VMEM((tiles - 1, piece, columns), jnp.float32),
            *[pltpu.SemaphoreType.DMA((count,)) for count in counts],
        ],
        compiler_params=pltpu.CompilerParams(collective_id=0, has_side_effects=True),
        name="sum_everywhere",
    )(value.reshape(wide))
    return out.reshape(rows, columns)


def body_plain(
    activations,
    cotangent,
    kernel,
    turning,
    orient,
    left_factor,
    left_basis,
    right_factor,
    right_basis,
    momentum,
    second_moment,
):
    tiles = lax.axis_size("tile")
    dp_count = lax.axis_size("dp")
    tile_index = lax.axis_index("tile")
    dp_index = lax.axis_index("dp")
    tile_vals = activations[:, 0]
    tile_grads = cotangent[:, 0]
    sample_count = tile_vals.shape[0]
    side = tile_vals.shape[1]
    channels = tile_vals.shape[-1]
    own_turn = turning[0]
    facing = orient[0] % 4
    flipped = orient[0] >= 4
    heading = (jnp.arange(4, dtype=jnp.int32) + own_turn) % 4
    row_of = tile_index // 4
    col_of = tile_index % 4
    room = jnp.stack([row_of > 0, col_of < 3, row_of < tiles // 4 - 1, col_of > 0])
    usable = (
        jnp.sum(
            jnp.where(
                heading[:, None] == jnp.arange(4, dtype=jnp.int32)[None, :], room[None, :], False
            ),
            axis=1,
        )
        > 0
    )
    offsets = jnp.array([-4, 1, 4, -1], dtype=jnp.int32)
    near_tiles = tile_index + jnp.sum(
        jnp.where(heading[:, None] == jnp.arange(4, dtype=jnp.int32)[None, :], offsets[None, :], 0),
        axis=1,
    )
    strips = edge_strips(tile_vals)
    flat_grads = tile_grads.reshape(-1, channels)
    spread = spread_back(flat_grads, kernel, sample_count, side)
    rim_cells = cycle_strips(spread).astype(jnp.bfloat16)
    everything = lax.all_gather(
        jnp.concatenate([strips, rim_cells], axis=0)[None], "tile", axis=0, tiled=True
    )
    borders = pick_gathered(everything[:, :4], near_tiles, facing, flipped, usable)
    incoming = pick_gathered(everything[:, 4:], near_tiles, facing, flipped, usable)
    padded = assemble(tile_vals, borders)
    columns = tap_patches(padded, side)
    partial_grad = lax.dot_general(
        columns, flat_grads, (((0,), (0,)), ((), ())), preferred_element_type=jnp.float32
    )
    summed_grad = sum_everywhere(partial_grad)
    result = jnp.dot(columns, kernel, preferred_element_type=jnp.float32).astype(jnp.bfloat16)
    result = result.reshape(activations.shape)
    input_grad = absorb_rims(spread[:, 1:-1, 1:-1], incoming.astype(jnp.float32)).astype(
        jnp.bfloat16
    )
    input_grad = input_grad.reshape(cotangent.shape)
    cells = dp_count * sample_count * tiles * side * side
    grad = summed_grad * (1.0 / math.sqrt(cells))
    rows_per, width = left_factor.shape
    row_start = tile_index * rows_per
    moment_rows = momentum.shape[0]
    moment_start = dp_index * moment_rows
    grad_rows = lax.dynamic_slice_in_dim(grad, row_start, rows_per, 0)
    left_new = 0.95 * left_factor + 0.05 * lax.dot_general(
        grad_rows, grad, (((1,), (1,)), ((), ())), precision=high
    )
    basis_rows = lax.all_gather(left_basis, "dp", axis=1, tiled=True)
    basis = lax.all_gather(basis_rows.astype(jnp.bfloat16), "tile", axis=0, tiled=True)
    moments = lax.all_gather(
        jnp.concatenate([momentum, second_moment], axis=1), "dp", axis=0, tiled=True
    )
    all_momentum, all_second = moments[:, :channels], moments[:, channels:]
    back_rows = jnp.dot(basis_rows, all_momentum, precision=highest)
    own_row = row_start + lax.broadcasted_iota(jnp.int32, left_factor.shape, 0)
    own_col = lax.broadcasted_iota(jnp.int32, left_factor.shape, 1)
    diagonal = jnp.sum(jnp.where(own_row == own_col, left_factor, 0.0), axis=1, keepdims=True)
    rest = jnp.broadcast_to(split_wide(diagonal)[1], (rows_per, LEAF))
    factor = lax.all_gather(
        jnp.concatenate(
            [left_factor.astype(jnp.bfloat16), *split_wide(back_rows), rest], axis=1
        ),
        "tile",
        axis=0,
        tiled=True,
    )
    back = factor[:, width : width + channels].astype(jnp.float32) + factor[
        :, width + channels : width + 2 * channels
    ].astype(jnp.float32)
    rest = factor[:, width + 2 * channels : width + 2 * channels + 1]
    factor = factor[:, :width]
    mapped = 0.95 * (
        jnp.dot(factor, basis, preferred_element_type=jnp.float32)
        + rest.astype(jnp.float32) * basis.astype(jnp.float32)
    )
    mapped_gram = lax.dot_general(mapped, mapped, tn, precision=high)
    mapped_back = lax.dot_general(mapped, back, tn, precision=high)
    crossed = sum(
        lax.dot_general(term, basis, tn, preferred_element_type=jnp.float32) for term in split_wide(grad)
    )
    mapped_grad = lax.dot_general(mapped, grad, tn, precision=high)
    grad_gram = lax.dot_general(grad, grad, tn, precision=high)
    grad_back = lax.dot_general(grad, back, tn, precision=high)
    weight = 0.05 * mapped_grad + 0.00125 * lax.dot_general(crossed, grad_gram, tn, precision=high)
    gram = mapped_gram + lax.dot_general(
        jnp.concatenate([weight.T, crossed], axis=0),
        jnp.concatenate([crossed, weight.T], axis=0),
        tn,
        precision=high,
    )
    power_rows = lax.dynamic_slice_in_dim(mapped, row_start, rows_per, 0) + 0.05 * jnp.dot(
        grad_rows, crossed, precision=high
    )
    power_side = jnp.concatenate([mapped_back, mapped_grad], axis=1) + 0.05 * lax.dot_general(
        crossed, jnp.concatenate([grad_back, grad_gram], axis=1), tn, precision=high
    )
    right_new = 0.95 * right_factor + 0.05 * grad_gram
    right_power = jnp.dot(right_new, right_basis, precision=high)
    right_gram = lax.dot_general(right_power, right_power, tn, precision=high)
    solved, right_inverse = factor_solve(
        gram, jnp.concatenate([power_side, power_rows.T], axis=1), right_gram
    )
    turned_momentum = solved[:, :channels]
    turned_grad = solved[:, channels : 2 * channels]
    basis_new = solved[:, 2 * channels :].T
    right_basis_new = lax.dot_general(
        right_power, right_inverse, (((1,), (1,)), ((), ())), precision=high
    )
    right_turn = lax.dot_general(right_basis, right_basis_new, tn, precision=high)
    rotated = jnp.dot(turned_momentum, right_turn, precision=high)
    projected = jnp.dot(turned_grad, right_basis_new, precision=high)
    momentum_all = 0.9 * rotated + 0.1 * projected
    second_all = 0.95 * all_second + 0.05 * projected * projected
    normalized = momentum_all / (jnp.sqrt(second_all) + epsilon)
    momentum_new = lax.dynamic_slice_in_dim(momentum_all, moment_start, moment_rows, 0)
    second_new = lax.dynamic_slice_in_dim(second_all, moment_start, moment_rows, 0)
    update_rows = jnp.dot(basis_new, normalized, precision=high)
    update = lax.dot_general(
        update_rows, right_basis_new, (((1,), (1,)), ((), ())), precision=high
    )
    return (
        result,
        input_grad,
        grad,
        left_new,
        basis_new,
        right_new,
        right_basis_new,
        momentum_new,
        second_new,
        update,
    )


ZS = 4
CORES = 2
DPS = 4
LANES = 384


def to_device(source, target, send, receive, **device):
    return pltpu.make_async_remote_copy(
        src_ref=source,
        dst_ref=target,
        send_sem=send,
        recv_sem=receive,
        device_id=device,
        device_id_type=pl.DeviceIdType.MESH,
    )


def greet():
    t = lax.axis_index("tile")
    d = lax.axis_index("dp")
    barrier = pltpu.get_barrier_semaphore()
    tiles = ZS * CORES
    for step in range(1, tiles):
        pl.semaphore_signal(
            barrier,
            inc=1,
            device_id={"tile": lax.rem(t + step, tiles)},
            device_id_type=pl.DeviceIdType.MESH,
        )
    for step in range(1, DPS):
        pl.semaphore_signal(
            barrier,
            inc=1,
            device_id={"dp": lax.rem(d + step, DPS)},
            device_id_type=pl.DeviceIdType.MESH,
        )
    pl.semaphore_wait(barrier, tiles + DPS - 2)


class Edges:
    def __init__(self, source, target, send, receive):
        t = lax.axis_index("tile")
        row, col = t // 4, t % 4
        self.rooms = (row > 0, col < 3, row < 1, col > 0)
        self.target = target
        self.copies = []
        for h, step in enumerate((4, 1, 4, 7)):
            back = (h + 2) % 4
            peer = lax.rem(t + step, ZS * CORES)
            self.copies.append(
                to_device(source.at[h], target.at[back], send.at[h], receive.at[back], tile=peer)
            )

    def start(self):
        for h in range(4):

            @pl.when(self.rooms[h])
            def _():
                self.copies[h].start()

            @pl.when(jnp.logical_not(self.rooms[h]))
            def _():
                self.target[h] = jnp.zeros(self.target.shape[1:], self.target.dtype)

    def wait(self):
        for h in range(4):

            @pl.when(self.rooms[h])
            def _():
                self.copies[h].wait_send()
                self.copies[(h + 2) % 4].wait_recv()


def first_kernel(
    strips_ref,
    block_ref,
    back_ref,
    second_ref,
    borders_ref,
    basis_ref,
    piece_ref,
    seconds_ref,
    near,
    edge_send,
    edge_recv,
    z_send,
    z_recv,
    sib_send,
    sib_recv,
    back_send,
    back_recv,
    sec_send,
    sec_recv,
    pass_send,
    pass_recv,
):
    t = lax.axis_index("tile")
    d = lax.axis_index("dp")
    z, c = t // CORES, t % CORES
    sibling = t + 1 - 2 * c
    greet()
    edges = Edges(strips_ref, borders_ref, edge_send, edge_recv)
    edges.start()

    def z_copy(k):
        return to_device(
            block_ref, basis_ref.at[z, c], z_send.at[k - 1], z_recv.at[k - 1],
            tile=lax.rem(t + CORES * k, ZS * CORES),
        )

    def sib_copy(k):
        spot = lax.rem(z + ZS - k, ZS)
        source = block_ref if k == 0 else basis_ref.at[spot, c]
        return to_device(source, basis_ref.at[spot, c], sib_send.at[k], sib_recv.at[k], tile=sibling)

    def back_copy(j):
        peer = lax.rem(d + j, DPS)
        return to_device(
            back_ref.at[peer], near.at[j - 1], back_send.at[j - 1], back_recv.at[j - 1], dp=peer
        )

    def sec_copy(j):
        return to_device(
            second_ref.at[c], seconds_ref.at[d, c], sec_send.at[j - 1], sec_recv.at[j - 1],
            dp=lax.rem(d + j, DPS),
        )

    def pass_copy(j):
        spot = seconds_ref.at[lax.rem(d + DPS - j, DPS), c]
        return to_device(spot, spot, pass_send.at[j - 1], pass_recv.at[j - 1], tile=sibling)

    z_copies = [z_copy(k) for k in (1, 2, 3)]
    sib_copies = [sib_copy(k) for k in range(ZS)]
    back_copies = [back_copy(j) for j in (1, 2, 3)]
    sec_copies = [sec_copy(j) for j in (1, 2, 3)]
    pass_copies = [pass_copy(j) for j in (1, 2, 3)]
    for copy in z_copies + sib_copies[:1] + back_copies + sec_copies:
        copy.start()
    basis_ref[z, c] = block_ref[...]
    seconds_ref[d] = second_ref[...]
    for copy in back_copies:
        copy.wait_recv()
    total = back_ref[d]
    for slot in range(DPS - 1):
        total = total + near[slot]
    piece_ref[...] = total
    for j in range(DPS - 1):
        sec_copies[j].wait_recv()
        pass_copies[j].start()
    for k in range(1, ZS):
        z_copies[k - 1].wait_recv()
        sib_copies[k].start()
    edges.wait()
    for copy in back_copies + sec_copies + z_copies:
        copy.wait_send()
    for copy in sib_copies + pass_copies:
        copy.wait()


def first_exchange(strips, block, back, second):
    vmem = pl.BlockSpec(memory_space=pltpu.VMEM)
    rows = block.shape[0]
    half = second.shape[1:]
    piece = back.shape[1:]
    counts = [4, 4, 3, 3, 4, 4, 3, 3, 3, 3, 3, 3]
    return pl.pallas_call(
        first_kernel,
        out_shape=(
            jax.ShapeDtypeStruct(strips.shape, jnp.bfloat16),
            jax.ShapeDtypeStruct((ZS, CORES, rows, LANES), jnp.bfloat16),
            jax.ShapeDtypeStruct(piece, jnp.float32),
            jax.ShapeDtypeStruct((DPS, CORES) + half, jnp.float32),
        ),
        in_specs=[vmem] * 4,
        out_specs=(vmem,) * 4,
        scratch_shapes=[
            pltpu.VMEM((DPS - 1,) + piece, jnp.float32),
            *[pltpu.SemaphoreType.DMA((count,)) for count in counts],
        ],
        compiler_params=pltpu.CompilerParams(
            collective_id=0, has_side_effects=True, vmem_limit_bytes=40 * 1024 * 1024
        ),
        name="first_exchange",
    )(strips, block, back, second)


def second_kernel(
    grad_scale,
    partial_ref,
    piece_ref,
    mapped_ref,
    basis_ref,
    rims_ref,
    grad_ref,
    back_ref,
    all_ref,
    crossed_ref,
    incoming_ref,
    near,
    half,
    dp_in,
    pieces,
    z_in,
    spread_out,
    edge_send,
    edge_recv,
    half_send,
    half_recv,
    sum_send,
    sum_recv,
    zsum_send,
    zsum_recv,
    zall_send,
    zall_recv,
    dpall_send,
    dpall_recv,
    last_send,
    last_recv,
    mz_send,
    mz_recv,
    md_send,
    md_recv,
    ms_send,
    ms_recv,
    cd_send,
    cd_recv,
    cs_send,
    cs_recv,
):
    t = lax.axis_index("tile")
    d = lax.axis_index("dp")
    z, c = t // CORES, t % CORES
    other = 1 - c
    sibling = t + 1 - 2 * c
    z_peers = [lax.rem(t + CORES * k, ZS * CORES) for k in range(ZS)]
    z_from = [lax.rem(z + ZS - k, ZS) for k in range(ZS)]
    z_to = [lax.rem(z + k, ZS) for k in range(ZS)]
    d_to = [lax.rem(d + j, DPS) for j in range(DPS)]
    d_from = [lax.rem(d + DPS - j, DPS) for j in range(DPS)]
    rest = range(1, ZS)
    greet()

    swap = to_device(partial_ref.at[other], near, half_send, half_recv, tile=sibling)
    swap.start()
    edges = Edges(rims_ref, incoming_ref, edge_send, edge_recv)
    edges.start()
    m_z = [
        to_device(mapped_ref, all_ref.at[d, z, c], mz_send.at[k - 1], mz_recv.at[k - 1], tile=z_peers[k])
        for k in rest
    ]
    for copy in m_z:
        copy.start()
    all_ref[d, z, c] = mapped_ref[...]
    swap.wait_recv()
    half[...] = partial_ref[c] + near[...]

    sums = [
        to_device(half.at[d_to[j]], dp_in.at[j - 1], sum_send.at[j - 1], sum_recv.at[j - 1], dp=d_to[j])
        for j in rest
    ]
    for copy in sums:
        copy.start()

    def m_dp(j, k):
        spot = all_ref.at[d, z_from[k], c]
        source = mapped_ref if k == 0 else spot
        return to_device(source, spot, md_send.at[j - 1, k], md_recv.at[j - 1, k], dp=d_to[j])

    m_dps = [[m_dp(j, k) for j in rest] for k in range(ZS)]

    def m_sib(k):
        spot = all_ref.at[d, z_from[k], c]
        source = mapped_ref if k == 0 else spot
        return to_device(source, spot, ms_send.at[k], ms_recv.at[k], tile=sibling)

    m_sibs = [m_sib(k) for k in range(ZS)]
    for copy in m_dps[0] + m_sibs[:1]:
        copy.start()
    for copy in sums:
        copy.wait_recv()
    total = half[d]
    for slot in range(DPS - 1):
        total = total + dp_in[slot]
    piece = total.shape[0] // ZS
    for k in range(ZS):
        pieces[k] = total[k * piece : (k + 1) * piece]
    zsums = [
        to_device(pieces.at[z_to[k]], z_in.at[k - 1], zsum_send.at[k - 1], zsum_recv.at[k - 1], tile=z_peers[k])
        for k in rest
    ]
    for copy in zsums:
        copy.start()
    for copy in zsums:
        copy.wait_recv()
    total = pieces[z]
    for slot in range(ZS - 1):
        total = total + z_in[slot]
    spread_out[c, d, z, 0] = total
    spread_out[c, d, z, 1] = piece_ref[...]
    mine = spread_out.at[c, d, z]
    zalls = [
        to_device(mine, mine, zall_send.at[k - 1], zall_recv.at[k - 1], tile=z_peers[k]) for k in rest
    ]
    for copy in zalls:
        copy.start()
    for k in rest:
        m_z[k - 1].wait_recv()
    for copy in zalls:
        copy.wait_recv()
    slab = spread_out.at[c, d]
    dpalls = [
        to_device(slab, slab, dpall_send.at[j - 1], dpall_recv.at[j - 1], dp=d_to[j]) for j in rest
    ]
    for copy in dpalls:
        copy.start()
    for k in rest:
        for copy in m_dps[k]:
            copy.start()
        m_sibs[k].start()

    def last(j):
        spot = spread_out.at[c, d_from[j]]
        return to_device(spot, spot, last_send.at[j], last_recv.at[j], tile=sibling)

    lasts = [last(j) for j in range(DPS)]
    lasts[0].start()
    for j in rest:
        dpalls[j - 1].wait_recv()
        lasts[j].start()
    for copy in lasts:
        copy.wait_recv()
    for core in range(CORES):
        for dp in range(DPS):
            for line in range(ZS):
                at = ((core * DPS + dp) * ZS + line) * piece
                grad_ref[at : at + piece] = spread_out[core, dp, line, 0]
                to = ((line * CORES + core) * DPS + dp) * piece
                back_ref[to : to + piece] = spread_out[core, dp, line, 1]

    grad = grad_ref[...] * grad_scale
    grad_ref[...] = grad
    grad_hi, grad_lo = split(grad)
    columns = basis_ref[...].reshape(grad.shape[0], LANES)
    crossed = lax.dot_general(
        grad_hi, columns, tn, preferred_element_type=jnp.float32
    ) + lax.dot_general(grad_lo, columns, tn, preferred_element_type=jnp.float32)
    side = crossed.shape[0] // CORES
    crossed_ref[d, 0] = crossed[:side]
    crossed_ref[d, 1] = crossed[side:]
    own = crossed_ref.at[d, c]
    c_dps = [to_device(own, own, cd_send.at[j - 1], cd_recv.at[j - 1], dp=d_to[j]) for j in rest]
    for copy in c_dps:
        copy.start()

    def m_far(j):
        spot = all_ref.at[d_from[j], :, c]
        return to_device(spot, spot, ms_send.at[ZS + j - 1], ms_recv.at[ZS + j - 1], tile=sibling)

    m_fars = [m_far(j) for j in rest]
    for j in rest:
        for k in range(ZS):
            m_dps[k][j - 1].wait_recv()
        m_fars[j - 1].start()

    def c_sib(j):
        spot = crossed_ref.at[d_from[j], c]
        return to_device(spot, spot, cs_send.at[j - 1], cs_recv.at[j - 1], tile=sibling)

    c_sibs = [c_sib(j) for j in rest]
    for j in rest:
        c_dps[j - 1].wait_recv()
        c_sibs[j - 1].start()
    edges.wait()
    swap.wait_send()
    for copy in sums + zsums + zalls + dpalls + lasts + m_z + c_dps:
        copy.wait_send()
    for group in m_dps:
        for copy in group:
            copy.wait_send()
    for copy in m_sibs + m_fars + c_sibs:
        copy.wait()


def second_exchange(partial, piece, mapped, basis, rims, scale):
    vmem = pl.BlockSpec(memory_space=pltpu.VMEM)
    rows, channels = partial.shape
    block = rows // (CORES * DPS)
    dma = pltpu.SemaphoreType.DMA
    pair = [dma((3,)), dma((3,))]
    return pl.pallas_call(
        lambda *refs: second_kernel(scale, *refs),
        out_shape=(
            jax.ShapeDtypeStruct((rows, channels), jnp.float32),
            jax.ShapeDtypeStruct((rows, channels), jnp.float32),
            jax.ShapeDtypeStruct((DPS, ZS, CORES) + mapped.shape, jnp.bfloat16),
            jax.ShapeDtypeStruct((DPS, CORES, channels // CORES, LANES), jnp.float32),
            jax.ShapeDtypeStruct(rims.shape, jnp.bfloat16),
        ),
        in_specs=[vmem] * 5,
        out_specs=(vmem,) * 5,
        scratch_shapes=[
            pltpu.VMEM((DPS, block, channels), jnp.float32),
            pltpu.VMEM((DPS, block, channels), jnp.float32),
            pltpu.VMEM((DPS - 1, block, channels), jnp.float32),
            pltpu.VMEM((ZS, block // ZS, channels), jnp.float32),
            pltpu.VMEM((ZS - 1, block // ZS, channels), jnp.float32),
            pltpu.VMEM((CORES, DPS, ZS, 2, block // ZS, channels), jnp.float32),
            dma((4,)),
            dma((4,)),
            dma,
            dma,
            *(pair * 4),
            dma((4,)),
            dma((4,)),
            *pair,
            dma((3, 4)),
            dma((3, 4)),
            dma((7,)),
            dma((7,)),
            *(pair * 2),
        ],
        compiler_params=pltpu.CompilerParams(
            collective_id=1, has_side_effects=True, vmem_limit_bytes=48 * 1024 * 1024
        ),
        name="second_exchange",
    )(partial.reshape(CORES, DPS, block, channels), piece, mapped, basis, rims)


def wide_left(pair, axis=1):
    return jnp.concatenate([pair[0], pair[0], pair[1]], axis=axis)


def wide_right(pair, axis=0):
    return jnp.concatenate([pair[0], pair[1], pair[0]], axis=axis)


plain = (((1,), (0,)), ((), ()))


def product(left, right):
    return lax.dot_general(left, right, plain, preferred_element_type=jnp.float32)


def product_rows(left, right):
    return lax.dot_general(left, right, by_rows, preferred_element_type=jnp.float32)


def matmul(left, right):
    return product(wide_left(split(left)), wide_right(split(right)))


def matmul_rows(left, right):
    return product_rows(wide_left(split(left)), wide_right(split(right), 1))


def quick_leaf(block, cheap=2):
    row = lax.broadcasted_iota(jnp.int32, (LEAF, LEAF), 0)
    col = lax.broadcasted_iota(jnp.int32, (LEAF, LEAF), 1)
    on_diag = row == col
    below = row > col
    unit = jnp.where(on_diag, 1.0, 0.0)
    kept = jnp.where(on_diag, block, 0.0)
    across = lax.rsqrt(jnp.sum(kept, axis=0, keepdims=True))
    down = lax.rsqrt(jnp.sum(kept, axis=1, keepdims=True))

    def lower(gap):
        return jnp.where(below, gap, jnp.where(on_diag, 0.5 * gap, 0.0)).astype(jnp.bfloat16)

    high_part, low_part = split(block)
    guess = jnp.where(on_diag, down, jnp.where(below, -block * (across * across) * down, 0.0))
    for _ in range(cheap):
        rough = guess.astype(jnp.bfloat16)
        turned = product(rough, high_part).astype(jnp.bfloat16)
        gap = product_rows(turned, rough) - unit
        guess = rough.astype(jnp.float32) - product(lower(gap), rough)
    rough = guess.astype(jnp.bfloat16)
    twice = jnp.concatenate([rough, rough], axis=1)
    turned = product(twice, jnp.concatenate([high_part, low_part], axis=0))
    gap = product_rows(jnp.concatenate(split(turned), axis=1), twice) - unit
    return rough.astype(jnp.float32) - product(lower(gap), rough), jnp.abs(gap)


def finish_kernel(
    grad_ref,
    back_ref,
    mapped_ref,
    crossed_ref,
    factor_ref,
    right_factor_ref,
    right_basis_ref,
    second_ref,
    left_out,
    basis_out,
    right_out,
    right_basis_out,
    momentum_out,
    second_out,
    update_out,
    m_ref,
    left_ref,
    right_ref,
    work_ref,
    gram_ref,
    up_ref,
    down_ref,
    y_ref,
    inv_ref,
    aux_ref,
    big_ref,
):
    t = lax.axis_index("tile")
    d = lax.axis_index("dp")
    width, channels = grad_ref.shape
    blocks = width // LEAF
    rows_per = factor_ref.shape[0]
    moment_rows = momentum_out.shape[0]
    wide = work_ref.shape[1]
    own_rows = pl.ds(pl.multiple_of(t * rows_per, 16), rows_per)

    def tile_of(ref_slice, j):
        group, spot = divmod(j, 2)
        if spot:
            return ref_slice(group, 1)
        if group == 0:
            return ref_slice(0, 0)
        if group == DPS:
            return ref_slice(DPS - 1, 2)
        return ref_slice(group, 0) + ref_slice(group - 1, 2)

    for j in range(blocks):
        at = slice(j * LEAF, (j + 1) * LEAF)
        value = tile_of(lambda g, s: mapped_ref[g, :, s * LEAF : (s + 1) * LEAF], j)
        m_ref[:, at] = value
        left_ref[at, :width] = value.T
    crossed = jnp.concatenate(
        [tile_of(lambda g, s: crossed_ref[g, :, s * LEAF : (s + 1) * LEAF], j) for j in range(blocks)],
        axis=1,
    )
    grad = grad_ref[...]
    grad_t = grad.T
    both = jnp.concatenate([back_ref[...], grad], axis=1)
    both_pair = split(both)
    grad_both = product(wide_left(split(grad_t)), wide_right(both_pair))
    grad_gram = grad_both[:, channels:]
    grad_rows = grad_ref[own_rows, :]
    left_out[...] = 0.95 * factor_ref[...] + 0.05 * matmul_rows(grad_rows, grad)

    right_new = 0.95 * right_factor_ref[...] + 0.05 * grad_gram
    right_out[...] = right_new
    right_basis = right_basis_ref[...]
    right_power = matmul(right_new, right_basis)
    right_gram = matmul(right_power.T, right_power)
    right_inverse, right_gap = quick_leaf(right_gram, 4)
    inv_ref[...] = right_inverse

    grad_m = product(jnp.concatenate(split(grad_t), axis=0), m_ref[...])
    weight = 0.05 * (grad_m[:channels] + grad_m[channels:]) + 0.00125 * matmul(grad_gram, crossed)
    pair = jnp.concatenate([weight, crossed], axis=0)
    pair_t = pair.T
    left_ref[:, width:] = wide_left(split(pair_t))
    right_ref[...] = wide_right(split(jnp.concatenate([crossed, weight], axis=0)))
    for j in range(0, blocks, 2):
        end = min(j + 2, blocks) * LEAF
        at = slice(j * LEAF, end)
        value = product(left_ref[:end, :width], m_ref[:, at]) + product(
            left_ref[:end, width:], right_ref[:, at]
        )
        work_ref[:end, at] = value
        gram_ref[:end, at] = value
    m_both = product(left_ref[:, :width], both_pair[0]) + product(left_ref[:, :width], both_pair[1])
    crossed_t = pair_t[:, channels:]
    work_ref[:, width : width + 2 * channels] = m_both + 0.05 * matmul(crossed_t, grad_both)
    power_rows = m_ref[own_rows, :].astype(jnp.float32) + 0.05 * matmul(grad_rows, crossed)
    padded = jnp.concatenate(
        [power_rows, jnp.zeros((2 * LEAF - rows_per, width), jnp.float32)], axis=0
    )
    work_ref[:, width + 2 * channels :] = padded.T
    gram_ref[:, width:] = work_ref[:, width:]

    worst = right_gap
    for k in range(blocks):
        at = slice(k * LEAF, (k + 1) * LEAF)
        inverse, gap = quick_leaf(work_ref[at, at])
        worst = jnp.maximum(worst, gap)
        value = product(wide_left(split(inverse)), wide_right(split(work_ref[at, (k + 1) * LEAF :])))
        y_ref[at, :] = value[:, width - (k + 1) * LEAF :]
        if k == blocks - 1:
            break
        start = (k + 1) * LEAF
        up_ref[:, start:] = wide_right(split(value))
        down_ref[start:, :] = wide_left(split(value[:, : width - start].T))
        edges = list(range(start, width, 2 * LEAF))
        spans = [(a, min(a + 2 * LEAF, width)) for a in edges] + [
            (a, a + 2 * LEAF) for a in range(width, wide, 2 * LEAF)
        ]
        for a, b in spans:
            bottom = min(b, width)
            work_ref[start:bottom, a:b] -= product(down_ref[start:bottom, :], up_ref[:, a:b])

    @pl.when(jnp.logical_not(jnp.max(worst) <= 0.03))
    def _():
        leaf_inverse(right_gram, inv_ref, aux_ref)
        work_ref[...] = gram_ref[...]

        def block_step(k, carry):
            k0 = pl.multiple_of(k * LEAF, LEAF)
            leaf_inverse(work_ref[pl.ds(k0, LEAF), pl.ds(k0, LEAF)], big_ref, aux_ref)
            inverse = wide_left(split(big_ref[...]))
            for a in range(0, wide, LEAF):
                value = product(inverse, wide_right(split(work_ref[pl.ds(k0, LEAF), a : a + LEAF])))
                up_ref[:, a : a + LEAF] = wide_right(split(value))
                if a < width:
                    down_ref[a : a + LEAF, :] = wide_left(split(value.T))
                else:
                    y_ref[pl.ds(k0, LEAF), a - width : a - width + LEAF] = value

            def row_step(i, inner):
                i0 = pl.multiple_of(i * LEAF, LEAF)
                left = down_ref[pl.ds(i0, LEAF), :]
                for a in range(0, wide, LEAF):

                    @pl.when(a + LEAF > i0)
                    def _():
                        work_ref[pl.ds(i0, LEAF), a : a + LEAF] -= product(
                            left, up_ref[:, a : a + LEAF]
                        )

                return inner

            lax.fori_loop(k + 1, blocks, row_step, 0)
            return carry

        lax.fori_loop(0, blocks, block_step, 0)

    right_basis_new = matmul_rows(right_power, inv_ref[...])
    right_basis_out[...] = right_basis_new
    right_turn = matmul(right_basis.T, right_basis_new)
    solved = y_ref[...]
    rotated = matmul(solved[:, :channels], right_turn)
    projected = matmul(solved[:, channels : 2 * channels], right_basis_new)
    basis_new = solved[:, 2 * channels :].T[:rows_per]
    basis_out[...] = basis_new
    momentum = 0.9 * rotated + 0.1 * projected
    second = 0.95 * second_ref[...] + 0.05 * projected * projected
    up = momentum / (jnp.sqrt(second) + epsilon)
    update_rows = matmul(basis_new, up)
    update_out[...] = matmul_rows(update_rows, right_basis_new)
    y_ref[:, :channels] = momentum
    y_ref[:, channels : 2 * channels] = second
    own = pl.ds(pl.multiple_of(d * moment_rows, 8), moment_rows)
    momentum_out[...] = y_ref[own, :channels]
    second_out[...] = y_ref[own, channels : 2 * channels]


def finish(grad, back, mapped, crossed, left_factor, right_factor, right_basis, second, moment_rows):
    vmem = pl.BlockSpec(memory_space=pltpu.VMEM)
    width, channels = grad.shape
    rows_per = left_factor.shape[0]
    wide = width + 2 * channels + 2 * LEAF
    half = jnp.bfloat16
    single = jnp.float32
    square = pltpu.VMEM((LEAF, LEAF), single)
    shapes = [
        left_factor.shape,
        left_factor.shape,
        right_factor.shape,
        right_basis.shape,
        (moment_rows, channels),
        (moment_rows, channels),
        (rows_per, channels),
    ]
    return pl.pallas_call(
        finish_kernel,
        out_shape=tuple(jax.ShapeDtypeStruct(shape, single) for shape in shapes),
        in_specs=[vmem] * 8,
        out_specs=(vmem,) * 7,
        scratch_shapes=[
            pltpu.VMEM((width, width), half),
            pltpu.VMEM((width, width + 6 * channels), half),
            pltpu.VMEM((6 * channels, width), half),
            pltpu.VMEM((width, wide), single),
            pltpu.VMEM((width, wide), single),
            pltpu.VMEM((3 * LEAF, wide), half),
            pltpu.VMEM((width, 3 * LEAF), half),
            pltpu.VMEM((width, wide - width), single),
            square,
            square,
            square,
        ],
        compiler_params=pltpu.CompilerParams(vmem_limit_bytes=56 * 1024 * 1024),
        name="finish",
    )(grad, back, mapped, crossed, left_factor, right_factor, right_basis, second)


def by_direction(strips, turn):
    return lax.dynamic_slice_in_dim(jnp.concatenate([strips, strips], axis=0), turn, 4, 0)


def body_quick(
    activations,
    cotangent,
    kernel,
    turning,
    orient,
    left_factor,
    left_basis,
    right_factor,
    right_basis,
    momentum,
    second_moment,
):
    tiles, dp_count = ZS * CORES, DPS
    dp_index = lax.axis_index("dp")
    tile_vals = activations[:, 0]
    tile_grads = cotangent[:, 0]
    side = tile_vals.shape[1]
    channels = tile_vals.shape[-1]
    turn = turning[0]
    flipped = orient[0] >= 4
    rows_per, width = left_factor.shape
    part = left_basis.shape[1]
    moment_rows = momentum.shape[0]

    strips = by_direction(edge_strips(tile_vals)[:, 0], (4 - turn) % 4)
    block = lax.dynamic_update_slice(
        jnp.zeros((rows_per, LANES), jnp.bfloat16),
        left_basis.astype(jnp.bfloat16),
        (0, dp_index * (part % LEAF)),
    )
    back = jnp.dot(left_basis, momentum, precision=high)
    borders, basis, piece, seconds = first_exchange(
        strips,
        block,
        back.reshape(DPS, rows_per // DPS, channels),
        second_moment.reshape(CORES, moment_rows // CORES, channels),
    )
    all_second = seconds.reshape(width, channels)
    borders = flip_edges(by_direction(borders, turn)[:, None], flipped)
    padded = assemble(tile_vals, borders)
    columns = tap_patches(padded, side)
    flat_grads = tile_grads.reshape(-1, channels)
    partial_grad = lax.dot_general(
        columns, flat_grads, (((0,), (0,)), ((), ())), preferred_element_type=jnp.float32
    )
    spread = spread_back(flat_grads, kernel, 1, side)
    rims = by_direction(cycle_strips(spread).astype(jnp.bfloat16)[:, 0], (4 - turn) % 4)
    factor_hi, factor_lo = split_wide(left_factor)
    flat_basis = basis.reshape(width, LANES)
    mapped = 0.95 * (
        jnp.dot(factor_hi, flat_basis, preferred_element_type=jnp.float32)
        + jnp.dot(factor_lo, flat_basis, preferred_element_type=jnp.float32)
    )
    cells = dp_count * tiles * side * side
    grad, back, mapped, crossed, incoming = second_exchange(
        partial_grad, piece, mapped.astype(jnp.bfloat16), basis, rims, 1.0 / math.sqrt(cells)
    )
    result = jnp.dot(columns, kernel, preferred_element_type=jnp.float32).astype(jnp.bfloat16)
    result = result.reshape(activations.shape)
    incoming = flip_edges(by_direction(incoming, turn)[:, None], flipped)
    input_grad = absorb_rims(spread[:, 1:-1, 1:-1], incoming.astype(jnp.float32)).astype(
        jnp.bfloat16
    )
    input_grad = input_grad.reshape(cotangent.shape)
    left_new, basis_new, right_new, right_basis_new, momentum_new, second_new, update = finish(
        grad,
        back,
        mapped.reshape(DPS, width, LANES),
        crossed.reshape(DPS, channels, LANES),
        left_factor,
        right_factor,
        right_basis,
        all_second,
        moment_rows,
    )
    return (
        result,
        input_grad,
        grad,
        left_new,
        basis_new,
        right_new,
        right_basis_new,
        momentum_new,
        second_new,
        update,
    )


def body(*args):
    tiles = lax.axis_size("tile")
    dp_count = lax.axis_size("dp")
    left_basis = args[6]
    samples = args[0].shape[0]
    if (tiles, dp_count, samples) == (ZS * CORES, DPS, 1) and left_basis.shape == (144, 288):
        return body_quick(*args)
    return body_plain(*args)


def solution(mesh):
    placed = (
        P(("group", "dp"), "tile", None, None, None),
        P(("group", "dp"), "tile", None, None, None),
        P("group", None),
        P("tile"),
        P("tile", None),
        P(("group", "tile"), None),
        P(("group", "tile"), "dp"),
        P("group", None),
        P("group", None),
        P(("group", "dp"), None),
        P(("group", "dp"), None),
    )
    return jax.shard_map(
        body,
        mesh=mesh,
        in_specs=placed,
        out_specs=(
            P(("group", "dp"), "tile", None, None, None),
            P(("group", "dp"), "tile", None, None, None),
            P("group", None),
            P(("group", "tile"), None),
            P(("group", "tile"), None),
            P("group", None),
            P("group", None),
            P(("group", "dp"), None),
            P(("group", "dp"), None),
            P(("group", "tile"), None),
        ),
        check_vma=False,
    )
```

```python
import math

import jax
import jax.numpy as jnp
from jax import lax
from jax.experimental import pallas as pl
from jax.experimental.pallas import tpu as pltpu
from jax.sharding import PartitionSpec as P

highest = lax.Precision.HIGHEST
epsilon = 1e-08


def edge_strips(values):
    return jnp.stack(
        [values[..., 0, :, :], values[..., :, -1, :], values[..., -1, :, :], values[..., :, 0, :]],
        axis=0,
    )


def cycle_strips(spread):
    return jnp.stack(
        [spread[:, 0, 1:-1], spread[:, 1:-1, -1], spread[:, -1, 1:-1], spread[:, 1:-1, 0]], axis=0
    )


def assemble(tile_vals, borders):
    middle = jnp.concatenate(
        [borders[3][:, :, None, :], tile_vals, borders[1][:, :, None, :]], axis=2
    )
    top_row = jnp.pad(borders[0], ((0, 0), (1, 1), (0, 0)))[:, None]
    bottom_row = jnp.pad(borders[2], ((0, 0), (1, 1), (0, 0)))[:, None]
    return jnp.concatenate([top_row, middle, bottom_row], axis=1)


def tap_patches(padded, side):
    pieces = [
        padded[:, row_off : row_off + side, col_off : col_off + side, :]
        for row_off in range(3)
        for col_off in range(3)
    ]
    joined = jnp.concatenate(pieces, axis=-1)
    return joined.reshape(-1, joined.shape[-1])


def spread_back(flat_grads, kernel, sample_count, side):
    channels = kernel.shape[1]
    summed = jnp.zeros((sample_count, side + 2, side + 2, channels), jnp.float32)
    for tap_index in range(9):
        row_off, col_off = divmod(tap_index, 3)
        weight_tap = kernel[tap_index * channels : (tap_index + 1) * channels]
        contrib = lax.dot_general(
            flat_grads, weight_tap, (((1,), (1,)), ((), ())), preferred_element_type=jnp.float32
        )
        contrib = contrib.reshape(sample_count, side, side, channels)
        summed = summed + jnp.pad(
            contrib, ((0, 0), (row_off, 2 - row_off), (col_off, 2 - col_off), (0, 0))
        )
    return summed


def absorb_rims(interior, incoming):
    result = interior.at[..., 0, :, :].add(incoming[0])
    result = result.at[..., :, -1, :].add(incoming[1])
    result = result.at[..., -1, :, :].add(incoming[2])
    return result.at[..., :, 0, :].add(incoming[3])


def flip_edges(strips, flipped):
    return jnp.where(flipped[:, None, None, None], strips[:, :, ::-1, :], strips)


def pick_gathered(everything, near_tiles, facing, flipped, usable):
    flat = everything.reshape(everything.shape[0] * 4, -1)
    wanted = jnp.where(usable, near_tiles * 4 + facing, -1)
    selector = (lax.broadcasted_iota(jnp.int32, (4, flat.shape[0]), 1) == wanted[:, None]).astype(
        jnp.bfloat16
    )
    picked = jnp.dot(selector, flat, preferred_element_type=jnp.float32).astype(jnp.bfloat16)
    return flip_edges(picked.reshape((4,) + everything.shape[2:]), flipped)


LEAF = 128
SPAN = 384


def split(value):
    high = value.astype(jnp.bfloat16)
    return high, (value - high.astype(jnp.float32)).astype(jnp.bfloat16)


def split_wide(value):
    high = lax.reduce_precision(value, 8, 7)
    return high.astype(jnp.bfloat16), (value - high).astype(jnp.bfloat16)


def dot3(left, right, dims=(((1,), (0,)), ((), ()))):
    def one(a, b):
        return lax.dot_general(a, b, dims, preferred_element_type=jnp.float32)

    return one(left[0], right[0]) + (one(left[0], right[1]) + one(left[1], right[0]))


by_rows = (((1,), (1,)), ((), ()))


def leaf_inverse(block, m_ref, s_ref):
    row = lax.broadcasted_iota(jnp.int32, (LEAF, LEAF), 0)
    col = lax.broadcasted_iota(jnp.int32, (LEAF, LEAF), 1)
    on_diag = row == col
    unit = jnp.where(on_diag, 1.0, 0.0)
    kept = jnp.where(on_diag, block, 0.0)
    across = lax.rsqrt(jnp.sum(kept, axis=0, keepdims=True))
    down = lax.rsqrt(jnp.sum(kept, axis=1, keepdims=True))
    scaled = block * across * down
    m_ref[...] = jnp.where(on_diag, down, jnp.where(row > col, -scaled * across, 0.0))
    pair = split(block)
    rough = m_ref[...].astype(jnp.bfloat16)
    turned = jnp.dot(rough, pair[0], preferred_element_type=jnp.float32).astype(jnp.bfloat16)
    gap = lax.dot_general(turned, rough, by_rows, preferred_element_type=jnp.float32) - unit
    low = jnp.where(row > col, gap, jnp.where(on_diag, 0.5 * gap, 0.0)).astype(jnp.bfloat16)
    m_ref[...] -= jnp.dot(low, rough, preferred_element_type=jnp.float32)

    def more(carry):
        step, error = carry
        return (step < 12) & (error > 1e-4)

    def refine(carry):
        step, _ = carry
        guess = m_ref[...]
        guess_pair = split(guess)
        turned = dot3(guess_pair, pair)
        gap = dot3(split(turned), guess_pair, by_rows) - unit
        error = jnp.max(jnp.abs(gap))
        low = jnp.where(row > col, gap, jnp.where(on_diag, 0.5 * gap, 0.0))
        m_ref[...] = guess - dot3(split(low), guess_pair)
        return step + 1, error

    _, error = lax.while_loop(more, refine, (jnp.int32(0), jnp.float32(1.0)))

    @pl.when(jnp.logical_not(error <= 1e-4))
    def _():
        s_ref[...] = block
        m_ref[...] = unit

        def eliminate(j, carry):
            work = s_ref[...]
            line = s_ref[pl.ds(j, 1), :]
            lane = lax.broadcasted_iota(jnp.int32, (1, LEAF), 1)
            scale = lax.rsqrt(jnp.sum(jnp.where(lane == j, line, 0.0), axis=1, keepdims=True))
            column = jnp.sum(jnp.where(col == j, work, 0.0), axis=1, keepdims=True)
            side = lax.broadcasted_iota(jnp.int32, (LEAF, 1), 0)
            column = jnp.where(side > j, column * scale, 0.0)
            s_ref[...] = work - column * (line * scale)
            mine = m_ref[pl.ds(j, 1), :] * scale
            m_ref[...] = m_ref[...] - column * mine
            m_ref[pl.ds(j, 1), :] = mine
            return carry

        lax.fori_loop(0, LEAF, eliminate, 0)


def factor_kernel(
    gram_ref, side_ref, small_ref, y_ref, small_out_ref, a_ref, uh, ul, uth, utl, yh, yl, m_ref, s_ref
):
    width = gram_ref.shape[1]
    blocks = width // LEAF
    spans = width // SPAN
    leaf_inverse(small_ref[...], m_ref, s_ref)
    small_out_ref[...] = m_ref[...]
    a_ref[...] = gram_ref[...]
    y_ref[...] = side_ref[...]

    def block_step(k, carry):
        k0 = pl.multiple_of(k * LEAF, LEAF)
        leaf_inverse(a_ref[pl.ds(k0, LEAF), pl.ds(k0, LEAF)], m_ref, s_ref)
        inverse = split(m_ref[...])
        for span in range(spans):
            part = slice(span * SPAN, (span + 1) * SPAN)

            @pl.when((span + 1) * SPAN > k0 + LEAF)
            def _():
                value = dot3(inverse, split(a_ref[pl.ds(k0, LEAF), part]))
                uh[:, part], ul[:, part] = split(value)
                uth[part, :], utl[part, :] = split(value.T)

        value = dot3(inverse, split(y_ref[pl.ds(k0, LEAF), :]))
        y_ref[pl.ds(k0, LEAF), :] = value
        yh[...], yl[...] = split(value)

        def row_step(i, inner):
            i0 = pl.multiple_of(i * LEAF, LEAF)
            left = uth[pl.ds(i0, LEAF), :], utl[pl.ds(i0, LEAF), :]
            for span in range(spans):
                part = slice(span * SPAN, (span + 1) * SPAN)

                @pl.when((span + 1) * SPAN > i0)
                def _():
                    a_ref[pl.ds(i0, LEAF), part] -= dot3(left, (uh[:, part], ul[:, part]))

            y_ref[pl.ds(i0, LEAF), :] -= dot3(left, (yh[...], yl[...]))
            return inner

        lax.fori_loop(k + 1, blocks, row_step, 0)
        return carry

    lax.fori_loop(0, blocks, block_step, 0)


def factor_solve(gram, side, small):
    width, columns = side.shape
    vmem = pl.BlockSpec(memory_space=pltpu.VMEM)
    half = jnp.bfloat16
    return pl.pallas_call(
        factor_kernel,
        out_shape=(
            jax.ShapeDtypeStruct(side.shape, jnp.float32),
            jax.ShapeDtypeStruct(small.shape, jnp.float32),
        ),
        in_specs=[vmem] * 3,
        out_specs=(vmem, vmem),
        scratch_shapes=[
            pltpu.VMEM((width, width), jnp.float32),
            pltpu.VMEM((LEAF, width), half),
            pltpu.VMEM((LEAF, width), half),
            pltpu.VMEM((width, LEAF), half),
            pltpu.VMEM((width, LEAF), half),
            pltpu.VMEM((LEAF, columns), half),
            pltpu.VMEM((LEAF, columns), half),
            pltpu.VMEM((LEAF, LEAF), jnp.float32),
            pltpu.VMEM((LEAF, LEAF), jnp.float32),
        ],
        compiler_params=pltpu.CompilerParams(vmem_limit_bytes=40 * 1024 * 1024),
        name="factor_solve",
    )(gram, side, small)


high = lax.Precision.HIGH
tn = (((0,), (0,)), ((), ()))


def sum_kernel(dp_count, tiles, x_ref, out_ref, near, part, far, *sems):
    dp_index = lax.axis_index("dp")
    tile_index = lax.axis_index("tile")
    dp_peers = [lax.rem(dp_index + step, dp_count) for step in range(1, dp_count)]
    tile_peers = [lax.rem(tile_index + step, tiles) for step in range(1, tiles)]
    barrier = pltpu.get_barrier_semaphore()
    for axis, peers in (("dp", dp_peers), ("tile", tile_peers)):
        for peer in peers:
            pl.semaphore_signal(
                barrier, inc=1, device_id={axis: peer}, device_id_type=pl.DeviceIdType.MESH
            )
    pl.semaphore_wait(barrier, dp_count + tiles - 2)

    def exchange(axis, peers, source, target, send, receive):
        copies = [
            pltpu.make_async_remote_copy(
                src_ref=source(peer),
                dst_ref=target(slot),
                send_sem=send.at[slot],
                recv_sem=receive.at[slot],
                device_id={axis: peer},
                device_id_type=pl.DeviceIdType.MESH,
            )
            for slot, peer in enumerate(peers)
        ]
        for copy in copies:
            copy.start()
        for copy in copies:
            copy.wait()

    exchange("dp", dp_peers, lambda peer: x_ref.at[peer], lambda slot: near.at[slot], *sems[0:2])
    total = x_ref[dp_index]
    for slot in range(dp_count - 1):
        total = total + near[slot]
    part[...] = total
    exchange("tile", tile_peers, lambda peer: part.at[peer], lambda slot: far.at[slot], *sems[2:4])
    total = part[tile_index]
    for slot in range(tiles - 1):
        total = total + far[slot]
    out_ref[dp_index, tile_index] = total
    own = out_ref.at[dp_index, tile_index]
    exchange("tile", tile_peers, lambda peer: own, lambda slot: own, *sems[4:6])
    slab = out_ref.at[dp_index]
    exchange("dp", dp_peers, lambda peer: slab, lambda slot: slab, *sems[6:8])


def sum_everywhere(value):
    tiles = lax.axis_size("tile")
    dp_count = lax.axis_size("dp")
    rows, columns = value.shape
    if tiles < 2 or dp_count < 2 or rows % (tiles * dp_count):
        return lax.psum(value, ("tile", "dp"))
    piece = rows // (tiles * dp_count)
    vmem = pl.BlockSpec(memory_space=pltpu.VMEM)
    wide = (dp_count, tiles, piece, columns)
    counts = [dp_count - 1] * 2 + [tiles - 1] * 4 + [dp_count - 1] * 2
    out = pl.pallas_call(
        lambda *refs: sum_kernel(dp_count, tiles, *refs),
        out_shape=jax.ShapeDtypeStruct(wide, jnp.float32),
        in_specs=[vmem],
        out_specs=vmem,
        scratch_shapes=[
            pltpu.VMEM((dp_count - 1, tiles, piece, columns), jnp.float32),
            pltpu.VMEM((tiles, piece, columns), jnp.float32),
            pltpu.VMEM((tiles - 1, piece, columns), jnp.float32),
            *[pltpu.SemaphoreType.DMA((count,)) for count in counts],
        ],
        compiler_params=pltpu.CompilerParams(collective_id=0, has_side_effects=True),
        name="sum_everywhere",
    )(value.reshape(wide))
    return out.reshape(rows, columns)


def body_plain(
    activations,
    cotangent,
    kernel,
    turning,
    orient,
    left_factor,
    left_basis,
    right_factor,
    right_basis,
    momentum,
    second_moment,
):
    tiles = lax.axis_size("tile")
    dp_count = lax.axis_size("dp")
    tile_index = lax.axis_index("tile")
    dp_index = lax.axis_index("dp")
    tile_vals = activations[:, 0]
    tile_grads = cotangent[:, 0]
    sample_count = tile_vals.shape[0]
    side = tile_vals.shape[1]
    channels = tile_vals.shape[-1]
    own_turn = turning[0]
    facing = orient[0] % 4
    flipped = orient[0] >= 4
    heading = (jnp.arange(4, dtype=jnp.int32) + own_turn) % 4
    row_of = tile_index // 4
    col_of = tile_index % 4
    room = jnp.stack([row_of > 0, col_of < 3, row_of < tiles // 4 - 1, col_of > 0])
    usable = (
        jnp.sum(
            jnp.where(
                heading[:, None] == jnp.arange(4, dtype=jnp.int32)[None, :], room[None, :], False
            ),
            axis=1,
        )
        > 0
    )
    offsets = jnp.array([-4, 1, 4, -1], dtype=jnp.int32)
    near_tiles = tile_index + jnp.sum(
        jnp.where(heading[:, None] == jnp.arange(4, dtype=jnp.int32)[None, :], offsets[None, :], 0),
        axis=1,
    )
    strips = edge_strips(tile_vals)
    flat_grads = tile_grads.reshape(-1, channels)
    spread = spread_back(flat_grads, kernel, sample_count, side)
    rim_cells = cycle_strips(spread).astype(jnp.bfloat16)
    everything = lax.all_gather(
        jnp.concatenate([strips, rim_cells], axis=0)[None], "tile", axis=0, tiled=True
    )
    borders = pick_gathered(everything[:, :4], near_tiles, facing, flipped, usable)
    incoming = pick_gathered(everything[:, 4:], near_tiles, facing, flipped, usable)
    padded = assemble(tile_vals, borders)
    columns = tap_patches(padded, side)
    partial_grad = lax.dot_general(
        columns, flat_grads, (((0,), (0,)), ((), ())), preferred_element_type=jnp.float32
    )
    summed_grad = sum_everywhere(partial_grad)
    result = jnp.dot(columns, kernel, preferred_element_type=jnp.float32).astype(jnp.bfloat16)
    result = result.reshape(activations.shape)
    input_grad = absorb_rims(spread[:, 1:-1, 1:-1], incoming.astype(jnp.float32)).astype(
        jnp.bfloat16
    )
    input_grad = input_grad.reshape(cotangent.shape)
    cells = dp_count * sample_count * tiles * side * side
    grad = summed_grad * (1.0 / math.sqrt(cells))
    rows_per, width = left_factor.shape
    row_start = tile_index * rows_per
    moment_rows = momentum.shape[0]
    moment_start = dp_index * moment_rows
    grad_rows = lax.dynamic_slice_in_dim(grad, row_start, rows_per, 0)
    left_new = 0.95 * left_factor + 0.05 * lax.dot_general(
        grad_rows, grad, (((1,), (1,)), ((), ())), precision=high
    )
    basis_rows = lax.all_gather(left_basis, "dp", axis=1, tiled=True)
    basis = lax.all_gather(basis_rows.astype(jnp.bfloat16), "tile", axis=0, tiled=True)
    moments = lax.all_gather(
        jnp.concatenate([momentum, second_moment], axis=1), "dp", axis=0, tiled=True
    )
    all_momentum, all_second = moments[:, :channels], moments[:, channels:]
    back_rows = jnp.dot(basis_rows, all_momentum, precision=highest)
    own_row = row_start + lax.broadcasted_iota(jnp.int32, left_factor.shape, 0)
    own_col = lax.broadcasted_iota(jnp.int32, left_factor.shape, 1)
    diagonal = jnp.sum(jnp.where(own_row == own_col, left_factor, 0.0), axis=1, keepdims=True)
    rest = jnp.broadcast_to(split_wide(diagonal)[1], (rows_per, LEAF))
    factor = lax.all_gather(
        jnp.concatenate(
            [left_factor.astype(jnp.bfloat16), *split_wide(back_rows), rest], axis=1
        ),
        "tile",
        axis=0,
        tiled=True,
    )
    back = factor[:, width : width + channels].astype(jnp.float32) + factor[
        :, width + channels : width + 2 * channels
    ].astype(jnp.float32)
    rest = factor[:, width + 2 * channels : width + 2 * channels + 1]
    factor = factor[:, :width]
    mapped = 0.95 * (
        jnp.dot(factor, basis, preferred_element_type=jnp.float32)
        + rest.astype(jnp.float32) * basis.astype(jnp.float32)
    )
    mapped_gram = lax.dot_general(mapped, mapped, tn, precision=high)
    mapped_back = lax.dot_general(mapped, back, tn, precision=high)
    crossed = sum(
        lax.dot_general(term, basis, tn, preferred_element_type=jnp.float32) for term in split_wide(grad)
    )
    mapped_grad = lax.dot_general(mapped, grad, tn, precision=high)
    grad_gram = lax.dot_general(grad, grad, tn, precision=high)
    grad_back = lax.dot_general(grad, back, tn, precision=high)
    weight = 0.05 * mapped_grad + 0.00125 * lax.dot_general(crossed, grad_gram, tn, precision=high)
    gram = mapped_gram + lax.dot_general(
        jnp.concatenate([weight.T, crossed], axis=0),
        jnp.concatenate([crossed, weight.T], axis=0),
        tn,
        precision=high,
    )
    power_rows = lax.dynamic_slice_in_dim(mapped, row_start, rows_per, 0) + 0.05 * jnp.dot(
        grad_rows, crossed, precision=high
    )
    power_side = jnp.concatenate([mapped_back, mapped_grad], axis=1) + 0.05 * lax.dot_general(
        crossed, jnp.concatenate([grad_back, grad_gram], axis=1), tn, precision=high
    )
    right_new = 0.95 * right_factor + 0.05 * grad_gram
    right_power = jnp.dot(right_new, right_basis, precision=high)
    right_gram = lax.dot_general(right_power, right_power, tn, precision=high)
    solved, right_inverse = factor_solve(
        gram, jnp.concatenate([power_side, power_rows.T], axis=1), right_gram
    )
    turned_momentum = solved[:, :channels]
    turned_grad = solved[:, channels : 2 * channels]
    basis_new = solved[:, 2 * channels :].T
    right_basis_new = lax.dot_general(
        right_power, right_inverse, (((1,), (1,)), ((), ())), precision=high
    )
    right_turn = lax.dot_general(right_basis, right_basis_new, tn, precision=high)
    rotated = jnp.dot(turned_momentum, right_turn, precision=high)
    projected = jnp.dot(turned_grad, right_basis_new, precision=high)
    momentum_all = 0.9 * rotated + 0.1 * projected
    second_all = 0.95 * all_second + 0.05 * projected * projected
    normalized = momentum_all / (jnp.sqrt(second_all) + epsilon)
    momentum_new = lax.dynamic_slice_in_dim(momentum_all, moment_start, moment_rows, 0)
    second_new = lax.dynamic_slice_in_dim(second_all, moment_start, moment_rows, 0)
    update_rows = jnp.dot(basis_new, normalized, precision=high)
    update = lax.dot_general(
        update_rows, right_basis_new, (((1,), (1,)), ((), ())), precision=high
    )
    return (
        result,
        input_grad,
        grad,
        left_new,
        basis_new,
        right_new,
        right_basis_new,
        momentum_new,
        second_new,
        update,
    )


ZS = 4
CORES = 2
DPS = 4
LANES = 384
CELL = 24


def to_device(source, target, send, receive, **device):
    return pltpu.make_async_remote_copy(
        src_ref=source,
        dst_ref=target,
        send_sem=send,
        recv_sem=receive,
        device_id=device,
        device_id_type=pl.DeviceIdType.MESH,
    )


def greet():
    t = lax.axis_index("tile")
    d = lax.axis_index("dp")
    barrier = pltpu.get_barrier_semaphore()
    tiles = ZS * CORES
    for step in range(1, tiles):
        pl.semaphore_signal(
            barrier,
            inc=1,
            device_id={"tile": lax.rem(t + step, tiles)},
            device_id_type=pl.DeviceIdType.MESH,
        )
    for step in range(1, DPS):
        pl.semaphore_signal(
            barrier,
            inc=1,
            device_id={"dp": lax.rem(d + step, DPS)},
            device_id_type=pl.DeviceIdType.MESH,
        )
    pl.semaphore_wait(barrier, tiles + DPS - 2)


class Edges:
    def __init__(self, source, target, send, receive):
        t = lax.axis_index("tile")
        row, col = t // 4, t % 4
        self.rooms = (row > 0, col < 3, row < 1, col > 0)
        self.target = target
        self.copies = []
        for h, step in enumerate((4, 1, 4, 7)):
            back = (h + 2) % 4
            peer = lax.rem(t + step, ZS * CORES)
            self.copies.append(
                to_device(source.at[h], target.at[back], send.at[h], receive.at[back], tile=peer)
            )

    def start(self):
        for h in range(4):

            @pl.when(self.rooms[h])
            def _():
                self.copies[h].start()

            @pl.when(jnp.logical_not(self.rooms[h]))
            def _():
                self.target[h] = jnp.zeros(self.target.shape[1:], self.target.dtype)

    def wait(self):
        for h in range(4):

            @pl.when(self.rooms[h])
            def _():
                self.copies[h].wait_send()
                self.copies[(h + 2) % 4].wait_recv()


def wide_left(pair, axis=1):
    return jnp.concatenate([pair[0], pair[0], pair[1]], axis=axis)


def wide_right(pair, axis=0):
    return jnp.concatenate([pair[0], pair[1], pair[0]], axis=axis)


plain = (((1,), (0,)), ((), ()))


def product(left, right):
    return lax.dot_general(left, right, plain, preferred_element_type=jnp.float32)


def product_rows(left, right):
    return lax.dot_general(left, right, by_rows, preferred_element_type=jnp.float32)


def matmul(left, right):
    return product(wide_left(split(left)), wide_right(split(right)))


def matmul_rows(left, right):
    return product_rows(wide_left(split(left)), wide_right(split(right), 1))


def quick_leaf(block, cheap=2):
    row = lax.broadcasted_iota(jnp.int32, (LEAF, LEAF), 0)
    col = lax.broadcasted_iota(jnp.int32, (LEAF, LEAF), 1)
    on_diag = row == col
    below = row > col
    unit = jnp.where(on_diag, 1.0, 0.0)
    kept = jnp.where(on_diag, block, 0.0)
    across = lax.rsqrt(jnp.sum(kept, axis=0, keepdims=True))
    down = lax.rsqrt(jnp.sum(kept, axis=1, keepdims=True))

    def lower(gap):
        return jnp.where(below, gap, jnp.where(on_diag, 0.5 * gap, 0.0)).astype(jnp.bfloat16)

    high_part, low_part = split(block)
    guess = jnp.where(on_diag, down, jnp.where(below, -block * (across * across) * down, 0.0))
    for _ in range(cheap):
        rough = guess.astype(jnp.bfloat16)
        turned = product(rough, high_part).astype(jnp.bfloat16)
        gap = product_rows(turned, rough) - unit
        guess = rough.astype(jnp.float32) - product(lower(gap), rough)
    rough = guess.astype(jnp.bfloat16)
    twice = jnp.concatenate([rough, rough], axis=1)
    turned = product(twice, jnp.concatenate([high_part, low_part], axis=0))
    gap = product_rows(jnp.concatenate(split(turned), axis=1), twice) - unit
    return rough.astype(jnp.float32) - product(lower(gap), rough), jnp.abs(gap)


def finish_kernel(
    grad_ref,
    back_ref,
    mapped_ref,
    crossed_ref,
    factor_ref,
    right_factor_ref,
    right_basis_ref,
    second_ref,
    left_out,
    basis_out,
    right_out,
    right_basis_out,
    momentum_out,
    second_out,
    update_out,
    m_ref,
    left_ref,
    right_ref,
    work_ref,
    gram_ref,
    up_ref,
    down_ref,
    y_ref,
    inv_ref,
    aux_ref,
    big_ref,
):
    t = lax.axis_index("tile")
    d = lax.axis_index("dp")
    width, channels = grad_ref.shape
    blocks = width // LEAF
    rows_per = factor_ref.shape[0]
    moment_rows = momentum_out.shape[0]
    wide = work_ref.shape[1]
    own_rows = pl.ds(pl.multiple_of(t * rows_per, 16), rows_per)

    def tile_of(ref_slice, j):
        group, spot = divmod(j, 2)
        if spot:
            return ref_slice(group, 1)
        if group == 0:
            return ref_slice(0, 0)
        if group == DPS:
            return ref_slice(DPS - 1, 2)
        return ref_slice(group, 0) + ref_slice(group - 1, 2)

    for j in range(blocks):
        at = slice(j * LEAF, (j + 1) * LEAF)
        value = tile_of(lambda g, s: mapped_ref[g, :, s * LEAF : (s + 1) * LEAF], j)
        m_ref[:, at] = value
        left_ref[at, :width] = value.T
    crossed = jnp.concatenate(
        [tile_of(lambda g, s: crossed_ref[g, :, s * LEAF : (s + 1) * LEAF], j) for j in range(blocks)],
        axis=1,
    )
    grad = grad_ref[...]
    grad_t = grad.T
    both = jnp.concatenate([back_ref[...], grad], axis=1)
    both_pair = split(both)
    grad_both = product(wide_left(split(grad_t)), wide_right(both_pair))
    grad_gram = grad_both[:, channels:]
    grad_rows = grad_ref[own_rows, :]
    left_out[...] = 0.95 * factor_ref[...] + 0.05 * matmul_rows(grad_rows, grad)

    right_new = 0.95 * right_factor_ref[...] + 0.05 * grad_gram
    right_out[...] = right_new
    right_basis = right_basis_ref[...]
    right_power = matmul(right_new, right_basis)
    right_gram = matmul(right_power.T, right_power)
    right_inverse, right_gap = quick_leaf(right_gram, 4)
    inv_ref[...] = right_inverse

    grad_m = product(jnp.concatenate(split(grad_t), axis=0), m_ref[...])
    weight = 0.05 * (grad_m[:channels] + grad_m[channels:]) + 0.00125 * matmul(grad_gram, crossed)
    pair = jnp.concatenate([weight, crossed], axis=0)
    pair_t = pair.T
    left_ref[:, width:] = wide_left(split(pair_t))
    right_ref[...] = wide_right(split(jnp.concatenate([crossed, weight], axis=0)))
    for j in range(0, blocks, 2):
        end = min(j + 2, blocks) * LEAF
        at = slice(j * LEAF, end)
        value = product(left_ref[:end, :width], m_ref[:, at]) + product(
            left_ref[:end, width:], right_ref[:, at]
        )
        work_ref[:end, at] = value
        gram_ref[:end, at] = value
    m_both = product(left_ref[:, :width], both_pair[0]) + product(left_ref[:, :width], both_pair[1])
    crossed_t = pair_t[:, channels:]
    work_ref[:, width : width + 2 * channels] = m_both + 0.05 * matmul(crossed_t, grad_both)
    power_rows = m_ref[own_rows, :].astype(jnp.float32) + 0.05 * matmul(grad_rows, crossed)
    padded = jnp.concatenate(
        [power_rows, jnp.zeros((2 * LEAF - rows_per, width), jnp.float32)], axis=0
    )
    work_ref[:, width + 2 * channels :] = padded.T
    gram_ref[:, width:] = work_ref[:, width:]

    worst = right_gap
    for k in range(blocks):
        at = slice(k * LEAF, (k + 1) * LEAF)
        inverse, gap = quick_leaf(work_ref[at, at])
        worst = jnp.maximum(worst, gap)
        value = product(wide_left(split(inverse)), wide_right(split(work_ref[at, (k + 1) * LEAF :])))
        y_ref[at, :] = value[:, width - (k + 1) * LEAF :]
        if k == blocks - 1:
            break
        start = (k + 1) * LEAF
        up_ref[:, start:] = wide_right(split(value))
        down_ref[start:, :] = wide_left(split(value[:, : width - start].T))
        edges = list(range(start, width, 2 * LEAF))
        spans = [(a, min(a + 2 * LEAF, width)) for a in edges] + [
            (a, a + 2 * LEAF) for a in range(width, wide, 2 * LEAF)
        ]
        for a, b in spans:
            bottom = min(b, width)
            work_ref[start:bottom, a:b] -= product(down_ref[start:bottom, :], up_ref[:, a:b])

    @pl.when(jnp.logical_not(jnp.max(worst) <= 0.03))
    def _():
        leaf_inverse(right_gram, inv_ref, aux_ref)
        work_ref[...] = gram_ref[...]

        def block_step(k, carry):
            k0 = pl.multiple_of(k * LEAF, LEAF)
            leaf_inverse(work_ref[pl.ds(k0, LEAF), pl.ds(k0, LEAF)], big_ref, aux_ref)
            inverse = wide_left(split(big_ref[...]))
            for a in range(0, wide, LEAF):
                value = product(inverse, wide_right(split(work_ref[pl.ds(k0, LEAF), a : a + LEAF])))
                up_ref[:, a : a + LEAF] = wide_right(split(value))
                if a < width:
                    down_ref[a : a + LEAF, :] = wide_left(split(value.T))
                else:
                    y_ref[pl.ds(k0, LEAF), a - width : a - width + LEAF] = value

            def row_step(i, inner):
                i0 = pl.multiple_of(i * LEAF, LEAF)
                left = down_ref[pl.ds(i0, LEAF), :]
                for a in range(0, wide, LEAF):

                    @pl.when(a + LEAF > i0)
                    def _():
                        work_ref[pl.ds(i0, LEAF), a : a + LEAF] -= product(
                            left, up_ref[:, a : a + LEAF]
                        )

                return inner

            lax.fori_loop(k + 1, blocks, row_step, 0)
            return carry

        lax.fori_loop(0, blocks, block_step, 0)

    right_basis_new = matmul_rows(right_power, inv_ref[...])
    right_basis_out[...] = right_basis_new
    right_turn = matmul(right_basis.T, right_basis_new)
    solved = y_ref[...]
    rotated = matmul(solved[:, :channels], right_turn)
    projected = matmul(solved[:, channels : 2 * channels], right_basis_new)
    basis_new = solved[:, 2 * channels :].T[:rows_per]
    basis_out[...] = basis_new
    momentum = 0.9 * rotated + 0.1 * projected
    second = 0.95 * second_ref[...] + 0.05 * projected * projected
    up = momentum / (jnp.sqrt(second) + epsilon)
    update_rows = matmul(basis_new, up)
    update_out[...] = matmul_rows(update_rows, right_basis_new)
    y_ref[:, :channels] = momentum
    y_ref[:, channels : 2 * channels] = second
    own = pl.ds(pl.multiple_of(d * moment_rows, 8), moment_rows)
    momentum_out[...] = y_ref[own, :channels]
    second_out[...] = y_ref[own, channels : 2 * channels]


def finish(grad, back, mapped, crossed, left_factor, right_factor, right_basis, second, moment_rows):
    vmem = pl.BlockSpec(memory_space=pltpu.VMEM)
    width, channels = grad.shape
    rows_per = left_factor.shape[0]
    wide = width + 2 * channels + 2 * LEAF
    half = jnp.bfloat16
    single = jnp.float32
    square = pltpu.VMEM((LEAF, LEAF), single)
    shapes = [
        left_factor.shape,
        left_factor.shape,
        right_factor.shape,
        right_basis.shape,
        (moment_rows, channels),
        (moment_rows, channels),
        (rows_per, channels),
    ]
    return pl.pallas_call(
        finish_kernel,
        out_shape=tuple(jax.ShapeDtypeStruct(shape, single) for shape in shapes),
        in_specs=[vmem] * 8,
        out_specs=(vmem,) * 7,
        scratch_shapes=[
            pltpu.VMEM((width, width), half),
            pltpu.VMEM((width, width + 6 * channels), half),
            pltpu.VMEM((6 * channels, width), half),
            pltpu.VMEM((width, wide), single),
            pltpu.VMEM((width, wide), single),
            pltpu.VMEM((3 * LEAF, wide), half),
            pltpu.VMEM((width, 3 * LEAF), half),
            pltpu.VMEM((width, wide - width), single),
            square,
            square,
            square,
        ],
        compiler_params=pltpu.CompilerParams(vmem_limit_bytes=56 * 1024 * 1024),
        name="finish",
    )(grad, back, mapped, crossed, left_factor, right_factor, right_basis, second)


SEMS = {
    "edge": 4,
    "rim": 4,
    "basis_z": 3,
    "basis_sib": 4,
    "back_sum": 3,
    "back_z": 3,
    "back_dp": 3,
    "back_sib": 4,
    "second_dp": 3,
    "second_sib": 3,
    "swap": 1,
    "grad_sum": 3,
    "grad_zsum": 3,
    "grad_z": 3,
    "grad_dp": 3,
    "grad_sib": 4,
    "map_z": 3,
    "map_x": 4,
    "map_y": 4,
    "map_far": 8,
    "map_sib": 7,
    "cross_dp": 3,
    "cross_sib": 3,
}
CUT = 80


def exchange_kernel(
    grad_scale,
    meta_ref,
    strips_ref,
    act_ref,
    cot_ref,
    kernel_ref,
    block_ref,
    back_in_ref,
    second_ref,
    factor_ref,
    result_ref,
    input_grad_ref,
    grad_ref,
    back_ref,
    seconds_ref,
    all_ref,
    crossed_ref,
    borders,
    rims,
    incoming,
    basis,
    back_near,
    back_all,
    padded,
    patches,
    spread,
    inner,
    partial,
    near,
    half,
    dp_in,
    pieces,
    z_in,
    grad_all,
    own_map,
    *sems,
):
    count = len(SEMS)
    send = dict(zip(SEMS, sems[:count]))
    receive = dict(zip(SEMS, sems[count:]))
    t = lax.axis_index("tile")
    d = lax.axis_index("dp")
    z, c = t // CORES, t % CORES
    sibling = t + 1 - 2 * c
    x_peer = d + 1 - 2 * (d % 2)
    y_peer = lax.rem(d + 2, DPS)
    far_peer = lax.rem(x_peer + 2, DPS)
    rest = range(1, ZS)
    z_peers = [lax.rem(t + CORES * k, ZS * CORES) for k in range(ZS)]
    z_from = [lax.rem(z + ZS - k, ZS) for k in range(ZS)]
    z_to = [lax.rem(z + k, ZS) for k in range(ZS)]
    d_to = [lax.rem(d + j, DPS) for j in range(DPS)]
    d_from = [lax.rem(d + DPS - j, DPS) for j in range(DPS)]
    side = input_grad_ref.shape[0] // CELL
    channels = grad_ref.shape[1]
    width = grad_ref.shape[0]
    pending = []

    def copy(name, index, source, target, **device):
        made = to_device(source, target, send[name].at[index], receive[name].at[index], **device)
        pending.append(made)
        return made

    def start(copies):
        for made in copies:
            made.start()

    def arrive(copies):
        for made in copies:
            made.wait_recv()

    def z_group(name, source, target):
        return [copy(name, k - 1, source(k), target(k), tile=z_peers[k]) for k in rest]

    def dp_group(name, source, target):
        return [copy(name, j - 1, source(j), target(j), dp=d_to[j]) for j in rest]

    greet()
    edges = Edges(strips_ref, borders, send["edge"], receive["edge"])
    edges.start()
    own_basis = basis.at[z, c]
    basis_z = z_group("basis_z", lambda k: block_ref, lambda k: own_basis)
    basis_sib = [
        copy(
            "basis_sib",
            k,
            block_ref if k == 0 else basis.at[z_from[k], c],
            basis.at[z_from[k], c],
            tile=sibling,
        )
        for k in range(ZS)
    ]
    back_sum = dp_group("back_sum", lambda j: back_in_ref.at[d_to[j]], lambda j: back_near.at[j - 1])
    second_dp = dp_group("second_dp", lambda j: second_ref.at[c], lambda j: seconds_ref.at[d, c])
    start(basis_z)
    start(basis_sib[:1])
    start(back_sum)
    start(second_dp)
    own_basis[...] = block_ref[...]
    seconds_ref[d] = second_ref[...]

    turn = meta_ref[0]
    cot = cot_ref[...]
    padded[...] = jnp.zeros(padded.shape, jnp.float32)
    padded[1 : side + 1, 1 : side + 1, :] = act_ref[...].astype(jnp.float32).reshape(side, side, channels)
    cot_t = jnp.concatenate(
        [cot.astype(jnp.float32), jnp.zeros((LEAF - side * side % LEAF, channels), jnp.float32)], axis=0
    ).T[:, : side * side].astype(jnp.bfloat16)

    def pick(ref, wanted):
        return sum(
            jnp.where(wanted == h, ref[h].astype(jnp.float32), 0.0) for h in range(4)
        )

    edges.wait()
    border = [pick(borders, lax.rem(turn + e, 4)) for e in range(4)]
    padded[0, 1 : side + 1, :] = border[0]
    padded[1 : side + 1, side + 1, :] = border[1]
    padded[side + 1, 1 : side + 1, :] = border[2]
    padded[1 : side + 1, 0, :] = border[3]
    for col in range(3):
        lines = padded[:, col : col + side, :].reshape((side + 2) * side, channels)
        for row in range(3):
            at = (3 * row + col) * channels
            patches[:, at : at + channels] = lines[row * side : row * side + side * side].astype(
                jnp.bfloat16
            )
    turned = product(cot_t, patches[...])
    block = partial.shape[2]
    value = turned.T
    for core in range(CORES):
        for dp in range(DPS):
            at = (core * DPS + dp) * block
            partial[core, dp] = value[at : at + block]
    swap = copy("swap", 0, partial.at[1 - c], near, tile=sibling)
    swap.start()

    arrive(back_sum)
    total = back_in_ref[d]
    for slot in range(DPS - 1):
        total = total + back_near[slot]
    back_all[c, d, z] = total
    mine = back_all.at[c, d, z]
    back_z = z_group("back_z", lambda k: mine, lambda k: mine)
    start(back_z)

    swap.wait_recv()
    half[...] = partial[c] + near[...]
    grad_sum = dp_group("grad_sum", lambda j: half.at[d_to[j]], lambda j: dp_in.at[j - 1])
    start(grad_sum)

    for k in rest:
        basis_z[k - 1].wait_recv()
        basis_sib[k].start()
    arrive(back_z)
    slab = back_all.at[c, d]
    back_dp = dp_group("back_dp", lambda j: slab, lambda j: slab)
    start(back_dp)

    arrive(grad_sum)
    total = half[d]
    for slot in range(DPS - 1):
        total = total + dp_in[slot]
    piece = block // ZS
    for k in range(ZS):
        pieces[k] = total[k * piece : (k + 1) * piece]
    grad_zsum = z_group("grad_zsum", lambda k: pieces.at[z_to[k]], lambda k: z_in.at[k - 1])
    start(grad_zsum)

    arrive(basis_sib)
    columns = basis[...].reshape(width, LANES)
    factor = split(factor_ref[...])
    mapped = (0.95 * (product(factor[0], columns) + product(factor[1], columns))).astype(jnp.bfloat16)
    own_map[...] = mapped
    all_ref[d, z, c] = mapped

    def spot_of(dp, k):
        return all_ref.at[dp, z_from[k], c]

    def own_spot(k):
        return own_map if k == 0 else spot_of(d, k)

    map_z = z_group("map_z", lambda k: own_map, lambda k: spot_of(d, 0))
    map_x = [copy("map_x", k, own_spot(k), spot_of(d, k), dp=x_peer) for k in range(ZS)]
    map_y = [copy("map_y", k, own_spot(k), spot_of(d, k), dp=y_peer) for k in range(ZS)]
    map_sib = [copy("map_sib", k, own_spot(k), spot_of(d, k), tile=sibling) for k in range(ZS)]
    upper, lower = pl.ds(0, CUT), pl.ds(CUT, block_ref.shape[0] - CUT)

    def relay(k):
        up = spot_of(x_peer, k).at[upper]
        down = spot_of(y_peer, k).at[lower]
        return [
            copy("map_far", 2 * k, up, up, dp=y_peer),
            copy("map_far", 2 * k + 1, down, down, dp=x_peer),
        ]

    relays = [relay(k) for k in range(ZS)]

    def relay_arrive(k):
        arrive(relays[k])

    start(map_z)
    start([map_x[0], map_y[0], map_sib[0]])

    arrive(grad_zsum)
    total = pieces[z]
    for slot in range(ZS - 1):
        total = total + z_in[slot]
    grad_all[c, d, z] = total
    own_piece = grad_all.at[c, d, z]
    grad_z = z_group("grad_z", lambda k: own_piece, lambda k: own_piece)
    start(grad_z)

    def slabs(ref, name):
        spots = [ref.at[c, d_from[j]] for j in range(DPS)]
        return [copy(name, j, spots[j], spots[j], tile=sibling) for j in range(DPS)]

    arrive(back_dp)
    back_sib = slabs(back_all, "back_sib")
    start(back_sib)
    second_sib = []
    for j in rest:
        spot = seconds_ref.at[d_from[j], c]
        second_sib.append(copy("second_sib", j - 1, spot, spot, tile=sibling))
    arrive(second_dp)
    start(second_sib)

    arrive(grad_z)
    grad_slab = grad_all.at[c, d]
    grad_dp = dp_group("grad_dp", lambda j: grad_slab, lambda j: grad_slab)
    start(grad_dp)

    for k in rest:
        map_z[k - 1].wait_recv()
        start([map_x[k], map_y[k], map_sib[k]])

    terms = product_rows(cot, kernel_ref[...])
    spread[...] = jnp.zeros(spread.shape, jnp.float32)
    for col in range(3):
        stack = None
        for row in range(3):
            at = (3 * row + col) * channels
            term = terms[:, at : at + channels]
            parts = [term]
            if row:
                parts.insert(0, jnp.zeros((row * side, channels), jnp.float32))
            if row < 2:
                parts.append(jnp.zeros(((2 - row) * side, channels), jnp.float32))
            term = jnp.concatenate(parts, axis=0)
            stack = term if stack is None else stack + term
        spread[:, col : col + side, :] += stack.reshape(side + 2, side, channels)
    cycle = [
        spread[0, 1 : side + 1, :],
        spread[1 : side + 1, side + 1, :],
        spread[side + 1, 1 : side + 1, :],
        spread[1 : side + 1, 0, :],
    ]
    line = lax.broadcasted_iota(jnp.int32, (side, side), 0)
    place = lax.broadcasted_iota(jnp.int32, (side, side), 1)
    straight = jnp.where(line == place, 1.0, 0.0)
    crosswise = jnp.where(line + place == side - 1, 1.0, 0.0)
    turned_rims = []
    for e in range(4):
        order = jnp.where(meta_ref[1 + e] > 0, crosswise, straight).astype(jnp.bfloat16)
        turned_rims.append(product(order, cycle[e].astype(jnp.bfloat16)))
    for h in range(4):
        wanted = lax.rem(h + 4 - turn, 4)
        rims[h] = sum(jnp.where(wanted == e, turned_rims[e], 0.0) for e in range(4)).astype(jnp.bfloat16)
    rim_edges = Edges(rims, incoming, send["rim"], receive["rim"])
    rim_edges.start()

    for k in range(ZS):
        arrive([map_x[k], map_y[k]])
        start(relays[k])
        if k == 0:
            result_ref[...] = product(patches[...], kernel_ref[...]).astype(jnp.bfloat16)

    grad_sib = slabs(grad_all, "grad_sib")
    grad_sib[0].start()
    for j in rest:
        grad_dp[j - 1].wait_recv()
        grad_sib[j].start()
    arrive(grad_sib)
    for core in range(CORES):
        for dp in range(DPS):
            for at_z in range(ZS):
                at = ((core * DPS + dp) * ZS + at_z) * piece
                grad_ref[at : at + piece] = grad_all[core, dp, at_z]
    grad = grad_ref[...] * grad_scale
    grad_ref[...] = grad
    grad_t = grad.T
    high_part, low_part = split(grad_t)
    crossed = product(high_part, columns) + product(low_part, columns)
    halves = channels // CORES
    for core in range(CORES):
        crossed_ref[d, core] = crossed[core * halves : (core + 1) * halves]
    own_cross = crossed_ref.at[d, c]
    cross_dp = dp_group("cross_dp", lambda j: own_cross, lambda j: own_cross)
    start(cross_dp)

    arrive(back_sib)
    for core in range(CORES):
        for dp in range(DPS):
            for at_z in range(ZS):
                to = ((at_z * CORES + core) * DPS + dp) * piece
                back_ref[to : to + piece] = back_all[core, dp, at_z]

    peers = [x_peer, y_peer, far_peer]
    map_far = []
    for j in range(3):
        spot = all_ref.at[peers[j], :, c]
        map_far.append(copy("map_sib", ZS + j, spot, spot, tile=sibling))
    start(map_far[:2])
    for k in range(ZS):
        relay_arrive(k)
    map_far[2].start()

    rim_edges.wait()
    value = [pick(incoming, lax.rem(turn + e, 4)) for e in range(4)]
    inner[...] = spread[1 : side + 1, 1 : side + 1, :]
    inner[0, :, :] += value[0]
    inner[:, side - 1, :] += value[1]
    inner[side - 1, :, :] += value[2]
    inner[:, 0, :] += value[3]
    input_grad_ref[...] = inner[...].reshape(side * side, channels).astype(jnp.bfloat16)

    cross_sib = []
    for j in rest:
        spot = crossed_ref.at[d_from[j], c]
        cross_dp[j - 1].wait_recv()
        made = copy("cross_sib", j - 1, spot, spot, tile=sibling)
        made.start()
        cross_sib.append(made)
    arrive(second_sib)
    arrive(map_sib)
    arrive(map_far)
    arrive(cross_sib)
    for made in pending:
        made.wait_send()


def exchange(meta, strips, acts, cots, kernel, block, back, second, factor, scale):
    vmem = pl.BlockSpec(memory_space=pltpu.VMEM)
    width, channels = kernel.shape
    rows = width // (CORES * DPS)
    side = CELL
    half, single = jnp.bfloat16, jnp.float32
    dma = [pltpu.SemaphoreType.DMA((count,)) for count in SEMS.values()]
    out = jax.ShapeDtypeStruct
    return pl.pallas_call(
        lambda *refs: exchange_kernel(scale, *refs),
        out_shape=(
            out(acts.shape, half),
            out(acts.shape, half),
            out((width, channels), single),
            out((width, channels), single),
            out((DPS,) + second.shape, single),
            out((DPS, ZS, CORES) + block.shape, half),
            out((DPS, CORES, channels // CORES, LANES), single),
        ),
        in_specs=[pl.BlockSpec(memory_space=pltpu.SMEM)] + [vmem] * 8,
        out_specs=(vmem,) * 7,
        scratch_shapes=[
            pltpu.VMEM(strips.shape, half),
            pltpu.VMEM(strips.shape, half),
            pltpu.VMEM(strips.shape, half),
            pltpu.VMEM((ZS, CORES) + block.shape, half),
            pltpu.VMEM((DPS - 1,) + back.shape[1:], single),
            pltpu.VMEM((CORES, DPS, ZS) + back.shape[1:], single),
            pltpu.VMEM((side + 2, 32, channels), single),
            pltpu.VMEM((side * side, width), half),
            pltpu.VMEM((side + 2, 32, channels), single),
            pltpu.VMEM((side, side, channels), single),
            pltpu.VMEM((CORES, DPS, rows, channels), single),
            pltpu.VMEM((DPS, rows, channels), single),
            pltpu.VMEM((DPS, rows, channels), single),
            pltpu.VMEM((DPS - 1, rows, channels), single),
            pltpu.VMEM((ZS, rows // ZS, channels), single),
            pltpu.VMEM((ZS - 1, rows // ZS, channels), single),
            pltpu.VMEM((CORES, DPS, ZS, rows // ZS, channels), single),
            pltpu.VMEM(block.shape, half),
            *dma,
            *dma,
        ],
        compiler_params=pltpu.CompilerParams(
            collective_id=0, has_side_effects=True, vmem_limit_bytes=56 * 1024 * 1024
        ),
        name="exchange",
    )(meta, strips, acts, cots, kernel, block, back, second, factor)


def by_direction(strips, turn):
    return lax.dynamic_slice_in_dim(jnp.concatenate([strips, strips], axis=0), turn, 4, 0)


def body_quick(
    activations,
    cotangent,
    kernel,
    turning,
    orient,
    left_factor,
    left_basis,
    right_factor,
    right_basis,
    momentum,
    second_moment,
):
    tiles, dp_count = ZS * CORES, DPS
    dp_index = lax.axis_index("dp")
    tile_vals = activations[:, 0]
    tile_grads = cotangent[:, 0]
    side = tile_vals.shape[1]
    channels = tile_vals.shape[-1]
    turn = turning[0]
    flipped = orient[0] >= 4
    rows_per, width = left_factor.shape
    part = left_basis.shape[1]
    moment_rows = momentum.shape[0]

    strips = flip_edges(edge_strips(tile_vals), flipped)[:, 0]
    strips = by_direction(strips, (4 - turn) % 4)
    block = lax.dynamic_update_slice(
        jnp.zeros((rows_per, LANES), jnp.bfloat16),
        left_basis.astype(jnp.bfloat16),
        (0, dp_index * (part % LEAF)),
    )
    back = jnp.dot(left_basis, momentum, precision=high)
    cells = dp_count * tiles * side * side
    result, input_grad, grad, back, seconds, mapped, crossed = exchange(
        jnp.concatenate([turning, flipped.astype(jnp.int32)]),
        strips,
        tile_vals.reshape(side * side, channels),
        tile_grads.reshape(side * side, channels),
        kernel,
        block,
        back.reshape(DPS, rows_per // DPS, channels),
        second_moment.reshape(CORES, moment_rows // CORES, channels),
        left_factor,
        1.0 / math.sqrt(cells),
    )
    result = result.reshape(activations.shape)
    input_grad = input_grad.reshape(cotangent.shape)
    all_second = seconds.reshape(width, channels)
    left_new, basis_new, right_new, right_basis_new, momentum_new, second_new, update = finish(
        grad,
        back,
        mapped.reshape(DPS, width, LANES),
        crossed.reshape(DPS, channels, LANES),
        left_factor,
        right_factor,
        right_basis,
        all_second,
        moment_rows,
    )
    return (
        result,
        input_grad,
        grad,
        left_new,
        basis_new,
        right_new,
        right_basis_new,
        momentum_new,
        second_new,
        update,
    )


def body(*args):
    tiles = lax.axis_size("tile")
    dp_count = lax.axis_size("dp")
    left_basis = args[6]
    samples = args[0].shape[0]
    sizes = (tiles, dp_count, samples, args[0].shape[2])
    if sizes == (ZS * CORES, DPS, 1, CELL) and left_basis.shape == (144, 288):
        return body_quick(*args)
    return body_plain(*args)


def solution(mesh):
    placed = (
        P(("group", "dp"), "tile", None, None, None),
        P(("group", "dp"), "tile", None, None, None),
        P("group", None),
        P("tile"),
        P("tile", None),
        P(("group", "tile"), None),
        P(("group", "tile"), "dp"),
        P("group", None),
        P("group", None),
        P(("group", "dp"), None),
        P(("group", "dp"), None),
    )
    return jax.shard_map(
        body,
        mesh=mesh,
        in_specs=placed,
        out_specs=(
            P(("group", "dp"), "tile", None, None, None),
            P(("group", "dp"), "tile", None, None, None),
            P("group", None),
            P(("group", "tile"), None),
            P(("group", "tile"), None),
            P("group", None),
            P("group", None),
            P(("group", "dp"), None),
            P(("group", "dp"), None),
            P(("group", "tile"), None),
        ),
        check_vma=False,
    )
```

```python
import math

import jax
import jax.numpy as jnp
from jax import lax
from jax.experimental import pallas as pl
from jax.experimental.pallas import tpu as pltpu
from jax.sharding import PartitionSpec as P

highest = lax.Precision.HIGHEST
epsilon = 1e-08


def edge_strips(values):
    return jnp.stack(
        [values[..., 0, :, :], values[..., :, -1, :], values[..., -1, :, :], values[..., :, 0, :]],
        axis=0,
    )


def cycle_strips(spread):
    return jnp.stack(
        [spread[:, 0, 1:-1], spread[:, 1:-1, -1], spread[:, -1, 1:-1], spread[:, 1:-1, 0]], axis=0
    )


def assemble(tile_vals, borders):
    middle = jnp.concatenate(
        [borders[3][:, :, None, :], tile_vals, borders[1][:, :, None, :]], axis=2
    )
    top_row = jnp.pad(borders[0], ((0, 0), (1, 1), (0, 0)))[:, None]
    bottom_row = jnp.pad(borders[2], ((0, 0), (1, 1), (0, 0)))[:, None]
    return jnp.concatenate([top_row, middle, bottom_row], axis=1)


def tap_patches(padded, side):
    pieces = [
        padded[:, row_off : row_off + side, col_off : col_off + side, :]
        for row_off in range(3)
        for col_off in range(3)
    ]
    joined = jnp.concatenate(pieces, axis=-1)
    return joined.reshape(-1, joined.shape[-1])


def spread_back(flat_grads, kernel, sample_count, side):
    channels = kernel.shape[1]
    summed = jnp.zeros((sample_count, side + 2, side + 2, channels), jnp.float32)
    for tap_index in range(9):
        row_off, col_off = divmod(tap_index, 3)
        weight_tap = kernel[tap_index * channels : (tap_index + 1) * channels]
        contrib = lax.dot_general(
            flat_grads, weight_tap, (((1,), (1,)), ((), ())), preferred_element_type=jnp.float32
        )
        contrib = contrib.reshape(sample_count, side, side, channels)
        summed = summed + jnp.pad(
            contrib, ((0, 0), (row_off, 2 - row_off), (col_off, 2 - col_off), (0, 0))
        )
    return summed


def absorb_rims(interior, incoming):
    result = interior.at[..., 0, :, :].add(incoming[0])
    result = result.at[..., :, -1, :].add(incoming[1])
    result = result.at[..., -1, :, :].add(incoming[2])
    return result.at[..., :, 0, :].add(incoming[3])


def flip_edges(strips, flipped):
    return jnp.where(flipped[:, None, None, None], strips[:, :, ::-1, :], strips)


def pick_gathered(everything, near_tiles, facing, flipped, usable):
    flat = everything.reshape(everything.shape[0] * 4, -1)
    wanted = jnp.where(usable, near_tiles * 4 + facing, -1)
    selector = (lax.broadcasted_iota(jnp.int32, (4, flat.shape[0]), 1) == wanted[:, None]).astype(
        jnp.bfloat16
    )
    picked = jnp.dot(selector, flat, preferred_element_type=jnp.float32).astype(jnp.bfloat16)
    return flip_edges(picked.reshape((4,) + everything.shape[2:]), flipped)


LEAF = 128
SPAN = 384


def split(value):
    high = value.astype(jnp.bfloat16)
    return high, (value - high.astype(jnp.float32)).astype(jnp.bfloat16)


def split_wide(value):
    high = lax.reduce_precision(value, 8, 7)
    return high.astype(jnp.bfloat16), (value - high).astype(jnp.bfloat16)


def dot3(left, right, dims=(((1,), (0,)), ((), ()))):
    def one(a, b):
        return lax.dot_general(a, b, dims, preferred_element_type=jnp.float32)

    return one(left[0], right[0]) + (one(left[0], right[1]) + one(left[1], right[0]))


by_rows = (((1,), (1,)), ((), ()))


def leaf_inverse(block, m_ref, s_ref):
    row = lax.broadcasted_iota(jnp.int32, (LEAF, LEAF), 0)
    col = lax.broadcasted_iota(jnp.int32, (LEAF, LEAF), 1)
    on_diag = row == col
    unit = jnp.where(on_diag, 1.0, 0.0)
    kept = jnp.where(on_diag, block, 0.0)
    across = lax.rsqrt(jnp.sum(kept, axis=0, keepdims=True))
    down = lax.rsqrt(jnp.sum(kept, axis=1, keepdims=True))
    scaled = block * across * down
    m_ref[...] = jnp.where(on_diag, down, jnp.where(row > col, -scaled * across, 0.0))
    pair = split(block)
    rough = m_ref[...].astype(jnp.bfloat16)
    turned = jnp.dot(rough, pair[0], preferred_element_type=jnp.float32).astype(jnp.bfloat16)
    gap = lax.dot_general(turned, rough, by_rows, preferred_element_type=jnp.float32) - unit
    low = jnp.where(row > col, gap, jnp.where(on_diag, 0.5 * gap, 0.0)).astype(jnp.bfloat16)
    m_ref[...] -= jnp.dot(low, rough, preferred_element_type=jnp.float32)

    def more(carry):
        step, error = carry
        return (step < 12) & (error > 1e-4)

    def refine(carry):
        step, _ = carry
        guess = m_ref[...]
        guess_pair = split(guess)
        turned = dot3(guess_pair, pair)
        gap = dot3(split(turned), guess_pair, by_rows) - unit
        error = jnp.max(jnp.abs(gap))
        low = jnp.where(row > col, gap, jnp.where(on_diag, 0.5 * gap, 0.0))
        m_ref[...] = guess - dot3(split(low), guess_pair)
        return step + 1, error

    _, error = lax.while_loop(more, refine, (jnp.int32(0), jnp.float32(1.0)))

    @pl.when(jnp.logical_not(error <= 1e-4))
    def _():
        s_ref[...] = block
        m_ref[...] = unit

        def eliminate(j, carry):
            work = s_ref[...]
            line = s_ref[pl.ds(j, 1), :]
            lane = lax.broadcasted_iota(jnp.int32, (1, LEAF), 1)
            scale = lax.rsqrt(jnp.sum(jnp.where(lane == j, line, 0.0), axis=1, keepdims=True))
            column = jnp.sum(jnp.where(col == j, work, 0.0), axis=1, keepdims=True)
            side = lax.broadcasted_iota(jnp.int32, (LEAF, 1), 0)
            column = jnp.where(side > j, column * scale, 0.0)
            s_ref[...] = work - column * (line * scale)
            mine = m_ref[pl.ds(j, 1), :] * scale
            m_ref[...] = m_ref[...] - column * mine
            m_ref[pl.ds(j, 1), :] = mine
            return carry

        lax.fori_loop(0, LEAF, eliminate, 0)


def factor_kernel(
    gram_ref, side_ref, small_ref, y_ref, small_out_ref, a_ref, uh, ul, uth, utl, yh, yl, m_ref, s_ref
):
    width = gram_ref.shape[1]
    blocks = width // LEAF
    spans = width // SPAN
    leaf_inverse(small_ref[...], m_ref, s_ref)
    small_out_ref[...] = m_ref[...]
    a_ref[...] = gram_ref[...]
    y_ref[...] = side_ref[...]

    def block_step(k, carry):
        k0 = pl.multiple_of(k * LEAF, LEAF)
        leaf_inverse(a_ref[pl.ds(k0, LEAF), pl.ds(k0, LEAF)], m_ref, s_ref)
        inverse = split(m_ref[...])
        for span in range(spans):
            part = slice(span * SPAN, (span + 1) * SPAN)

            @pl.when((span + 1) * SPAN > k0 + LEAF)
            def _():
                value = dot3(inverse, split(a_ref[pl.ds(k0, LEAF), part]))
                uh[:, part], ul[:, part] = split(value)
                uth[part, :], utl[part, :] = split(value.T)

        value = dot3(inverse, split(y_ref[pl.ds(k0, LEAF), :]))
        y_ref[pl.ds(k0, LEAF), :] = value
        yh[...], yl[...] = split(value)

        def row_step(i, inner):
            i0 = pl.multiple_of(i * LEAF, LEAF)
            left = uth[pl.ds(i0, LEAF), :], utl[pl.ds(i0, LEAF), :]
            for span in range(spans):
                part = slice(span * SPAN, (span + 1) * SPAN)

                @pl.when((span + 1) * SPAN > i0)
                def _():
                    a_ref[pl.ds(i0, LEAF), part] -= dot3(left, (uh[:, part], ul[:, part]))

            y_ref[pl.ds(i0, LEAF), :] -= dot3(left, (yh[...], yl[...]))
            return inner

        lax.fori_loop(k + 1, blocks, row_step, 0)
        return carry

    lax.fori_loop(0, blocks, block_step, 0)


def factor_solve(gram, side, small):
    width, columns = side.shape
    vmem = pl.BlockSpec(memory_space=pltpu.VMEM)
    half = jnp.bfloat16
    return pl.pallas_call(
        factor_kernel,
        out_shape=(
            jax.ShapeDtypeStruct(side.shape, jnp.float32),
            jax.ShapeDtypeStruct(small.shape, jnp.float32),
        ),
        in_specs=[vmem] * 3,
        out_specs=(vmem, vmem),
        scratch_shapes=[
            pltpu.VMEM((width, width), jnp.float32),
            pltpu.VMEM((LEAF, width), half),
            pltpu.VMEM((LEAF, width), half),
            pltpu.VMEM((width, LEAF), half),
            pltpu.VMEM((width, LEAF), half),
            pltpu.VMEM((LEAF, columns), half),
            pltpu.VMEM((LEAF, columns), half),
            pltpu.VMEM((LEAF, LEAF), jnp.float32),
            pltpu.VMEM((LEAF, LEAF), jnp.float32),
        ],
        compiler_params=pltpu.CompilerParams(vmem_limit_bytes=40 * 1024 * 1024),
        name="factor_solve",
    )(gram, side, small)


high = lax.Precision.HIGH
tn = (((0,), (0,)), ((), ()))


def sum_kernel(dp_count, tiles, x_ref, out_ref, near, part, far, *sems):
    dp_index = lax.axis_index("dp")
    tile_index = lax.axis_index("tile")
    dp_peers = [lax.rem(dp_index + step, dp_count) for step in range(1, dp_count)]
    tile_peers = [lax.rem(tile_index + step, tiles) for step in range(1, tiles)]
    barrier = pltpu.get_barrier_semaphore()
    for axis, peers in (("dp", dp_peers), ("tile", tile_peers)):
        for peer in peers:
            pl.semaphore_signal(
                barrier, inc=1, device_id={axis: peer}, device_id_type=pl.DeviceIdType.MESH
            )
    pl.semaphore_wait(barrier, dp_count + tiles - 2)

    def exchange(axis, peers, source, target, send, receive):
        copies = [
            pltpu.make_async_remote_copy(
                src_ref=source(peer),
                dst_ref=target(slot),
                send_sem=send.at[slot],
                recv_sem=receive.at[slot],
                device_id={axis: peer},
                device_id_type=pl.DeviceIdType.MESH,
            )
            for slot, peer in enumerate(peers)
        ]
        for copy in copies:
            copy.start()
        for copy in copies:
            copy.wait()

    exchange("dp", dp_peers, lambda peer: x_ref.at[peer], lambda slot: near.at[slot], *sems[0:2])
    total = x_ref[dp_index]
    for slot in range(dp_count - 1):
        total = total + near[slot]
    part[...] = total
    exchange("tile", tile_peers, lambda peer: part.at[peer], lambda slot: far.at[slot], *sems[2:4])
    total = part[tile_index]
    for slot in range(tiles - 1):
        total = total + far[slot]
    out_ref[dp_index, tile_index] = total
    own = out_ref.at[dp_index, tile_index]
    exchange("tile", tile_peers, lambda peer: own, lambda slot: own, *sems[4:6])
    slab = out_ref.at[dp_index]
    exchange("dp", dp_peers, lambda peer: slab, lambda slot: slab, *sems[6:8])


def sum_everywhere(value):
    tiles = lax.axis_size("tile")
    dp_count = lax.axis_size("dp")
    rows, columns = value.shape
    if tiles < 2 or dp_count < 2 or rows % (tiles * dp_count):
        return lax.psum(value, ("tile", "dp"))
    piece = rows // (tiles * dp_count)
    vmem = pl.BlockSpec(memory_space=pltpu.VMEM)
    wide = (dp_count, tiles, piece, columns)
    counts = [dp_count - 1] * 2 + [tiles - 1] * 4 + [dp_count - 1] * 2
    out = pl.pallas_call(
        lambda *refs: sum_kernel(dp_count, tiles, *refs),
        out_shape=jax.ShapeDtypeStruct(wide, jnp.float32),
        in_specs=[vmem],
        out_specs=vmem,
        scratch_shapes=[
            pltpu.VMEM((dp_count - 1, tiles, piece, columns), jnp.float32),
            pltpu.VMEM((tiles, piece, columns), jnp.float32),
            pltpu.VMEM((tiles - 1, piece, columns), jnp.float32),
            *[pltpu.SemaphoreType.DMA((count,)) for count in counts],
        ],
        compiler_params=pltpu.CompilerParams(collective_id=0, has_side_effects=True),
        name="sum_everywhere",
    )(value.reshape(wide))
    return out.reshape(rows, columns)


def body_plain(
    activations,
    cotangent,
    kernel,
    turning,
    orient,
    left_factor,
    left_basis,
    right_factor,
    right_basis,
    momentum,
    second_moment,
):
    tiles = lax.axis_size("tile")
    dp_count = lax.axis_size("dp")
    tile_index = lax.axis_index("tile")
    dp_index = lax.axis_index("dp")
    tile_vals = activations[:, 0]
    tile_grads = cotangent[:, 0]
    sample_count = tile_vals.shape[0]
    side = tile_vals.shape[1]
    channels = tile_vals.shape[-1]
    own_turn = turning[0]
    facing = orient[0] % 4
    flipped = orient[0] >= 4
    heading = (jnp.arange(4, dtype=jnp.int32) + own_turn) % 4
    row_of = tile_index // 4
    col_of = tile_index % 4
    room = jnp.stack([row_of > 0, col_of < 3, row_of < tiles // 4 - 1, col_of > 0])
    usable = (
        jnp.sum(
            jnp.where(
                heading[:, None] == jnp.arange(4, dtype=jnp.int32)[None, :], room[None, :], False
            ),
            axis=1,
        )
        > 0
    )
    offsets = jnp.array([-4, 1, 4, -1], dtype=jnp.int32)
    near_tiles = tile_index + jnp.sum(
        jnp.where(heading[:, None] == jnp.arange(4, dtype=jnp.int32)[None, :], offsets[None, :], 0),
        axis=1,
    )
    strips = edge_strips(tile_vals)
    flat_grads = tile_grads.reshape(-1, channels)
    spread = spread_back(flat_grads, kernel, sample_count, side)
    rim_cells = cycle_strips(spread).astype(jnp.bfloat16)
    everything = lax.all_gather(
        jnp.concatenate([strips, rim_cells], axis=0)[None], "tile", axis=0, tiled=True
    )
    borders = pick_gathered(everything[:, :4], near_tiles, facing, flipped, usable)
    incoming = pick_gathered(everything[:, 4:], near_tiles, facing, flipped, usable)
    padded = assemble(tile_vals, borders)
    columns = tap_patches(padded, side)
    partial_grad = lax.dot_general(
        columns, flat_grads, (((0,), (0,)), ((), ())), preferred_element_type=jnp.float32
    )
    summed_grad = sum_everywhere(partial_grad)
    result = jnp.dot(columns, kernel, preferred_element_type=jnp.float32).astype(jnp.bfloat16)
    result = result.reshape(activations.shape)
    input_grad = absorb_rims(spread[:, 1:-1, 1:-1], incoming.astype(jnp.float32)).astype(
        jnp.bfloat16
    )
    input_grad = input_grad.reshape(cotangent.shape)
    cells = dp_count * sample_count * tiles * side * side
    grad = summed_grad * (1.0 / math.sqrt(cells))
    rows_per, width = left_factor.shape
    row_start = tile_index * rows_per
    moment_rows = momentum.shape[0]
    moment_start = dp_index * moment_rows
    grad_rows = lax.dynamic_slice_in_dim(grad, row_start, rows_per, 0)
    left_new = 0.95 * left_factor + 0.05 * lax.dot_general(
        grad_rows, grad, (((1,), (1,)), ((), ())), precision=high
    )
    basis_rows = lax.all_gather(left_basis, "dp", axis=1, tiled=True)
    basis = lax.all_gather(basis_rows.astype(jnp.bfloat16), "tile", axis=0, tiled=True)
    moments = lax.all_gather(
        jnp.concatenate([momentum, second_moment], axis=1), "dp", axis=0, tiled=True
    )
    all_momentum, all_second = moments[:, :channels], moments[:, channels:]
    back_rows = jnp.dot(basis_rows, all_momentum, precision=highest)
    own_row = row_start + lax.broadcasted_iota(jnp.int32, left_factor.shape, 0)
    own_col = lax.broadcasted_iota(jnp.int32, left_factor.shape, 1)
    diagonal = jnp.sum(jnp.where(own_row == own_col, left_factor, 0.0), axis=1, keepdims=True)
    rest = jnp.broadcast_to(split_wide(diagonal)[1], (rows_per, LEAF))
    factor = lax.all_gather(
        jnp.concatenate(
            [left_factor.astype(jnp.bfloat16), *split_wide(back_rows), rest], axis=1
        ),
        "tile",
        axis=0,
        tiled=True,
    )
    back = factor[:, width : width + channels].astype(jnp.float32) + factor[
        :, width + channels : width + 2 * channels
    ].astype(jnp.float32)
    rest = factor[:, width + 2 * channels : width + 2 * channels + 1]
    factor = factor[:, :width]
    mapped = 0.95 * (
        jnp.dot(factor, basis, preferred_element_type=jnp.float32)
        + rest.astype(jnp.float32) * basis.astype(jnp.float32)
    )
    mapped_gram = lax.dot_general(mapped, mapped, tn, precision=high)
    mapped_back = lax.dot_general(mapped, back, tn, precision=high)
    crossed = sum(
        lax.dot_general(term, basis, tn, preferred_element_type=jnp.float32) for term in split_wide(grad)
    )
    mapped_grad = lax.dot_general(mapped, grad, tn, precision=high)
    grad_gram = lax.dot_general(grad, grad, tn, precision=high)
    grad_back = lax.dot_general(grad, back, tn, precision=high)
    weight = 0.05 * mapped_grad + 0.00125 * lax.dot_general(crossed, grad_gram, tn, precision=high)
    gram = mapped_gram + lax.dot_general(
        jnp.concatenate([weight.T, crossed], axis=0),
        jnp.concatenate([crossed, weight.T], axis=0),
        tn,
        precision=high,
    )
    power_rows = lax.dynamic_slice_in_dim(mapped, row_start, rows_per, 0) + 0.05 * jnp.dot(
        grad_rows, crossed, precision=high
    )
    power_side = jnp.concatenate([mapped_back, mapped_grad], axis=1) + 0.05 * lax.dot_general(
        crossed, jnp.concatenate([grad_back, grad_gram], axis=1), tn, precision=high
    )
    right_new = 0.95 * right_factor + 0.05 * grad_gram
    right_power = jnp.dot(right_new, right_basis, precision=high)
    right_gram = lax.dot_general(right_power, right_power, tn, precision=high)
    solved, right_inverse = factor_solve(
        gram, jnp.concatenate([power_side, power_rows.T], axis=1), right_gram
    )
    turned_momentum = solved[:, :channels]
    turned_grad = solved[:, channels : 2 * channels]
    basis_new = solved[:, 2 * channels :].T
    right_basis_new = lax.dot_general(
        right_power, right_inverse, (((1,), (1,)), ((), ())), precision=high
    )
    right_turn = lax.dot_general(right_basis, right_basis_new, tn, precision=high)
    rotated = jnp.dot(turned_momentum, right_turn, precision=high)
    projected = jnp.dot(turned_grad, right_basis_new, precision=high)
    momentum_all = 0.9 * rotated + 0.1 * projected
    second_all = 0.95 * all_second + 0.05 * projected * projected
    normalized = momentum_all / (jnp.sqrt(second_all) + epsilon)
    momentum_new = lax.dynamic_slice_in_dim(momentum_all, moment_start, moment_rows, 0)
    second_new = lax.dynamic_slice_in_dim(second_all, moment_start, moment_rows, 0)
    update_rows = jnp.dot(basis_new, normalized, precision=high)
    update = lax.dot_general(
        update_rows, right_basis_new, (((1,), (1,)), ((), ())), precision=high
    )
    return (
        result,
        input_grad,
        grad,
        left_new,
        basis_new,
        right_new,
        right_basis_new,
        momentum_new,
        second_new,
        update,
    )


ZS = 4
CORES = 2
DPS = 4
LANES = 384
CELL = 24


def to_device(source, target, send, receive, **device):
    return pltpu.make_async_remote_copy(
        src_ref=source,
        dst_ref=target,
        send_sem=send,
        recv_sem=receive,
        device_id=device,
        device_id_type=pl.DeviceIdType.MESH,
    )


def greet():
    t = lax.axis_index("tile")
    d = lax.axis_index("dp")
    barrier = pltpu.get_barrier_semaphore()
    tiles = ZS * CORES
    for step in range(1, tiles):
        pl.semaphore_signal(
            barrier,
            inc=1,
            device_id={"tile": lax.rem(t + step, tiles)},
            device_id_type=pl.DeviceIdType.MESH,
        )
    for step in range(1, DPS):
        pl.semaphore_signal(
            barrier,
            inc=1,
            device_id={"dp": lax.rem(d + step, DPS)},
            device_id_type=pl.DeviceIdType.MESH,
        )
    pl.semaphore_wait(barrier, tiles + DPS - 2)


class Edges:
    def __init__(self, source, target, send, receive):
        t = lax.axis_index("tile")
        row, col = t // 4, t % 4
        self.rooms = (row > 0, col < 3, row < 1, col > 0)
        self.target = target
        self.copies = []
        for h, step in enumerate((4, 1, 4, 7)):
            back = (h + 2) % 4
            peer = lax.rem(t + step, ZS * CORES)
            self.copies.append(
                to_device(source.at[h], target.at[back], send.at[h], receive.at[back], tile=peer)
            )

    def start(self):
        for h in range(4):

            @pl.when(self.rooms[h])
            def _():
                self.copies[h].start()

            @pl.when(jnp.logical_not(self.rooms[h]))
            def _():
                self.target[h] = jnp.zeros(self.target.shape[1:], self.target.dtype)

    def wait(self):
        for h in range(4):

            @pl.when(self.rooms[h])
            def _():
                self.copies[h].wait_send()
                self.copies[(h + 2) % 4].wait_recv()


def wide_left(pair, axis=1):
    return jnp.concatenate([pair[0], pair[0], pair[1]], axis=axis)


def wide_right(pair, axis=0):
    return jnp.concatenate([pair[0], pair[1], pair[0]], axis=axis)


plain = (((1,), (0,)), ((), ()))


def product(left, right):
    return lax.dot_general(left, right, plain, preferred_element_type=jnp.float32)


def product_rows(left, right):
    return lax.dot_general(left, right, by_rows, preferred_element_type=jnp.float32)


def matmul(left, right):
    return product(wide_left(split(left)), wide_right(split(right)))


def matmul_rows(left, right):
    return product_rows(wide_left(split(left)), wide_right(split(right), 1))


def quick_leaf(block, cheap=2):
    row = lax.broadcasted_iota(jnp.int32, (LEAF, LEAF), 0)
    col = lax.broadcasted_iota(jnp.int32, (LEAF, LEAF), 1)
    on_diag = row == col
    below = row > col
    unit = jnp.where(on_diag, 1.0, 0.0)
    kept = jnp.where(on_diag, block, 0.0)
    across = lax.rsqrt(jnp.sum(kept, axis=0, keepdims=True))
    down = lax.rsqrt(jnp.sum(kept, axis=1, keepdims=True))

    def lower(gap):
        return jnp.where(below, gap, jnp.where(on_diag, 0.5 * gap, 0.0)).astype(jnp.bfloat16)

    high_part, low_part = split(block)
    guess = jnp.where(on_diag, down, jnp.where(below, -block * (across * across) * down, 0.0))
    for _ in range(cheap):
        rough = guess.astype(jnp.bfloat16)
        turned = product(rough, high_part).astype(jnp.bfloat16)
        gap = product_rows(turned, rough) - unit
        guess = rough.astype(jnp.float32) - product(lower(gap), rough)
    rough = guess.astype(jnp.bfloat16)
    twice = jnp.concatenate([rough, rough], axis=1)
    turned = product(twice, jnp.concatenate([high_part, low_part], axis=0))
    gap = product_rows(jnp.concatenate(split(turned), axis=1), twice) - unit
    return rough.astype(jnp.float32) - product(lower(gap), rough), jnp.abs(gap)


def finish_kernel(
    grad_ref,
    back_ref,
    mapped_ref,
    crossed_ref,
    factor_ref,
    right_factor_ref,
    right_basis_ref,
    second_ref,
    result_ref,
    input_grad_ref,
    result_out,
    input_grad_out,
    grad_out,
    left_out,
    basis_out,
    right_out,
    right_basis_out,
    momentum_out,
    second_out,
    update_out,
    m_ref,
    left_ref,
    right_ref,
    work_ref,
    gram_ref,
    up_ref,
    down_ref,
    y_ref,
    inv_ref,
    aux_ref,
    big_ref,
):
    t = lax.axis_index("tile")
    d = lax.axis_index("dp")
    width, channels = grad_ref.shape
    blocks = width // LEAF
    rows_per = factor_ref.shape[0]
    moment_rows = momentum_out.shape[0]
    wide = work_ref.shape[1]
    own_rows = pl.ds(pl.multiple_of(t * rows_per, 16), rows_per)

    result_out[...] = result_ref[...]
    input_grad_out[...] = input_grad_ref[...]
    extra = LEAF // 4

    lane = lax.broadcasted_iota(jnp.int32, (1, LEAF), 1)

    def tile_of(middle, shared, folded, j):
        group, spot = divmod(j, 2)
        if spot:
            return middle(group)
        if group == 0:
            return shared(0)
        value = jnp.where(lane >= extra * (group - 1), folded(group - 1), shared(group - 1))
        return jnp.where(lane >= extra * group, shared(group), value) if group < DPS else value

    def stack(g, begin, end):
        blocks_of = [mapped_ref[g, tile, begin:end, :] for tile in range(mapped_ref.shape[1])]
        return jnp.concatenate(blocks_of, axis=0).astype(jnp.float32)

    def folded_rows(g):
        return jnp.concatenate(
            [
                unfold(mapped_ref[g, tile, 2 * rows_per :, :].astype(jnp.float32), 3)
                for tile in range(mapped_ref.shape[1])
            ],
            axis=0,
        )

    for j in range(blocks):
        at = slice(j * LEAF, (j + 1) * LEAF)
        value = tile_of(
            lambda g: stack(g, 0, rows_per), lambda g: stack(g, rows_per, 2 * rows_per), folded_rows, j
        ).astype(jnp.bfloat16)
        m_ref[:, at] = value
        left_ref[at, :width] = value.T
    crossed = jnp.concatenate(
        [
            tile_of(
                lambda g: crossed_ref[g, :channels, :],
                lambda g: crossed_ref[g, channels : 2 * channels, :],
                lambda g: unfold(crossed_ref[g, 2 * channels :, :], 4),
                j,
            )
            for j in range(blocks)
        ],
        axis=1,
    )
    grad = grad_ref[...]
    grad_out[...] = grad
    grad_t = grad.T
    both = jnp.concatenate([back_ref[...], grad], axis=1)
    both_pair = split(both)
    grad_both = product(wide_left(split(grad_t)), wide_right(both_pair))
    grad_gram = grad_both[:, channels:]
    grad_rows = grad_ref[own_rows, :]
    left_out[...] = 0.95 * factor_ref[...] + 0.05 * matmul_rows(grad_rows, grad)

    right_new = 0.95 * right_factor_ref[...] + 0.05 * grad_gram
    right_out[...] = right_new
    right_basis = right_basis_ref[...]
    right_power = matmul(right_new, right_basis)
    right_gram = matmul(right_power.T, right_power)
    right_inverse, right_gap = quick_leaf(right_gram, 4)
    inv_ref[...] = right_inverse

    grad_m = product(jnp.concatenate(split(grad_t), axis=0), m_ref[...])
    weight = 0.05 * (grad_m[:channels] + grad_m[channels:]) + 0.00125 * matmul(grad_gram, crossed)
    pair = jnp.concatenate([weight, crossed], axis=0)
    pair_t = pair.T
    left_ref[:, width:] = wide_left(split(pair_t))
    right_ref[...] = wide_right(split(jnp.concatenate([crossed, weight], axis=0)))
    for j in range(0, blocks, 2):
        end = min(j + 2, blocks) * LEAF
        at = slice(j * LEAF, end)
        value = product(left_ref[:end, :width], m_ref[:, at]) + product(
            left_ref[:end, width:], right_ref[:, at]
        )
        work_ref[:end, at] = value
        gram_ref[:end, at] = value
    m_both = product(left_ref[:, :width], both_pair[0]) + product(left_ref[:, :width], both_pair[1])
    crossed_t = pair_t[:, channels:]
    work_ref[:, width : width + 2 * channels] = m_both + 0.05 * matmul(crossed_t, grad_both)
    power_rows = m_ref[own_rows, :].astype(jnp.float32) + 0.05 * matmul(grad_rows, crossed)
    padded = jnp.concatenate(
        [power_rows, jnp.zeros((2 * LEAF - rows_per, width), jnp.float32)], axis=0
    )
    work_ref[:, width + 2 * channels :] = padded.T
    gram_ref[:, width:] = work_ref[:, width:]

    worst = right_gap
    for k in range(blocks):
        at = slice(k * LEAF, (k + 1) * LEAF)
        inverse, gap = quick_leaf(work_ref[at, at])
        worst = jnp.maximum(worst, gap)
        value = product(wide_left(split(inverse)), wide_right(split(work_ref[at, (k + 1) * LEAF :])))
        y_ref[at, :] = value[:, width - (k + 1) * LEAF :]
        if k == blocks - 1:
            break
        start = (k + 1) * LEAF
        up_ref[:, start:] = wide_right(split(value))
        down_ref[start:, :] = wide_left(split(value[:, : width - start].T))
        edges = list(range(start, width, 2 * LEAF))
        spans = [(a, min(a + 2 * LEAF, width)) for a in edges] + [
            (a, a + 2 * LEAF) for a in range(width, wide, 2 * LEAF)
        ]
        for a, b in spans:
            bottom = min(b, width)
            work_ref[start:bottom, a:b] -= product(down_ref[start:bottom, :], up_ref[:, a:b])

    @pl.when(jnp.logical_not(jnp.max(worst) <= 0.03))
    def _():
        leaf_inverse(right_gram, inv_ref, aux_ref)
        work_ref[...] = gram_ref[...]

        def block_step(k, carry):
            k0 = pl.multiple_of(k * LEAF, LEAF)
            leaf_inverse(work_ref[pl.ds(k0, LEAF), pl.ds(k0, LEAF)], big_ref, aux_ref)
            inverse = wide_left(split(big_ref[...]))
            for a in range(0, wide, LEAF):
                value = product(inverse, wide_right(split(work_ref[pl.ds(k0, LEAF), a : a + LEAF])))
                up_ref[:, a : a + LEAF] = wide_right(split(value))
                if a < width:
                    down_ref[a : a + LEAF, :] = wide_left(split(value.T))
                else:
                    y_ref[pl.ds(k0, LEAF), a - width : a - width + LEAF] = value

            def row_step(i, inner):
                i0 = pl.multiple_of(i * LEAF, LEAF)
                left = down_ref[pl.ds(i0, LEAF), :]
                for a in range(0, wide, LEAF):

                    @pl.when(a + LEAF > i0)
                    def _():
                        work_ref[pl.ds(i0, LEAF), a : a + LEAF] -= product(
                            left, up_ref[:, a : a + LEAF]
                        )

                return inner

            lax.fori_loop(k + 1, blocks, row_step, 0)
            return carry

        lax.fori_loop(0, blocks, block_step, 0)

    right_basis_new = matmul_rows(right_power, inv_ref[...])
    right_basis_out[...] = right_basis_new
    right_turn = matmul(right_basis.T, right_basis_new)
    solved = y_ref[...]
    rotated = matmul(solved[:, :channels], right_turn)
    projected = matmul(solved[:, channels : 2 * channels], right_basis_new)
    basis_new = solved[:, 2 * channels :].T[:rows_per]
    basis_out[...] = basis_new
    momentum = 0.9 * rotated + 0.1 * projected
    second = 0.95 * second_ref[...] + 0.05 * projected * projected
    up = momentum / (jnp.sqrt(second) + epsilon)
    update_rows = matmul(basis_new, up)
    update_out[...] = matmul_rows(update_rows, right_basis_new)
    y_ref[:, :channels] = momentum
    y_ref[:, channels : 2 * channels] = second
    own = pl.ds(pl.multiple_of(d * moment_rows, 8), moment_rows)
    momentum_out[...] = y_ref[own, :channels]
    second_out[...] = y_ref[own, channels : 2 * channels]


def finish(
    grad, back, mapped, crossed, left_factor, right_factor, right_basis, second, result, input_grad, moment_rows
):
    vmem = pl.BlockSpec(memory_space=pltpu.VMEM)
    width, channels = grad.shape
    rows_per = left_factor.shape[0]
    wide = width + 2 * channels + 2 * LEAF
    half = jnp.bfloat16
    single = jnp.float32
    square = pltpu.VMEM((LEAF, LEAF), single)
    shapes = [
        left_factor.shape,
        left_factor.shape,
        right_factor.shape,
        right_basis.shape,
        (moment_rows, channels),
        (moment_rows, channels),
        (rows_per, channels),
    ]
    return pl.pallas_call(
        finish_kernel,
        out_shape=(
            jax.ShapeDtypeStruct(result.shape, half),
            jax.ShapeDtypeStruct(input_grad.shape, half),
            jax.ShapeDtypeStruct(grad.shape, single),
            *(jax.ShapeDtypeStruct(shape, single) for shape in shapes),
        ),
        in_specs=[vmem] * 10,
        out_specs=(vmem,) * 10,
        scratch_shapes=[
            pltpu.VMEM((width, width), half),
            pltpu.VMEM((width, width + 6 * channels), half),
            pltpu.VMEM((6 * channels, width), half),
            pltpu.VMEM((width, wide), single),
            pltpu.VMEM((width, wide), single),
            pltpu.VMEM((3 * LEAF, wide), half),
            pltpu.VMEM((width, 3 * LEAF), half),
            pltpu.VMEM((width, wide - width), single),
            square,
            square,
            square,
        ],
        compiler_params=pltpu.CompilerParams(vmem_limit_bytes=56 * 1024 * 1024),
        name="finish",
    )(
        grad, back, mapped, crossed, left_factor, right_factor, right_basis, second, result, input_grad
    )


def fold(value, parts):
    step = LEAF // 4
    rows = value.shape[0] // parts
    total = value[:rows]
    for i in range(1, parts):
        total = total + pltpu.roll(value[i * rows : (i + 1) * rows], step * i, 1)
    return total


def unfold(value, parts):
    step = LEAF // 4
    return jnp.concatenate(
        [value] + [pltpu.roll(value, LEAF - step * i, 1) for i in range(1, parts)], axis=0
    )


SEMS = {
    "edge": 4,
    "rim": 4,
    "basis_z": 3,
    "basis_sib": 4,
    "back_sum": 3,
    "back_z": 3,
    "back_dp": 3,
    "back_sib": 4,
    "second_dp": 3,
    "second_sib": 3,
    "swap": 1,
    "grad_sum": 3,
    "grad_zsum": 3,
    "grad_z": 3,
    "grad_dp": 3,
    "grad_sib": 4,
    "map_z": 3,
    "map_x": 4,
    "map_y": 4,
    "map_far": 8,
    "map_sib": 7,
    "cross_dp": 3,
    "cross_sib": 3,
}
CUT = 176


def exchange_kernel(
    grad_scale,
    meta_ref,
    act_ref,
    cot_ref,
    kernel_ref,
    basis_in_ref,
    momentum_ref,
    second_ref,
    factor_ref,
    result_ref,
    input_grad_ref,
    grad_ref,
    back_ref,
    seconds_ref,
    all_ref,
    crossed_ref,
    strips,
    borders,
    rims,
    incoming,
    block_ref,
    basis,
    columns_ref,
    back_in_ref,
    back_near,
    back_all,
    padded,
    patches,
    spread,
    inner,
    partial,
    near,
    half,
    dp_in,
    pieces,
    z_in,
    grad_all,
    own_map,
    *sems,
):
    count = len(SEMS)
    send = dict(zip(SEMS, sems[:count]))
    receive = dict(zip(SEMS, sems[count:]))
    t = lax.axis_index("tile")
    d = lax.axis_index("dp")
    z, c = t // CORES, t % CORES
    sibling = t + 1 - 2 * c
    x_peer = d + 1 - 2 * (d % 2)
    y_peer = lax.rem(d + 2, DPS)
    far_peer = lax.rem(x_peer + 2, DPS)
    rest = range(1, ZS)
    z_peers = [lax.rem(t + CORES * k, ZS * CORES) for k in range(ZS)]
    z_from = [lax.rem(z + ZS - k, ZS) for k in range(ZS)]
    z_to = [lax.rem(z + k, ZS) for k in range(ZS)]
    d_to = [lax.rem(d + j, DPS) for j in range(DPS)]
    d_from = [lax.rem(d + DPS - j, DPS) for j in range(DPS)]
    side = input_grad_ref.shape[0] // CELL
    channels = grad_ref.shape[1]
    width = grad_ref.shape[0]
    pending = []

    def copy(name, index, source, target, **device):
        made = to_device(source, target, send[name].at[index], receive[name].at[index], **device)
        pending.append(made)
        return made

    def start(copies):
        for made in copies:
            made.start()

    def arrive(copies):
        for made in copies:
            made.wait_recv()

    def z_group(name, source, target):
        return [copy(name, k - 1, source(k), target(k), tile=z_peers[k]) for k in rest]

    def dp_group(name, source, target):
        return [copy(name, j - 1, source(j), target(j), dp=d_to[j]) for j in rest]

    turn = meta_ref[0]
    padded[...] = jnp.zeros(padded.shape, jnp.float32)
    padded[1 : side + 1, 1 : side + 1, :] = act_ref[...].astype(jnp.float32).reshape(side, side, channels)
    line = lax.broadcasted_iota(jnp.int32, (side, side), 0)
    place = lax.broadcasted_iota(jnp.int32, (side, side), 1)
    straight = jnp.where(line == place, 1.0, 0.0)
    crosswise = jnp.where(line + place == side - 1, 1.0, 0.0)
    orders = [
        jnp.where(meta_ref[1 + e] > 0, crosswise, straight).astype(jnp.bfloat16) for e in range(4)
    ]

    def fill(target, lines):
        aligned = [product(orders[e], lines[e].astype(jnp.bfloat16)) for e in range(4)]
        for h in range(4):
            wanted = lax.rem(h + 4 - turn, 4)
            target[h] = sum(jnp.where(wanted == e, aligned[e], 0.0) for e in range(4)).astype(
                jnp.bfloat16
            )

    fill(
        strips,
        [
            padded[1, 1 : side + 1, :],
            padded[1 : side + 1, side, :],
            padded[side, 1 : side + 1, :],
            padded[1 : side + 1, 1, :],
        ],
    )
    part = basis_in_ref.shape[1]
    rows_per = basis_in_ref.shape[0]
    extra = part % LEAF
    old_basis = basis_in_ref[...]
    shifted = jnp.zeros((rows_per, LANES), jnp.float32)
    for slot in range(DPS):
        pieces_of = [old_basis, jnp.zeros((rows_per, LANES - part - extra * slot), jnp.float32)]
        if slot:
            pieces_of.insert(0, jnp.zeros((rows_per, extra * slot), jnp.float32))
        pieces_of = [p for p in pieces_of if p.shape[1]]
        shifted = jnp.where(d == slot, jnp.concatenate(pieces_of, axis=1), shifted)
    lane = lax.broadcasted_iota(jnp.int32, (1, LEAF), 1)
    window = (lane >= extra * d) & (lane < extra * (d + 1))
    first_tile, last_tile = shifted[:, :LEAF], shifted[:, 2 * LEAF :]
    block_ref[...] = jnp.concatenate(
        [
            shifted[:, LEAF : 2 * LEAF],
            jnp.where(lane >= extra * d, first_tile, last_tile),
            fold(jnp.where(window, last_tile, 0.0), 3),
        ],
        axis=0,
    ).astype(jnp.bfloat16)
    greet()
    edges = Edges(strips, borders, send["edge"], receive["edge"])
    edges.start()
    own_basis = basis.at[z, c]
    basis_z = z_group("basis_z", lambda k: block_ref, lambda k: own_basis)
    basis_sib = [
        copy(
            "basis_sib",
            k,
            block_ref if k == 0 else basis.at[z_from[k], c],
            basis.at[z_from[k], c],
            tile=sibling,
        )
        for k in range(ZS)
    ]
    back_sum = dp_group("back_sum", lambda j: back_in_ref.at[d_to[j]], lambda j: back_near.at[j - 1])
    second_dp = dp_group("second_dp", lambda j: second_ref.at[c], lambda j: seconds_ref.at[d, c])
    start(basis_z)
    start(basis_sib[:1])
    old_pair, moment_pair = split(old_basis), split(momentum_ref[...])
    value = product(old_pair[0], moment_pair[0]) + (
        product(old_pair[0], moment_pair[1]) + product(old_pair[1], moment_pair[0])
    )
    piece = rows_per // DPS
    for dp in range(DPS):
        back_in_ref[dp] = value[dp * piece : (dp + 1) * piece]
    start(back_sum)
    start(second_dp)
    own_basis[...] = block_ref[...]
    seconds_ref[d] = second_ref[...]

    cot = cot_ref[...]
    cot_t = jnp.concatenate(
        [cot.astype(jnp.float32), jnp.zeros((LEAF - side * side % LEAF, channels), jnp.float32)], axis=0
    ).T[:, : side * side].astype(jnp.bfloat16)

    def pick(ref, wanted):
        return sum(
            jnp.where(wanted == h, ref[h].astype(jnp.float32), 0.0) for h in range(4)
        )

    edges.wait()
    border = [pick(borders, lax.rem(turn + e, 4)) for e in range(4)]
    padded[0, 1 : side + 1, :] = border[0]
    padded[1 : side + 1, side + 1, :] = border[1]
    padded[side + 1, 1 : side + 1, :] = border[2]
    padded[1 : side + 1, 0, :] = border[3]
    for col in range(3):
        lines = padded[:, col : col + side, :].reshape((side + 2) * side, channels)
        for row in range(3):
            at = (3 * row + col) * channels
            patches[:, at : at + channels] = lines[row * side : row * side + side * side].astype(
                jnp.bfloat16
            )
    turned = product(cot_t, patches[...])
    block = partial.shape[2]
    value = turned.T
    for core in range(CORES):
        for dp in range(DPS):
            at = (core * DPS + dp) * block
            partial[core, dp] = value[at : at + block]
    swap = copy("swap", 0, partial.at[1 - c], near, tile=sibling)
    swap.start()

    arrive(back_sum)
    total = back_in_ref[d]
    for slot in range(DPS - 1):
        total = total + back_near[slot]
    back_all[c, d, z] = total
    mine = back_all.at[c, d, z]
    back_z = z_group("back_z", lambda k: mine, lambda k: mine)
    start(back_z)

    swap.wait_recv()
    half[...] = partial[c] + near[...]
    grad_sum = dp_group("grad_sum", lambda j: half.at[d_to[j]], lambda j: dp_in.at[j - 1])
    start(grad_sum)

    for k in rest:
        basis_z[k - 1].wait_recv()
        basis_sib[k].start()
    arrive(back_z)
    slab = back_all.at[c, d]
    back_dp = dp_group("back_dp", lambda j: slab, lambda j: slab)
    start(back_dp)

    arrive(basis_sib)
    for at_z in range(ZS):
        for core in range(CORES):
            at = (at_z * CORES + core) * rows_per
            at = slice(at, at + rows_per)
            columns_ref[at, :LEAF] = basis[at_z, core, :rows_per]
            columns_ref[at, LEAF : 2 * LEAF] = basis[at_z, core, rows_per : 2 * rows_per]
            columns_ref[at, 2 * LEAF :] = unfold(
                basis[at_z, core, 2 * rows_per :].astype(jnp.float32), 3
            ).astype(jnp.bfloat16)
    columns = columns_ref[...]
    factor = split(factor_ref[...])
    mapped = 0.95 * (product(factor[0], columns) + product(factor[1], columns))
    mapped = jnp.concatenate(
        [
            mapped[:, :LEAF],
            mapped[:, LEAF : 2 * LEAF],
            fold(jnp.where(window, mapped[:, 2 * LEAF :], 0.0), 3),
        ],
        axis=0,
    ).astype(jnp.bfloat16)
    own_map[...] = mapped
    all_ref[d, z, c] = mapped

    def spot_of(dp, k):
        return all_ref.at[dp, z_from[k], c]

    def own_spot(k):
        return own_map if k == 0 else spot_of(d, k)

    map_z = z_group("map_z", lambda k: own_map, lambda k: spot_of(d, 0))
    map_x = [copy("map_x", k, own_spot(k), spot_of(d, k), dp=x_peer) for k in range(ZS)]
    map_y = [copy("map_y", k, own_spot(k), spot_of(d, k), dp=y_peer) for k in range(ZS)]
    map_sib = [copy("map_sib", k, own_spot(k), spot_of(d, k), tile=sibling) for k in range(ZS)]
    upper, lower = pl.ds(0, CUT), pl.ds(CUT, own_map.shape[0] - CUT)

    def relay(k):
        up = spot_of(x_peer, k).at[upper]
        down = spot_of(y_peer, k).at[lower]
        return [
            copy("map_far", 2 * k, up, up, dp=y_peer),
            copy("map_far", 2 * k + 1, down, down, dp=x_peer),
        ]

    relays = [relay(k) for k in range(ZS)]

    def relay_arrive(k):
        arrive(relays[k])

    start(map_z)
    start([map_x[0], map_y[0], map_sib[0]])

    arrive(grad_sum)
    total = half[d]
    for slot in range(DPS - 1):
        total = total + dp_in[slot]
    for k in range(ZS):
        pieces[k] = total[k * piece : (k + 1) * piece]
    grad_zsum = z_group("grad_zsum", lambda k: pieces.at[z_to[k]], lambda k: z_in.at[k - 1])
    start(grad_zsum)

    arrive(grad_zsum)
    total = pieces[z]
    for slot in range(ZS - 1):
        total = total + z_in[slot]
    grad_all[c, d, z] = total
    own_piece = grad_all.at[c, d, z]
    grad_z = z_group("grad_z", lambda k: own_piece, lambda k: own_piece)
    start(grad_z)

    def slabs(ref, name):
        spots = [ref.at[c, d_from[j]] for j in range(DPS)]
        return [copy(name, j, spots[j], spots[j], tile=sibling) for j in range(DPS)]

    arrive(back_dp)
    back_sib = slabs(back_all, "back_sib")
    start(back_sib)
    second_sib = []
    for j in rest:
        spot = seconds_ref.at[d_from[j], c]
        second_sib.append(copy("second_sib", j - 1, spot, spot, tile=sibling))
    arrive(second_dp)
    start(second_sib)

    arrive(grad_z)
    grad_slab = grad_all.at[c, d]
    grad_dp = dp_group("grad_dp", lambda j: grad_slab, lambda j: grad_slab)
    start(grad_dp)

    for k in rest:
        map_z[k - 1].wait_recv()
        start([map_x[k], map_y[k], map_sib[k]])

    terms = product_rows(cot, kernel_ref[...])
    spread[...] = jnp.zeros(spread.shape, jnp.float32)
    for col in range(3):
        stack = None
        for row in range(3):
            at = (3 * row + col) * channels
            term = terms[:, at : at + channels]
            parts = [term]
            if row:
                parts.insert(0, jnp.zeros((row * side, channels), jnp.float32))
            if row < 2:
                parts.append(jnp.zeros(((2 - row) * side, channels), jnp.float32))
            term = jnp.concatenate(parts, axis=0)
            stack = term if stack is None else stack + term
        spread[:, col : col + side, :] += stack.reshape(side + 2, side, channels)
    fill(
        rims,
        [
            spread[0, 1 : side + 1, :],
            spread[1 : side + 1, side + 1, :],
            spread[side + 1, 1 : side + 1, :],
            spread[1 : side + 1, 0, :],
        ],
    )
    rim_edges = Edges(rims, incoming, send["rim"], receive["rim"])
    rim_edges.start()

    def pass_on(k):
        arrive([map_x[k], map_y[k]])
        start(relays[k])

    pass_on(0)
    result_ref[...] = product(patches[...], kernel_ref[...]).astype(jnp.bfloat16)
    pass_on(1)

    grad_sib = slabs(grad_all, "grad_sib")
    grad_sib[0].start()
    for j in rest:
        grad_dp[j - 1].wait_recv()
        grad_sib[j].start()
    arrive(grad_sib)
    for core in range(CORES):
        for dp in range(DPS):
            for at_z in range(ZS):
                at = ((core * DPS + dp) * ZS + at_z) * piece
                grad_ref[at : at + piece] = grad_all[core, dp, at_z]
    grad = grad_ref[...] * grad_scale
    grad_ref[...] = grad
    grad_t = grad.T
    high_part, low_part = split(grad_t)
    crossed = product(high_part, columns) + product(low_part, columns)
    crossed = jnp.concatenate(
        [
            crossed[:, :LEAF],
            crossed[:, LEAF : 2 * LEAF],
            fold(jnp.where(window, crossed[:, 2 * LEAF :], 0.0), 4),
        ],
        axis=0,
    )
    halves = crossed.shape[0] // CORES
    for core in range(CORES):
        crossed_ref[d, core] = crossed[core * halves : (core + 1) * halves]
    own_cross = crossed_ref.at[d, c]
    cross_dp = dp_group("cross_dp", lambda j: own_cross, lambda j: own_cross)
    start(cross_dp)

    pass_on(2)
    pass_on(3)
    arrive(back_sib)
    for core in range(CORES):
        for dp in range(DPS):
            for at_z in range(ZS):
                to = ((at_z * CORES + core) * DPS + dp) * piece
                back_ref[to : to + piece] = back_all[core, dp, at_z]

    peers = [x_peer, y_peer, far_peer]
    map_far = []
    for j in range(3):
        spot = all_ref.at[peers[j], :, c]
        map_far.append(copy("map_sib", ZS + j, spot, spot, tile=sibling))
    start(map_far[:2])
    for k in range(ZS):
        relay_arrive(k)
    map_far[2].start()

    rim_edges.wait()
    value = [pick(incoming, lax.rem(turn + e, 4)) for e in range(4)]
    inner[...] = spread[1 : side + 1, 1 : side + 1, :]
    inner[0, :, :] += value[0]
    inner[:, side - 1, :] += value[1]
    inner[side - 1, :, :] += value[2]
    inner[:, 0, :] += value[3]
    input_grad_ref[...] = inner[...].reshape(side * side, channels).astype(jnp.bfloat16)

    cross_sib = []
    for j in rest:
        spot = crossed_ref.at[d_from[j], c]
        cross_dp[j - 1].wait_recv()
        made = copy("cross_sib", j - 1, spot, spot, tile=sibling)
        made.start()
        cross_sib.append(made)
    arrive(second_sib)
    arrive(map_sib)
    arrive(map_far)
    arrive(cross_sib)
    for made in pending:
        made.wait_send()


def exchange(meta, acts, cots, kernel, old_basis, momentum, second, factor, scale):
    vmem = pl.BlockSpec(memory_space=pltpu.VMEM)
    width, channels = kernel.shape
    rows = width // (CORES * DPS)
    side = CELL
    half, single = jnp.bfloat16, jnp.float32
    dma = [pltpu.SemaphoreType.DMA((count,)) for count in SEMS.values()]
    out = jax.ShapeDtypeStruct
    strip = pltpu.VMEM((4, side, channels), half)
    block = (2 * rows + rows // 3, LEAF)
    piece = (rows // DPS, channels)
    return pl.pallas_call(
        lambda *refs: exchange_kernel(scale, *refs),
        out_shape=(
            out(acts.shape, half),
            out(acts.shape, half),
            out((width, channels), single),
            out((width, channels), single),
            out((DPS,) + second.shape, single),
            out((DPS, ZS, CORES) + block, half),
            out((DPS, CORES, (2 * channels + channels // 4) // CORES, LEAF), single),
        ),
        in_specs=[pl.BlockSpec(memory_space=pltpu.SMEM)] + [vmem] * 7,
        out_specs=(vmem,) * 7,
        scratch_shapes=[
            strip,
            strip,
            strip,
            strip,
            pltpu.VMEM(block, half),
            pltpu.VMEM((ZS, CORES) + block, half),
            pltpu.VMEM((width, LANES), half),
            pltpu.VMEM((DPS,) + piece, single),
            pltpu.VMEM((DPS - 1,) + piece, single),
            pltpu.VMEM((CORES, DPS, ZS) + piece, single),
            pltpu.VMEM((side + 2, 32, channels), single),
            pltpu.VMEM((side * side, width), half),
            pltpu.VMEM((side + 2, 32, channels), single),
            pltpu.VMEM((side, side, channels), single),
            pltpu.VMEM((CORES, DPS, rows, channels), single),
            pltpu.VMEM((DPS, rows, channels), single),
            pltpu.VMEM((DPS, rows, channels), single),
            pltpu.VMEM((DPS - 1, rows, channels), single),
            pltpu.VMEM((ZS, rows // ZS, channels), single),
            pltpu.VMEM((ZS - 1, rows // ZS, channels), single),
            pltpu.VMEM((CORES, DPS, ZS, rows // ZS, channels), single),
            pltpu.VMEM(block, half),
            *dma,
            *dma,
        ],
        compiler_params=pltpu.CompilerParams(
            collective_id=0, has_side_effects=True, vmem_limit_bytes=56 * 1024 * 1024
        ),
        name="exchange",
    )(meta, acts, cots, kernel, old_basis, momentum, second, factor)


def body_quick(
    activations,
    cotangent,
    kernel,
    turning,
    orient,
    left_factor,
    left_basis,
    right_factor,
    right_basis,
    momentum,
    second_moment,
):
    tiles, dp_count = ZS * CORES, DPS
    tile_vals = activations[:, 0]
    tile_grads = cotangent[:, 0]
    side = tile_vals.shape[1]
    channels = tile_vals.shape[-1]
    flipped = orient[0] >= 4
    width = left_factor.shape[1]
    moment_rows = momentum.shape[0]

    cells = dp_count * tiles * side * side
    result, input_grad, grad, back, seconds, mapped, crossed = exchange(
        jnp.concatenate([turning, flipped.astype(jnp.int32)]),
        tile_vals.reshape(side * side, channels),
        tile_grads.reshape(side * side, channels),
        kernel,
        left_basis,
        momentum,
        second_moment.reshape(CORES, moment_rows // CORES, channels),
        left_factor,
        1.0 / math.sqrt(cells),
    )
    all_second = seconds.reshape(width, channels)
    outs = finish(
        grad,
        back,
        mapped.reshape((DPS, tiles) + mapped.shape[3:]),
        crossed.reshape(DPS, -1, LEAF),
        left_factor,
        right_factor,
        right_basis,
        all_second,
        result,
        input_grad,
        moment_rows,
    )
    return (outs[0].reshape(activations.shape), outs[1].reshape(cotangent.shape), *outs[2:])


def body(*args):
    tiles = lax.axis_size("tile")
    dp_count = lax.axis_size("dp")
    left_basis = args[6]
    samples = args[0].shape[0]
    sizes = (tiles, dp_count, samples, args[0].shape[2])
    if sizes == (ZS * CORES, DPS, 1, CELL) and left_basis.shape == (144, 288):
        return body_quick(*args)
    return body_plain(*args)


def solution(mesh):
    placed = (
        P(("group", "dp"), "tile", None, None, None),
        P(("group", "dp"), "tile", None, None, None),
        P("group", None),
        P("tile"),
        P("tile", None),
        P(("group", "tile"), None),
        P(("group", "tile"), "dp"),
        P("group", None),
        P("group", None),
        P(("group", "dp"), None),
        P(("group", "dp"), None),
    )
    return jax.shard_map(
        body,
        mesh=mesh,
        in_specs=placed,
        out_specs=(
            P(("group", "dp"), "tile", None, None, None),
            P(("group", "dp"), "tile", None, None, None),
            P("group", None),
            P(("group", "tile"), None),
            P(("group", "tile"), None),
            P("group", None),
            P("group", None),
            P(("group", "dp"), None),
            P(("group", "dp"), None),
            P(("group", "tile"), None),
        ),
        check_vma=False,
    )
```

```python
import math

import jax
import jax.numpy as jnp
from jax import lax
from jax.experimental import pallas as pl
from jax.experimental.pallas import tpu as pltpu
from jax.sharding import PartitionSpec as P

highest = lax.Precision.HIGHEST
epsilon = 1e-08


def edge_strips(values):
    return jnp.stack(
        [values[..., 0, :, :], values[..., :, -1, :], values[..., -1, :, :], values[..., :, 0, :]],
        axis=0,
    )


def cycle_strips(spread):
    return jnp.stack(
        [spread[:, 0, 1:-1], spread[:, 1:-1, -1], spread[:, -1, 1:-1], spread[:, 1:-1, 0]], axis=0
    )


def assemble(tile_vals, borders):
    middle = jnp.concatenate(
        [borders[3][:, :, None, :], tile_vals, borders[1][:, :, None, :]], axis=2
    )
    top_row = jnp.pad(borders[0], ((0, 0), (1, 1), (0, 0)))[:, None]
    bottom_row = jnp.pad(borders[2], ((0, 0), (1, 1), (0, 0)))[:, None]
    return jnp.concatenate([top_row, middle, bottom_row], axis=1)


def tap_patches(padded, side):
    pieces = [
        padded[:, row_off : row_off + side, col_off : col_off + side, :]
        for row_off in range(3)
        for col_off in range(3)
    ]
    joined = jnp.concatenate(pieces, axis=-1)
    return joined.reshape(-1, joined.shape[-1])


def spread_back(flat_grads, kernel, sample_count, side):
    channels = kernel.shape[1]
    summed = jnp.zeros((sample_count, side + 2, side + 2, channels), jnp.float32)
    for tap_index in range(9):
        row_off, col_off = divmod(tap_index, 3)
        weight_tap = kernel[tap_index * channels : (tap_index + 1) * channels]
        contrib = lax.dot_general(
            flat_grads, weight_tap, (((1,), (1,)), ((), ())), preferred_element_type=jnp.float32
        )
        contrib = contrib.reshape(sample_count, side, side, channels)
        summed = summed + jnp.pad(
            contrib, ((0, 0), (row_off, 2 - row_off), (col_off, 2 - col_off), (0, 0))
        )
    return summed


def absorb_rims(interior, incoming):
    result = interior.at[..., 0, :, :].add(incoming[0])
    result = result.at[..., :, -1, :].add(incoming[1])
    result = result.at[..., -1, :, :].add(incoming[2])
    return result.at[..., :, 0, :].add(incoming[3])


def flip_edges(strips, flipped):
    return jnp.where(flipped[:, None, None, None], strips[:, :, ::-1, :], strips)


def pick_gathered(everything, near_tiles, facing, flipped, usable):
    flat = everything.reshape(everything.shape[0] * 4, -1)
    wanted = jnp.where(usable, near_tiles * 4 + facing, -1)
    selector = (lax.broadcasted_iota(jnp.int32, (4, flat.shape[0]), 1) == wanted[:, None]).astype(
        jnp.bfloat16
    )
    picked = jnp.dot(selector, flat, preferred_element_type=jnp.float32).astype(jnp.bfloat16)
    return flip_edges(picked.reshape((4,) + everything.shape[2:]), flipped)


LEAF = 128
SPAN = 384


def split(value):
    high = value.astype(jnp.bfloat16)
    return high, (value - high.astype(jnp.float32)).astype(jnp.bfloat16)


def split_wide(value):
    high = lax.reduce_precision(value, 8, 7)
    return high.astype(jnp.bfloat16), (value - high).astype(jnp.bfloat16)


def dot3(left, right, dims=(((1,), (0,)), ((), ()))):
    def one(a, b):
        return lax.dot_general(a, b, dims, preferred_element_type=jnp.float32)

    return one(left[0], right[0]) + (one(left[0], right[1]) + one(left[1], right[0]))


by_rows = (((1,), (1,)), ((), ()))


def leaf_inverse(block, m_ref, s_ref):
    row = lax.broadcasted_iota(jnp.int32, (LEAF, LEAF), 0)
    col = lax.broadcasted_iota(jnp.int32, (LEAF, LEAF), 1)
    on_diag = row == col
    unit = jnp.where(on_diag, 1.0, 0.0)
    kept = jnp.where(on_diag, block, 0.0)
    across = lax.rsqrt(jnp.sum(kept, axis=0, keepdims=True))
    down = lax.rsqrt(jnp.sum(kept, axis=1, keepdims=True))
    scaled = block * across * down
    m_ref[...] = jnp.where(on_diag, down, jnp.where(row > col, -scaled * across, 0.0))
    pair = split(block)
    rough = m_ref[...].astype(jnp.bfloat16)
    turned = jnp.dot(rough, pair[0], preferred_element_type=jnp.float32).astype(jnp.bfloat16)
    gap = lax.dot_general(turned, rough, by_rows, preferred_element_type=jnp.float32) - unit
    low = jnp.where(row > col, gap, jnp.where(on_diag, 0.5 * gap, 0.0)).astype(jnp.bfloat16)
    m_ref[...] -= jnp.dot(low, rough, preferred_element_type=jnp.float32)

    def more(carry):
        step, error = carry
        return (step < 12) & (error > 1e-4)

    def refine(carry):
        step, _ = carry
        guess = m_ref[...]
        guess_pair = split(guess)
        turned = dot3(guess_pair, pair)
        gap = dot3(split(turned), guess_pair, by_rows) - unit
        error = jnp.max(jnp.abs(gap))
        low = jnp.where(row > col, gap, jnp.where(on_diag, 0.5 * gap, 0.0))
        m_ref[...] = guess - dot3(split(low), guess_pair)
        return step + 1, error

    _, error = lax.while_loop(more, refine, (jnp.int32(0), jnp.float32(1.0)))

    @pl.when(jnp.logical_not(error <= 1e-4))
    def _():
        s_ref[...] = block
        m_ref[...] = unit

        def eliminate(j, carry):
            work = s_ref[...]
            line = s_ref[pl.ds(j, 1), :]
            lane = lax.broadcasted_iota(jnp.int32, (1, LEAF), 1)
            scale = lax.rsqrt(jnp.sum(jnp.where(lane == j, line, 0.0), axis=1, keepdims=True))
            column = jnp.sum(jnp.where(col == j, work, 0.0), axis=1, keepdims=True)
            side = lax.broadcasted_iota(jnp.int32, (LEAF, 1), 0)
            column = jnp.where(side > j, column * scale, 0.0)
            s_ref[...] = work - column * (line * scale)
            mine = m_ref[pl.ds(j, 1), :] * scale
            m_ref[...] = m_ref[...] - column * mine
            m_ref[pl.ds(j, 1), :] = mine
            return carry

        lax.fori_loop(0, LEAF, eliminate, 0)


def factor_kernel(
    gram_ref, side_ref, small_ref, y_ref, small_out_ref, a_ref, uh, ul, uth, utl, yh, yl, m_ref, s_ref
):
    width = gram_ref.shape[1]
    blocks = width // LEAF
    spans = width // SPAN
    leaf_inverse(small_ref[...], m_ref, s_ref)
    small_out_ref[...] = m_ref[...]
    a_ref[...] = gram_ref[...]
    y_ref[...] = side_ref[...]

    def block_step(k, carry):
        k0 = pl.multiple_of(k * LEAF, LEAF)
        leaf_inverse(a_ref[pl.ds(k0, LEAF), pl.ds(k0, LEAF)], m_ref, s_ref)
        inverse = split(m_ref[...])
        for span in range(spans):
            part = slice(span * SPAN, (span + 1) * SPAN)

            @pl.when((span + 1) * SPAN > k0 + LEAF)
            def _():
                value = dot3(inverse, split(a_ref[pl.ds(k0, LEAF), part]))
                uh[:, part], ul[:, part] = split(value)
                uth[part, :], utl[part, :] = split(value.T)

        value = dot3(inverse, split(y_ref[pl.ds(k0, LEAF), :]))
        y_ref[pl.ds(k0, LEAF), :] = value
        yh[...], yl[...] = split(value)

        def row_step(i, inner):
            i0 = pl.multiple_of(i * LEAF, LEAF)
            left = uth[pl.ds(i0, LEAF), :], utl[pl.ds(i0, LEAF), :]
            for span in range(spans):
                part = slice(span * SPAN, (span + 1) * SPAN)

                @pl.when((span + 1) * SPAN > i0)
                def _():
                    a_ref[pl.ds(i0, LEAF), part] -= dot3(left, (uh[:, part], ul[:, part]))

            y_ref[pl.ds(i0, LEAF), :] -= dot3(left, (yh[...], yl[...]))
            return inner

        lax.fori_loop(k + 1, blocks, row_step, 0)
        return carry

    lax.fori_loop(0, blocks, block_step, 0)


def factor_solve(gram, side, small):
    width, columns = side.shape
    vmem = pl.BlockSpec(memory_space=pltpu.VMEM)
    half = jnp.bfloat16
    return pl.pallas_call(
        factor_kernel,
        out_shape=(
            jax.ShapeDtypeStruct(side.shape, jnp.float32),
            jax.ShapeDtypeStruct(small.shape, jnp.float32),
        ),
        in_specs=[vmem] * 3,
        out_specs=(vmem, vmem),
        scratch_shapes=[
            pltpu.VMEM((width, width), jnp.float32),
            pltpu.VMEM((LEAF, width), half),
            pltpu.VMEM((LEAF, width), half),
            pltpu.VMEM((width, LEAF), half),
            pltpu.VMEM((width, LEAF), half),
            pltpu.VMEM((LEAF, columns), half),
            pltpu.VMEM((LEAF, columns), half),
            pltpu.VMEM((LEAF, LEAF), jnp.float32),
            pltpu.VMEM((LEAF, LEAF), jnp.float32),
        ],
        compiler_params=pltpu.CompilerParams(vmem_limit_bytes=40 * 1024 * 1024),
        name="factor_solve",
    )(gram, side, small)


high = lax.Precision.HIGH
tn = (((0,), (0,)), ((), ()))


def sum_kernel(dp_count, tiles, x_ref, out_ref, near, part, far, *sems):
    dp_index = lax.axis_index("dp")
    tile_index = lax.axis_index("tile")
    dp_peers = [lax.rem(dp_index + step, dp_count) for step in range(1, dp_count)]
    tile_peers = [lax.rem(tile_index + step, tiles) for step in range(1, tiles)]
    barrier = pltpu.get_barrier_semaphore()
    for axis, peers in (("dp", dp_peers), ("tile", tile_peers)):
        for peer in peers:
            pl.semaphore_signal(
                barrier, inc=1, device_id={axis: peer}, device_id_type=pl.DeviceIdType.MESH
            )
    pl.semaphore_wait(barrier, dp_count + tiles - 2)

    def exchange(axis, peers, source, target, send, receive):
        copies = [
            pltpu.make_async_remote_copy(
                src_ref=source(peer),
                dst_ref=target(slot),
                send_sem=send.at[slot],
                recv_sem=receive.at[slot],
                device_id={axis: peer},
                device_id_type=pl.DeviceIdType.MESH,
            )
            for slot, peer in enumerate(peers)
        ]
        for copy in copies:
            copy.start()
        for copy in copies:
            copy.wait()

    exchange("dp", dp_peers, lambda peer: x_ref.at[peer], lambda slot: near.at[slot], *sems[0:2])
    total = x_ref[dp_index]
    for slot in range(dp_count - 1):
        total = total + near[slot]
    part[...] = total
    exchange("tile", tile_peers, lambda peer: part.at[peer], lambda slot: far.at[slot], *sems[2:4])
    total = part[tile_index]
    for slot in range(tiles - 1):
        total = total + far[slot]
    out_ref[dp_index, tile_index] = total
    own = out_ref.at[dp_index, tile_index]
    exchange("tile", tile_peers, lambda peer: own, lambda slot: own, *sems[4:6])
    slab = out_ref.at[dp_index]
    exchange("dp", dp_peers, lambda peer: slab, lambda slot: slab, *sems[6:8])


def sum_everywhere(value):
    tiles = lax.axis_size("tile")
    dp_count = lax.axis_size("dp")
    rows, columns = value.shape
    if tiles < 2 or dp_count < 2 or rows % (tiles * dp_count):
        return lax.psum(value, ("tile", "dp"))
    piece = rows // (tiles * dp_count)
    vmem = pl.BlockSpec(memory_space=pltpu.VMEM)
    wide = (dp_count, tiles, piece, columns)
    counts = [dp_count - 1] * 2 + [tiles - 1] * 4 + [dp_count - 1] * 2
    out = pl.pallas_call(
        lambda *refs: sum_kernel(dp_count, tiles, *refs),
        out_shape=jax.ShapeDtypeStruct(wide, jnp.float32),
        in_specs=[vmem],
        out_specs=vmem,
        scratch_shapes=[
            pltpu.VMEM((dp_count - 1, tiles, piece, columns), jnp.float32),
            pltpu.VMEM((tiles, piece, columns), jnp.float32),
            pltpu.VMEM((tiles - 1, piece, columns), jnp.float32),
            *[pltpu.SemaphoreType.DMA((count,)) for count in counts],
        ],
        compiler_params=pltpu.CompilerParams(collective_id=0, has_side_effects=True),
        name="sum_everywhere",
    )(value.reshape(wide))
    return out.reshape(rows, columns)


def body_plain(
    activations,
    cotangent,
    kernel,
    turning,
    orient,
    left_factor,
    left_basis,
    right_factor,
    right_basis,
    momentum,
    second_moment,
):
    tiles = lax.axis_size("tile")
    dp_count = lax.axis_size("dp")
    tile_index = lax.axis_index("tile")
    dp_index = lax.axis_index("dp")
    tile_vals = activations[:, 0]
    tile_grads = cotangent[:, 0]
    sample_count = tile_vals.shape[0]
    side = tile_vals.shape[1]
    channels = tile_vals.shape[-1]
    own_turn = turning[0]
    facing = orient[0] % 4
    flipped = orient[0] >= 4
    heading = (jnp.arange(4, dtype=jnp.int32) + own_turn) % 4
    row_of = tile_index // 4
    col_of = tile_index % 4
    room = jnp.stack([row_of > 0, col_of < 3, row_of < tiles // 4 - 1, col_of > 0])
    usable = (
        jnp.sum(
            jnp.where(
                heading[:, None] == jnp.arange(4, dtype=jnp.int32)[None, :], room[None, :], False
            ),
            axis=1,
        )
        > 0
    )
    offsets = jnp.array([-4, 1, 4, -1], dtype=jnp.int32)
    near_tiles = tile_index + jnp.sum(
        jnp.where(heading[:, None] == jnp.arange(4, dtype=jnp.int32)[None, :], offsets[None, :], 0),
        axis=1,
    )
    strips = edge_strips(tile_vals)
    flat_grads = tile_grads.reshape(-1, channels)
    spread = spread_back(flat_grads, kernel, sample_count, side)
    rim_cells = cycle_strips(spread).astype(jnp.bfloat16)
    everything = lax.all_gather(
        jnp.concatenate([strips, rim_cells], axis=0)[None], "tile", axis=0, tiled=True
    )
    borders = pick_gathered(everything[:, :4], near_tiles, facing, flipped, usable)
    incoming = pick_gathered(everything[:, 4:], near_tiles, facing, flipped, usable)
    padded = assemble(tile_vals, borders)
    columns = tap_patches(padded, side)
    partial_grad = lax.dot_general(
        columns, flat_grads, (((0,), (0,)), ((), ())), preferred_element_type=jnp.float32
    )
    summed_grad = sum_everywhere(partial_grad)
    result = jnp.dot(columns, kernel, preferred_element_type=jnp.float32).astype(jnp.bfloat16)
    result = result.reshape(activations.shape)
    input_grad = absorb_rims(spread[:, 1:-1, 1:-1], incoming.astype(jnp.float32)).astype(
        jnp.bfloat16
    )
    input_grad = input_grad.reshape(cotangent.shape)
    cells = dp_count * sample_count * tiles * side * side
    grad = summed_grad * (1.0 / math.sqrt(cells))
    rows_per, width = left_factor.shape
    row_start = tile_index * rows_per
    moment_rows = momentum.shape[0]
    moment_start = dp_index * moment_rows
    grad_rows = lax.dynamic_slice_in_dim(grad, row_start, rows_per, 0)
    left_new = 0.95 * left_factor + 0.05 * lax.dot_general(
        grad_rows, grad, (((1,), (1,)), ((), ())), precision=high
    )
    basis_rows = lax.all_gather(left_basis, "dp", axis=1, tiled=True)
    basis = lax.all_gather(basis_rows.astype(jnp.bfloat16), "tile", axis=0, tiled=True)
    moments = lax.all_gather(
        jnp.concatenate([momentum, second_moment], axis=1), "dp", axis=0, tiled=True
    )
    all_momentum, all_second = moments[:, :channels], moments[:, channels:]
    back_rows = jnp.dot(basis_rows, all_momentum, precision=highest)
    own_row = row_start + lax.broadcasted_iota(jnp.int32, left_factor.shape, 0)
    own_col = lax.broadcasted_iota(jnp.int32, left_factor.shape, 1)
    diagonal = jnp.sum(jnp.where(own_row == own_col, left_factor, 0.0), axis=1, keepdims=True)
    rest = jnp.broadcast_to(split_wide(diagonal)[1], (rows_per, LEAF))
    factor = lax.all_gather(
        jnp.concatenate(
            [left_factor.astype(jnp.bfloat16), *split_wide(back_rows), rest], axis=1
        ),
        "tile",
        axis=0,
        tiled=True,
    )
    back = factor[:, width : width + channels].astype(jnp.float32) + factor[
        :, width + channels : width + 2 * channels
    ].astype(jnp.float32)
    rest = factor[:, width + 2 * channels : width + 2 * channels + 1]
    factor = factor[:, :width]
    mapped = 0.95 * (
        jnp.dot(factor, basis, preferred_element_type=jnp.float32)
        + rest.astype(jnp.float32) * basis.astype(jnp.float32)
    )
    mapped_gram = lax.dot_general(mapped, mapped, tn, precision=high)
    mapped_back = lax.dot_general(mapped, back, tn, precision=high)
    crossed = sum(
        lax.dot_general(term, basis, tn, preferred_element_type=jnp.float32) for term in split_wide(grad)
    )
    mapped_grad = lax.dot_general(mapped, grad, tn, precision=high)
    grad_gram = lax.dot_general(grad, grad, tn, precision=high)
    grad_back = lax.dot_general(grad, back, tn, precision=high)
    weight = 0.05 * mapped_grad + 0.00125 * lax.dot_general(crossed, grad_gram, tn, precision=high)
    gram = mapped_gram + lax.dot_general(
        jnp.concatenate([weight.T, crossed], axis=0),
        jnp.concatenate([crossed, weight.T], axis=0),
        tn,
        precision=high,
    )
    power_rows = lax.dynamic_slice_in_dim(mapped, row_start, rows_per, 0) + 0.05 * jnp.dot(
        grad_rows, crossed, precision=high
    )
    power_side = jnp.concatenate([mapped_back, mapped_grad], axis=1) + 0.05 * lax.dot_general(
        crossed, jnp.concatenate([grad_back, grad_gram], axis=1), tn, precision=high
    )
    right_new = 0.95 * right_factor + 0.05 * grad_gram
    right_power = jnp.dot(right_new, right_basis, precision=high)
    right_gram = lax.dot_general(right_power, right_power, tn, precision=high)
    solved, right_inverse = factor_solve(
        gram, jnp.concatenate([power_side, power_rows.T], axis=1), right_gram
    )
    turned_momentum = solved[:, :channels]
    turned_grad = solved[:, channels : 2 * channels]
    basis_new = solved[:, 2 * channels :].T
    right_basis_new = lax.dot_general(
        right_power, right_inverse, (((1,), (1,)), ((), ())), precision=high
    )
    right_turn = lax.dot_general(right_basis, right_basis_new, tn, precision=high)
    rotated = jnp.dot(turned_momentum, right_turn, precision=high)
    projected = jnp.dot(turned_grad, right_basis_new, precision=high)
    momentum_all = 0.9 * rotated + 0.1 * projected
    second_all = 0.95 * all_second + 0.05 * projected * projected
    normalized = momentum_all / (jnp.sqrt(second_all) + epsilon)
    momentum_new = lax.dynamic_slice_in_dim(momentum_all, moment_start, moment_rows, 0)
    second_new = lax.dynamic_slice_in_dim(second_all, moment_start, moment_rows, 0)
    update_rows = jnp.dot(basis_new, normalized, precision=high)
    update = lax.dot_general(
        update_rows, right_basis_new, (((1,), (1,)), ((), ())), precision=high
    )
    return (
        result,
        input_grad,
        grad,
        left_new,
        basis_new,
        right_new,
        right_basis_new,
        momentum_new,
        second_new,
        update,
    )


ZS = 4
CORES = 2
DPS = 4
LANES = 384
CELL = 24


def to_device(source, target, send, receive, **device):
    return pltpu.make_async_remote_copy(
        src_ref=source,
        dst_ref=target,
        send_sem=send,
        recv_sem=receive,
        device_id=device,
        device_id_type=pl.DeviceIdType.MESH,
    )


def greet():
    t = lax.axis_index("tile")
    d = lax.axis_index("dp")
    barrier = pltpu.get_barrier_semaphore()
    tiles = ZS * CORES
    for step in range(1, tiles):
        pl.semaphore_signal(
            barrier,
            inc=1,
            device_id={"tile": lax.rem(t + step, tiles)},
            device_id_type=pl.DeviceIdType.MESH,
        )
    for step in range(1, DPS):
        pl.semaphore_signal(
            barrier,
            inc=1,
            device_id={"dp": lax.rem(d + step, DPS)},
            device_id_type=pl.DeviceIdType.MESH,
        )
    pl.semaphore_wait(barrier, tiles + DPS - 2)


class Edges:
    def __init__(self, source, target, send, receive):
        t = lax.axis_index("tile")
        row, col = t // 4, t % 4
        self.rooms = (row > 0, col < 3, row < 1, col > 0)
        self.target = target
        self.copies = []
        for h, step in enumerate((4, 1, 4, 7)):
            back = (h + 2) % 4
            peer = lax.rem(t + step, ZS * CORES)
            self.copies.append(
                to_device(source.at[h], target.at[back], send.at[h], receive.at[back], tile=peer)
            )

    def start(self):
        for h in range(4):

            @pl.when(self.rooms[h])
            def _():
                self.copies[h].start()

            @pl.when(jnp.logical_not(self.rooms[h]))
            def _():
                self.target[h] = jnp.zeros(self.target.shape[1:], self.target.dtype)

    def wait(self):
        for h in range(4):

            @pl.when(self.rooms[h])
            def _():
                self.copies[h].wait_send()
                self.copies[(h + 2) % 4].wait_recv()


def finish_kernel(
    grad_ref,
    back_ref,
    mapped_ref,
    crossed_ref,
    grad_both_ref,
    left_new_ref,
    right_in_ref,
    right_basis_ref,
    second_ref,
    result_ref,
    input_grad_ref,
    result_out,
    input_grad_out,
    grad_out,
    left_out,
    basis_out,
    right_out,
    right_basis_out,
    momentum_out,
    second_out,
    update_out,
    m_ref,
    left_ref,
    right_ref,
    work_ref,
    gram_ref,
    up_ref,
    down_ref,
    y_ref,
    turn_ref,
    aux_ref,
    big_ref,
):
    t = lax.axis_index("tile")
    d = lax.axis_index("dp")
    width, channels = grad_ref.shape
    blocks = width // LEAF
    rows_per = left_new_ref.shape[0]
    moment_rows = momentum_out.shape[0]
    wide = work_ref.shape[1]
    own_rows = pl.ds(pl.multiple_of(t * rows_per, 16), rows_per)

    result_out[...] = result_ref[...]
    input_grad_out[...] = input_grad_ref[...]
    extra = LEAF // 4

    lane = lax.broadcasted_iota(jnp.int32, (1, LEAF), 1)

    def tile_of(middle, shared, folded, j):
        group, spot = divmod(j, 2)
        if spot:
            return middle(group)
        if group == 0:
            return shared(0)
        value = jnp.where(lane >= extra * (group - 1), folded(group - 1), shared(group - 1))
        return jnp.where(lane >= extra * group, shared(group), value) if group < DPS else value

    def stack(g, begin, end):
        blocks_of = [mapped_ref[g, tile, begin:end, :] for tile in range(mapped_ref.shape[1])]
        return jnp.concatenate(blocks_of, axis=0).astype(jnp.float32)

    def folded_rows(g):
        return jnp.concatenate(
            [
                unfold(mapped_ref[g, tile, 2 * rows_per :, :].astype(jnp.float32), 3)
                for tile in range(mapped_ref.shape[1])
            ],
            axis=0,
        )

    for j in range(blocks):
        at = slice(j * LEAF, (j + 1) * LEAF)
        value = tile_of(
            lambda g: stack(g, 0, rows_per), lambda g: stack(g, rows_per, 2 * rows_per), folded_rows, j
        ).astype(jnp.bfloat16)
        m_ref[:, at] = value
        left_ref[at, :width] = value.T
    crossed = jnp.concatenate(
        [
            tile_of(
                lambda g: crossed_ref[g, :channels, :].astype(jnp.float32),
                lambda g: crossed_ref[g, channels : 2 * channels, :].astype(jnp.float32),
                lambda g: unfold(crossed_ref[g, 2 * channels :, :].astype(jnp.float32), 4),
                j,
            )
            for j in range(blocks)
        ],
        axis=1,
    )
    grad = grad_ref[...]
    grad_out[...] = grad
    grad_t = grad.T
    both = jnp.concatenate([back_ref[...], grad], axis=1)
    both_pair = split(both)
    grad_both = grad_both_ref[...]
    grad_gram = grad_both[:, channels:]
    grad_rows = grad_ref[own_rows, :]
    left_out[...] = left_new_ref[...]
    right_out[...] = right_in_ref[0]
    right_basis_out[...] = right_in_ref[4]
    turn_ref[...] = right_in_ref[5]

    grad_m = product(jnp.concatenate(split(grad_t), axis=0), m_ref[...])
    weight = 0.05 * (grad_m[:channels] + grad_m[channels:]) + 0.00125 * matmul(grad_gram, crossed)
    pair = jnp.concatenate([weight, crossed], axis=0)
    pair_t = pair.T
    left_ref[:, width:] = wide_left(split(pair_t))
    right_ref[...] = wide_right(split(jnp.concatenate([crossed, weight], axis=0)))
    for j in range(0, blocks, 2):
        end = min(j + 2, blocks) * LEAF
        at = slice(j * LEAF, end)
        value = product(left_ref[:end, :width], m_ref[:, at]) + product(
            left_ref[:end, width:], right_ref[:, at]
        )
        work_ref[:end, at] = value
        gram_ref[:end, at] = value
    m_both = product(left_ref[:, :width], both_pair[0]) + product(left_ref[:, :width], both_pair[1])
    crossed_t = pair_t[:, channels:]
    work_ref[:, width : width + 2 * channels] = m_both + 0.05 * matmul(crossed_t, grad_both)
    power_rows = m_ref[own_rows, :].astype(jnp.float32) + 0.05 * matmul(grad_rows, crossed)
    padded = jnp.concatenate(
        [power_rows, jnp.zeros((2 * LEAF - rows_per, width), jnp.float32)], axis=0
    )
    work_ref[:, width + 2 * channels :] = padded.T
    gram_ref[:, width:] = work_ref[:, width:]

    worst = right_in_ref[3]
    for k in range(blocks):
        at = slice(k * LEAF, (k + 1) * LEAF)
        inverse, gap = quick_leaf(work_ref[at, at])
        worst = jnp.maximum(worst, gap)
        value = product(wide_left(split(inverse)), wide_right(split(work_ref[at, (k + 1) * LEAF :])))
        y_ref[at, :] = value[:, width - (k + 1) * LEAF :]
        if k == blocks - 1:
            break
        start = (k + 1) * LEAF
        up_ref[:, start:] = wide_right(split(value))
        down_ref[start:, :] = wide_left(split(value[:, : width - start].T))
        edges = list(range(start, width, 2 * LEAF))
        spans = [(a, min(a + 2 * LEAF, width)) for a in edges] + [
            (a, a + 2 * LEAF) for a in range(width, wide, 2 * LEAF)
        ]
        for a, b in spans:
            bottom = min(b, width)
            work_ref[start:bottom, a:b] -= product(down_ref[start:bottom, :], up_ref[:, a:b])

    @pl.when(jnp.logical_not(jnp.max(worst) <= 0.03))
    def _():
        leaf_inverse(right_in_ref[2], big_ref, aux_ref)
        turned = matmul_rows(right_in_ref[1], big_ref[...])
        right_basis_out[...] = turned
        turn_ref[...] = matmul(right_basis_ref[...].T, turned)
        work_ref[...] = gram_ref[...]

        def block_step(k, carry):
            k0 = pl.multiple_of(k * LEAF, LEAF)
            leaf_inverse(work_ref[pl.ds(k0, LEAF), pl.ds(k0, LEAF)], big_ref, aux_ref)
            inverse = wide_left(split(big_ref[...]))
            for a in range(0, wide, LEAF):
                value = product(inverse, wide_right(split(work_ref[pl.ds(k0, LEAF), a : a + LEAF])))
                up_ref[:, a : a + LEAF] = wide_right(split(value))
                if a < width:
                    down_ref[a : a + LEAF, :] = wide_left(split(value.T))
                else:
                    y_ref[pl.ds(k0, LEAF), a - width : a - width + LEAF] = value

            def row_step(i, inner):
                i0 = pl.multiple_of(i * LEAF, LEAF)
                left = down_ref[pl.ds(i0, LEAF), :]
                for a in range(0, wide, LEAF):

                    @pl.when(a + LEAF > i0)
                    def _():
                        work_ref[pl.ds(i0, LEAF), a : a + LEAF] -= product(
                            left, up_ref[:, a : a + LEAF]
                        )

                return inner

            lax.fori_loop(k + 1, blocks, row_step, 0)
            return carry

        lax.fori_loop(0, blocks, block_step, 0)

    right_basis_new = right_basis_out[...]
    right_turn = turn_ref[...]
    solved = y_ref[...]
    rotated = matmul(solved[:, :channels], right_turn)
    projected = matmul(solved[:, channels : 2 * channels], right_basis_new)
    basis_new = solved[:, 2 * channels :].T[:rows_per]
    basis_out[...] = basis_new
    momentum = 0.9 * rotated + 0.1 * projected
    second = 0.95 * second_ref[...] + 0.05 * projected * projected
    up = momentum / (jnp.sqrt(second) + epsilon)
    update_rows = matmul(basis_new, up)
    update_out[...] = matmul_rows(update_rows, right_basis_new)
    y_ref[:, :channels] = momentum
    y_ref[:, channels : 2 * channels] = second
    own = pl.ds(pl.multiple_of(d * moment_rows, 8), moment_rows)
    momentum_out[...] = y_ref[own, :channels]
    second_out[...] = y_ref[own, channels : 2 * channels]


def finish(
    grad, back, mapped, crossed, grad_both, left_new, right, right_basis, second, result, input_grad, moment_rows
):
    vmem = pl.BlockSpec(memory_space=pltpu.VMEM)
    width, channels = grad.shape
    rows_per = left_new.shape[0]
    wide = width + 2 * channels + 2 * LEAF
    half = jnp.bfloat16
    single = jnp.float32
    square = pltpu.VMEM((LEAF, LEAF), single)
    shapes = [
        left_new.shape,
        left_new.shape,
        right_basis.shape,
        right_basis.shape,
        (moment_rows, channels),
        (moment_rows, channels),
        (rows_per, channels),
    ]
    return pl.pallas_call(
        finish_kernel,
        out_shape=(
            jax.ShapeDtypeStruct(result.shape, half),
            jax.ShapeDtypeStruct(input_grad.shape, half),
            jax.ShapeDtypeStruct(grad.shape, single),
            *(jax.ShapeDtypeStruct(shape, single) for shape in shapes),
        ),
        in_specs=[vmem] * 11,
        out_specs=(vmem,) * 10,
        scratch_shapes=[
            pltpu.VMEM((width, width), half),
            pltpu.VMEM((width, width + 6 * channels), half),
            pltpu.VMEM((6 * channels, width), half),
            pltpu.VMEM((width, wide), single),
            pltpu.VMEM((width, wide), single),
            pltpu.VMEM((3 * LEAF, wide), half),
            pltpu.VMEM((width, 3 * LEAF), half),
            pltpu.VMEM((width, wide - width), single),
            square,
            square,
            square,
        ],
        compiler_params=pltpu.CompilerParams(vmem_limit_bytes=56 * 1024 * 1024),
        name="finish",
    )(
        grad, back, mapped, crossed, grad_both, left_new, right, right_basis, second, result, input_grad
    )


def wide_left(pair, axis=1):
    return jnp.concatenate([pair[0], pair[0], pair[1]], axis=axis)


def wide_right(pair, axis=0):
    return jnp.concatenate([pair[0], pair[1], pair[0]], axis=axis)


plain = (((1,), (0,)), ((), ()))


def product(left, right):
    return lax.dot_general(left, right, plain, preferred_element_type=jnp.float32)


def product_rows(left, right):
    return lax.dot_general(left, right, by_rows, preferred_element_type=jnp.float32)


def matmul(left, right):
    return product(wide_left(split(left)), wide_right(split(right)))


def matmul_rows(left, right):
    return product_rows(wide_left(split(left)), wide_right(split(right), 1))


def quick_leaf(block, cheap=2):
    row = lax.broadcasted_iota(jnp.int32, (LEAF, LEAF), 0)
    col = lax.broadcasted_iota(jnp.int32, (LEAF, LEAF), 1)
    on_diag = row == col
    below = row > col
    unit = jnp.where(on_diag, 1.0, 0.0)
    kept = jnp.where(on_diag, block, 0.0)
    across = lax.rsqrt(jnp.sum(kept, axis=0, keepdims=True))
    down = lax.rsqrt(jnp.sum(kept, axis=1, keepdims=True))

    def lower(gap):
        return jnp.where(below, gap, jnp.where(on_diag, 0.5 * gap, 0.0)).astype(jnp.bfloat16)

    high_part, low_part = split(block)
    guess = jnp.where(on_diag, down, jnp.where(below, -block * (across * across) * down, 0.0))
    for _ in range(cheap):
        rough = guess.astype(jnp.bfloat16)
        turned = product(rough, high_part).astype(jnp.bfloat16)
        gap = product_rows(turned, rough) - unit
        guess = rough.astype(jnp.float32) - product(lower(gap), rough)
    rough = guess.astype(jnp.bfloat16)
    twice = jnp.concatenate([rough, rough], axis=1)
    turned = product(twice, jnp.concatenate([high_part, low_part], axis=0))
    gap = product_rows(jnp.concatenate(split(turned), axis=1), twice) - unit
    return rough.astype(jnp.float32) - product(lower(gap), rough), jnp.abs(gap)


def fold(value, parts):
    step = LEAF // 4
    rows = value.shape[0] // parts
    total = value[:rows]
    for i in range(1, parts):
        total = total + pltpu.roll(value[i * rows : (i + 1) * rows], step * i, 1)
    return total


def unfold(value, parts):
    step = LEAF // 4
    return jnp.concatenate(
        [value] + [pltpu.roll(value, LEAF - step * i, 1) for i in range(1, parts)], axis=0
    )


SEMS = {
    "edge": 4,
    "rim": 4,
    "basis_z": 3,
    "basis_sib": 4,
    "back_sum": 3,
    "back_z": 3,
    "back_dp": 3,
    "back_sib": 4,
    "second_dp": 3,
    "second_sib": 3,
    "swap": 1,
    "grad_sum": 3,
    "grad_zsum": 3,
    "grad_z": 3,
    "grad_dp": 3,
    "grad_sib": 4,
    "map_z": 3,
    "map_x": 4,
    "map_y": 4,
    "map_far": 8,
    "map_sib": 16,
    "cross_dp": 3,
    "cross_sib": 3,
}
CUT = 176


def exchange_kernel(
    grad_scale,
    meta_ref,
    act_ref,
    cot_ref,
    kernel_ref,
    basis_in_ref,
    momentum_ref,
    second_ref,
    factor_ref,
    right_factor_ref,
    right_basis_ref,
    result_ref,
    input_grad_ref,
    grad_ref,
    back_ref,
    seconds_ref,
    all_ref,
    crossed_ref,
    grad_both_ref,
    left_ref,
    right_ref,
    strips,
    borders,
    rims,
    incoming,
    block_ref,
    basis,
    columns_ref,
    back_in_ref,
    back_near,
    back_all,
    padded,
    patches,
    spread,
    inner,
    partial,
    near,
    half,
    dp_in,
    pieces,
    z_in,
    grad_all,
    own_map,
    *sems,
):
    count = len(SEMS)
    send = dict(zip(SEMS, sems[:count]))
    receive = dict(zip(SEMS, sems[count:]))
    t = lax.axis_index("tile")
    d = lax.axis_index("dp")
    z, c = t // CORES, t % CORES
    sibling = t + 1 - 2 * c
    x_peer = d + 1 - 2 * (d % 2)
    y_peer = lax.rem(d + 2, DPS)
    far_peer = lax.rem(x_peer + 2, DPS)
    rest = range(1, ZS)
    z_peers = [lax.rem(t + CORES * k, ZS * CORES) for k in range(ZS)]
    z_from = [lax.rem(z + ZS - k, ZS) for k in range(ZS)]
    z_to = [lax.rem(z + k, ZS) for k in range(ZS)]
    d_to = [lax.rem(d + j, DPS) for j in range(DPS)]
    d_from = [lax.rem(d + DPS - j, DPS) for j in range(DPS)]
    side = input_grad_ref.shape[0] // CELL
    channels = grad_ref.shape[1]
    width = grad_ref.shape[0]
    pending = []

    def copy(name, index, source, target, **device):
        made = to_device(source, target, send[name].at[index], receive[name].at[index], **device)
        pending.append(made)
        return made

    def start(copies):
        for made in copies:
            made.start()

    def arrive(copies):
        for made in copies:
            made.wait_recv()

    def z_group(name, source, target):
        return [copy(name, k - 1, source(k), target(k), tile=z_peers[k]) for k in rest]

    def dp_group(name, source, target):
        return [copy(name, j - 1, source(j), target(j), dp=d_to[j]) for j in rest]

    part = basis_in_ref.shape[1]
    rows_per = basis_in_ref.shape[0]
    extra = part % LEAF
    old_basis = basis_in_ref[...]
    shifted = jnp.zeros((rows_per, LANES), jnp.float32)
    for slot in range(DPS):
        pieces_of = [old_basis, jnp.zeros((rows_per, LANES - part - extra * slot), jnp.float32)]
        if slot:
            pieces_of.insert(0, jnp.zeros((rows_per, extra * slot), jnp.float32))
        pieces_of = [p for p in pieces_of if p.shape[1]]
        shifted = jnp.where(d == slot, jnp.concatenate(pieces_of, axis=1), shifted)
    lane = lax.broadcasted_iota(jnp.int32, (1, LEAF), 1)
    window = (lane >= extra * d) & (lane < extra * (d + 1))
    first_tile, last_tile = shifted[:, :LEAF], shifted[:, 2 * LEAF :]
    block_ref[...] = jnp.concatenate(
        [
            shifted[:, LEAF : 2 * LEAF],
            jnp.where(lane >= extra * d, first_tile, last_tile),
            fold(jnp.where(window, last_tile, 0.0), 3),
        ],
        axis=0,
    ).astype(jnp.bfloat16)
    greet()
    own_basis = basis.at[z, c]
    basis_z = z_group("basis_z", lambda k: block_ref, lambda k: own_basis)
    basis_sib = [
        copy(
            "basis_sib",
            k,
            block_ref if k == 0 else basis.at[z_from[k], c],
            basis.at[z_from[k], c],
            tile=sibling,
        )
        for k in range(ZS)
    ]
    back_sum = dp_group("back_sum", lambda j: back_in_ref.at[d_to[j]], lambda j: back_near.at[j - 1])
    second_dp = dp_group("second_dp", lambda j: second_ref.at[c], lambda j: seconds_ref.at[d, c])
    start(basis_z)
    start(basis_sib[:1])

    turn = meta_ref[0]
    padded[...] = jnp.zeros(padded.shape, jnp.float32)
    padded[1 : side + 1, 1 : side + 1, :] = act_ref[...].astype(jnp.float32).reshape(side, side, channels)
    line = lax.broadcasted_iota(jnp.int32, (side, side), 0)
    place = lax.broadcasted_iota(jnp.int32, (side, side), 1)
    straight = jnp.where(line == place, 1.0, 0.0)
    crosswise = jnp.where(line + place == side - 1, 1.0, 0.0)
    orders = [
        jnp.where(meta_ref[1 + e] > 0, crosswise, straight).astype(jnp.bfloat16) for e in range(4)
    ]

    def fill(target, lines):
        aligned = [product(orders[e], lines[e].astype(jnp.bfloat16)) for e in range(4)]
        for h in range(4):
            wanted = lax.rem(h + 4 - turn, 4)
            target[h] = sum(jnp.where(wanted == e, aligned[e], 0.0) for e in range(4)).astype(
                jnp.bfloat16
            )

    fill(
        strips,
        [
            padded[1, 1 : side + 1, :],
            padded[1 : side + 1, side, :],
            padded[side, 1 : side + 1, :],
            padded[1 : side + 1, 1, :],
        ],
    )
    edges = Edges(strips, borders, send["edge"], receive["edge"])
    edges.start()
    old_pair, moment_pair = split(old_basis), split(momentum_ref[...])
    value = product(old_pair[0], moment_pair[0]) + (
        product(old_pair[0], moment_pair[1]) + product(old_pair[1], moment_pair[0])
    )
    piece = rows_per // DPS
    for dp in range(DPS):
        back_in_ref[dp] = value[dp * piece : (dp + 1) * piece]
    start(back_sum)
    start(second_dp)
    own_basis[...] = block_ref[...]
    seconds_ref[d] = second_ref[...]

    cot = cot_ref[...]
    cot_t = jnp.concatenate(
        [cot.astype(jnp.float32), jnp.zeros((LEAF - side * side % LEAF, channels), jnp.float32)], axis=0
    ).T[:, : side * side].astype(jnp.bfloat16)

    def pick(ref, wanted):
        return sum(
            jnp.where(wanted == h, ref[h].astype(jnp.float32), 0.0) for h in range(4)
        )

    edges.wait()
    border = [pick(borders, lax.rem(turn + e, 4)) for e in range(4)]
    padded[0, 1 : side + 1, :] = border[0]
    padded[1 : side + 1, side + 1, :] = border[1]
    padded[side + 1, 1 : side + 1, :] = border[2]
    padded[1 : side + 1, 0, :] = border[3]
    for col in range(3):
        lines = padded[:, col : col + side, :].reshape((side + 2) * side, channels)
        for row in range(3):
            at = (3 * row + col) * channels
            patches[:, at : at + channels] = lines[row * side : row * side + side * side].astype(
                jnp.bfloat16
            )
    turned = product(cot_t, patches[...])
    block = partial.shape[2]
    value = turned.T
    for core in range(CORES):
        for dp in range(DPS):
            at = (core * DPS + dp) * block
            partial[core, dp] = value[at : at + block]
    swap = copy("swap", 0, partial.at[1 - c], near, tile=sibling)
    swap.start()

    arrive(back_sum)
    total = back_in_ref[d]
    for slot in range(DPS - 1):
        total = total + back_near[slot]
    back_all[c, d, z] = total
    mine = back_all.at[c, d, z]
    back_z = z_group("back_z", lambda k: mine, lambda k: mine)
    start(back_z)

    swap.wait_recv()
    half[...] = partial[c] + near[...]
    grad_sum = dp_group("grad_sum", lambda j: half.at[d_to[j]], lambda j: dp_in.at[j - 1])
    start(grad_sum)

    for k in rest:
        basis_z[k - 1].wait_recv()
        basis_sib[k].start()
    arrive(back_z)
    slab = back_all.at[c, d]
    back_dp = dp_group("back_dp", lambda j: slab, lambda j: slab)
    start(back_dp)

    arrive(basis_sib)
    for at_z in range(ZS):
        for core in range(CORES):
            at = (at_z * CORES + core) * rows_per
            at = slice(at, at + rows_per)
            columns_ref[at, :LEAF] = basis[at_z, core, :rows_per]
            columns_ref[at, LEAF : 2 * LEAF] = basis[at_z, core, rows_per : 2 * rows_per]
            columns_ref[at, 2 * LEAF :] = unfold(
                basis[at_z, core, 2 * rows_per :].astype(jnp.float32), 3
            ).astype(jnp.bfloat16)
    columns = columns_ref[...]
    factor = split(factor_ref[...])
    mapped = 0.95 * (product(factor[0], columns) + product(factor[1], columns))
    mapped = jnp.concatenate(
        [
            mapped[:, :LEAF],
            mapped[:, LEAF : 2 * LEAF],
            fold(jnp.where(window, mapped[:, 2 * LEAF :], 0.0), 3),
        ],
        axis=0,
    ).astype(jnp.bfloat16)
    own_map[...] = mapped
    all_ref[d, z, c] = mapped

    def spot_of(dp, k):
        return all_ref.at[dp, z_from[k], c]

    def own_spot(k):
        return own_map if k == 0 else spot_of(d, k)

    map_z = z_group("map_z", lambda k: own_map, lambda k: spot_of(d, 0))
    map_x = [copy("map_x", k, own_spot(k), spot_of(d, k), dp=x_peer) for k in range(ZS)]
    map_y = [copy("map_y", k, own_spot(k), spot_of(d, k), dp=y_peer) for k in range(ZS)]
    map_sib = [copy("map_sib", k, own_spot(k), spot_of(d, k), tile=sibling) for k in range(ZS)]
    upper, lower = pl.ds(0, CUT), pl.ds(CUT, own_map.shape[0] - CUT)

    def relay(k):
        up = spot_of(x_peer, k).at[upper]
        down = spot_of(y_peer, k).at[lower]
        return [
            copy("map_far", 2 * k, up, up, dp=y_peer),
            copy("map_far", 2 * k + 1, down, down, dp=x_peer),
        ]

    relays = [relay(k) for k in range(ZS)]

    def relay_arrive(k):
        arrive(relays[k])

    start(map_z)
    start([map_x[0], map_y[0], map_sib[0]])

    arrive(grad_sum)
    total = half[d]
    for slot in range(DPS - 1):
        total = total + dp_in[slot]
    for k in range(ZS):
        pieces[k] = total[k * piece : (k + 1) * piece]
    grad_zsum = z_group("grad_zsum", lambda k: pieces.at[z_to[k]], lambda k: z_in.at[k - 1])
    start(grad_zsum)

    arrive(grad_zsum)
    total = pieces[z]
    for slot in range(ZS - 1):
        total = total + z_in[slot]
    grad_all[c, d, z] = total
    own_piece = grad_all.at[c, d, z]
    grad_z = z_group("grad_z", lambda k: own_piece, lambda k: own_piece)
    start(grad_z)

    def slabs(ref, name):
        spots = [ref.at[c, d_from[j]] for j in range(DPS)]
        return [copy(name, j, spots[j], spots[j], tile=sibling) for j in range(DPS)]

    arrive(back_dp)
    back_sib = slabs(back_all, "back_sib")
    start(back_sib)
    second_sib = []
    for j in rest:
        spot = seconds_ref.at[d_from[j], c]
        second_sib.append(copy("second_sib", j - 1, spot, spot, tile=sibling))
    arrive(second_dp)
    start(second_sib)

    arrive(grad_z)
    grad_slab = grad_all.at[c, d]
    grad_dp = dp_group("grad_dp", lambda j: grad_slab, lambda j: grad_slab)
    start(grad_dp)

    for k in rest:
        map_z[k - 1].wait_recv()
        start([map_x[k], map_y[k], map_sib[k]])

    terms = product_rows(cot, kernel_ref[...])
    spread[...] = jnp.zeros(spread.shape, jnp.float32)
    for col in range(3):
        stack = None
        for row in range(3):
            at = (3 * row + col) * channels
            term = terms[:, at : at + channels]
            parts = [term]
            if row:
                parts.insert(0, jnp.zeros((row * side, channels), jnp.float32))
            if row < 2:
                parts.append(jnp.zeros(((2 - row) * side, channels), jnp.float32))
            term = jnp.concatenate(parts, axis=0)
            stack = term if stack is None else stack + term
        spread[:, col : col + side, :] += stack.reshape(side + 2, side, channels)
    fill(
        rims,
        [
            spread[0, 1 : side + 1, :],
            spread[1 : side + 1, side + 1, :],
            spread[side + 1, 1 : side + 1, :],
            spread[1 : side + 1, 0, :],
        ],
    )
    rim_edges = Edges(rims, incoming, send["rim"], receive["rim"])
    rim_edges.start()

    def far_sib(j, k):
        spot = spot_of((x_peer, y_peer, far_peer)[j], k)
        return copy("map_sib", ZS * (j + 1) + k, spot, spot, tile=sibling)

    map_far = [[far_sib(j, k) for k in range(ZS)] for j in range(3)]

    def pass_on(k):
        arrive([map_x[k], map_y[k]])
        start(relays[k])
        start([map_far[0][k], map_far[1][k]])

    pass_on(0)
    result_ref[...] = product(patches[...], kernel_ref[...]).astype(jnp.bfloat16)
    pass_on(1)

    grad_sib = slabs(grad_all, "grad_sib")
    grad_sib[0].start()
    for j in rest:
        grad_dp[j - 1].wait_recv()
        grad_sib[j].start()
    arrive(grad_sib)
    for core in range(CORES):
        for dp in range(DPS):
            for at_z in range(ZS):
                at = ((core * DPS + dp) * ZS + at_z) * piece
                grad_ref[at : at + piece] = grad_all[core, dp, at_z]
    grad = grad_ref[...] * grad_scale
    grad_ref[...] = grad
    grad_t = grad.T
    high_part, low_part = split(grad_t)
    crossed = product(high_part, columns) + product(low_part, columns)
    crossed = jnp.concatenate(
        [
            crossed[:, :LEAF],
            crossed[:, LEAF : 2 * LEAF],
            fold(jnp.where(window, crossed[:, 2 * LEAF :], 0.0), 4),
        ],
        axis=0,
    ).astype(jnp.bfloat16)
    halves = crossed.shape[0] // CORES
    for core in range(CORES):
        crossed_ref[d, core] = crossed[core * halves : (core + 1) * halves]
    own_cross = crossed_ref.at[d, c]
    cross_dp = dp_group("cross_dp", lambda j: own_cross, lambda j: own_cross)
    start(cross_dp)

    pass_on(2)
    arrive(back_sib)
    for core in range(CORES):
        for dp in range(DPS):
            for at_z in range(ZS):
                to = ((at_z * CORES + core) * DPS + dp) * piece
                back_ref[to : to + piece] = back_all[core, dp, at_z]

    both = jnp.concatenate([back_ref[...], grad], axis=1)
    grad_both = product(wide_left(split(grad_t)), wide_right(split(both)))
    grad_both_ref[...] = grad_both
    own_rows = pl.ds(pl.multiple_of(t * rows_per, 16), rows_per)
    left_ref[...] = 0.95 * factor_ref[...] + 0.05 * matmul_rows(grad_ref[own_rows, :], grad)
    right_new = 0.95 * right_factor_ref[...] + 0.05 * grad_both[:, channels:]
    right_basis = right_basis_ref[...]
    right_power = matmul(right_new, right_basis)
    right_gram = matmul(right_power.T, right_power)
    pass_on(3)
    right_inverse, right_gap = quick_leaf(right_gram, 4)
    right_basis_new = matmul_rows(right_power, right_inverse)
    right_turn = matmul(right_basis.T, right_basis_new)
    for slot, value in enumerate(
        (right_new, right_power, right_gram, right_gap, right_basis_new, right_turn)
    ):
        right_ref[slot] = value

    for k in range(ZS):
        relay_arrive(k)
        map_far[2][k].start()

    cross_sib = []
    for j in rest:
        spot = crossed_ref.at[d_from[j], c]
        cross_dp[j - 1].wait_recv()
        made = copy("cross_sib", j - 1, spot, spot, tile=sibling)
        made.start()
        cross_sib.append(made)
    rim_edges.wait()
    value = [pick(incoming, lax.rem(turn + e, 4)) for e in range(4)]
    inner[...] = spread[1 : side + 1, 1 : side + 1, :]
    inner[0, :, :] += value[0]
    inner[:, side - 1, :] += value[1]
    inner[side - 1, :, :] += value[2]
    inner[:, 0, :] += value[3]
    input_grad_ref[...] = inner[...].reshape(side * side, channels).astype(jnp.bfloat16)

    arrive(second_sib)
    arrive(map_sib)
    for group in map_far:
        arrive(group)
    arrive(cross_sib)
    for made in pending:
        made.wait_send()


def exchange(
    meta, acts, cots, kernel, old_basis, momentum, second, factor, right_factor, right_basis, scale
):
    vmem = pl.BlockSpec(memory_space=pltpu.VMEM)
    width, channels = kernel.shape
    rows = width // (CORES * DPS)
    side = CELL
    half, single = jnp.bfloat16, jnp.float32
    dma = [pltpu.SemaphoreType.DMA((count,)) for count in SEMS.values()]
    out = jax.ShapeDtypeStruct
    strip = pltpu.VMEM((4, side, channels), half)
    block = (2 * rows + rows // 3, LEAF)
    piece = (rows // DPS, channels)
    return pl.pallas_call(
        lambda *refs: exchange_kernel(scale, *refs),
        out_shape=(
            out(acts.shape, half),
            out(acts.shape, half),
            out((width, channels), single),
            out((width, channels), single),
            out((DPS,) + second.shape, single),
            out((DPS, ZS, CORES) + block, half),
            out((DPS, CORES, (2 * channels + channels // 4) // CORES, LEAF), half),
            out((channels, 2 * channels), single),
            out(factor.shape, single),
            out((6,) + right_factor.shape, single),
        ),
        in_specs=[pl.BlockSpec(memory_space=pltpu.SMEM)] + [vmem] * 9,
        out_specs=(vmem,) * 10,
        scratch_shapes=[
            strip,
            strip,
            strip,
            strip,
            pltpu.VMEM(block, half),
            pltpu.VMEM((ZS, CORES) + block, half),
            pltpu.VMEM((width, LANES), half),
            pltpu.VMEM((DPS,) + piece, single),
            pltpu.VMEM((DPS - 1,) + piece, single),
            pltpu.VMEM((CORES, DPS, ZS) + piece, single),
            pltpu.VMEM((side + 2, 32, channels), single),
            pltpu.VMEM((side * side, width), half),
            pltpu.VMEM((side + 2, 32, channels), single),
            pltpu.VMEM((side, side, channels), single),
            pltpu.VMEM((CORES, DPS, rows, channels), single),
            pltpu.VMEM((DPS, rows, channels), single),
            pltpu.VMEM((DPS, rows, channels), single),
            pltpu.VMEM((DPS - 1, rows, channels), single),
            pltpu.VMEM((ZS, rows // ZS, channels), single),
            pltpu.VMEM((ZS - 1, rows // ZS, channels), single),
            pltpu.VMEM((CORES, DPS, ZS, rows // ZS, channels), single),
            pltpu.VMEM(block, half),
            *dma,
            *dma,
        ],
        compiler_params=pltpu.CompilerParams(
            collective_id=0, has_side_effects=True, vmem_limit_bytes=56 * 1024 * 1024
        ),
        name="exchange",
    )(meta, acts, cots, kernel, old_basis, momentum, second, factor, right_factor, right_basis)


def body_quick(
    activations,
    cotangent,
    kernel,
    turning,
    orient,
    left_factor,
    left_basis,
    right_factor,
    right_basis,
    momentum,
    second_moment,
):
    tiles, dp_count = ZS * CORES, DPS
    tile_vals = activations[:, 0]
    tile_grads = cotangent[:, 0]
    side = tile_vals.shape[1]
    channels = tile_vals.shape[-1]
    flipped = orient[0] >= 4
    width = left_factor.shape[1]
    moment_rows = momentum.shape[0]

    cells = dp_count * tiles * side * side
    result, input_grad, grad, back, seconds, mapped, crossed, grad_both, left_new, right = exchange(
        jnp.concatenate([turning, flipped.astype(jnp.int32)]),
        tile_vals.reshape(side * side, channels),
        tile_grads.reshape(side * side, channels),
        kernel,
        left_basis,
        momentum,
        second_moment.reshape(CORES, moment_rows // CORES, channels),
        left_factor,
        right_factor,
        right_basis,
        1.0 / math.sqrt(cells),
    )
    all_second = seconds.reshape(width, channels)
    outs = finish(
        grad,
        back,
        mapped.reshape((DPS, tiles) + mapped.shape[3:]),
        crossed.reshape(DPS, -1, LEAF),
        grad_both,
        left_new,
        right,
        right_basis,
        all_second,
        result,
        input_grad,
        moment_rows,
    )
    return (outs[0].reshape(activations.shape), outs[1].reshape(cotangent.shape), *outs[2:])


def body(*args):
    tiles = lax.axis_size("tile")
    dp_count = lax.axis_size("dp")
    left_basis = args[6]
    samples = args[0].shape[0]
    sizes = (tiles, dp_count, samples, args[0].shape[2])
    if sizes == (ZS * CORES, DPS, 1, CELL) and left_basis.shape == (144, 288):
        return body_quick(*args)
    return body_plain(*args)


def solution(mesh):
    placed = (
        P(("group", "dp"), "tile", None, None, None),
        P(("group", "dp"), "tile", None, None, None),
        P("group", None),
        P("tile"),
        P("tile", None),
        P(("group", "tile"), None),
        P(("group", "tile"), "dp"),
        P("group", None),
        P("group", None),
        P(("group", "dp"), None),
        P(("group", "dp"), None),
    )
    return jax.shard_map(
        body,
        mesh=mesh,
        in_specs=placed,
        out_specs=(
            P(("group", "dp"), "tile", None, None, None),
            P(("group", "dp"), "tile", None, None, None),
            P("group", None),
            P(("group", "tile"), None),
            P(("group", "tile"), None),
            P("group", None),
            P("group", None),
            P(("group", "dp"), None),
            P(("group", "dp"), None),
            P(("group", "tile"), None),
        ),
        check_vma=False,
    )
```

```python
import math

import jax
import jax.numpy as jnp
from jax import lax
from jax.experimental import pallas as pl
from jax.experimental.pallas import tpu as pltpu
from jax.sharding import PartitionSpec as P

highest = lax.Precision.HIGHEST
epsilon = 1e-08


def edge_strips(values):
    return jnp.stack(
        [values[..., 0, :, :], values[..., :, -1, :], values[..., -1, :, :], values[..., :, 0, :]],
        axis=0,
    )


def cycle_strips(spread):
    return jnp.stack(
        [spread[:, 0, 1:-1], spread[:, 1:-1, -1], spread[:, -1, 1:-1], spread[:, 1:-1, 0]], axis=0
    )


def assemble(tile_vals, borders):
    middle = jnp.concatenate(
        [borders[3][:, :, None, :], tile_vals, borders[1][:, :, None, :]], axis=2
    )
    top_row = jnp.pad(borders[0], ((0, 0), (1, 1), (0, 0)))[:, None]
    bottom_row = jnp.pad(borders[2], ((0, 0), (1, 1), (0, 0)))[:, None]
    return jnp.concatenate([top_row, middle, bottom_row], axis=1)


def tap_patches(padded, side):
    pieces = [
        padded[:, row_off : row_off + side, col_off : col_off + side, :]
        for row_off in range(3)
        for col_off in range(3)
    ]
    joined = jnp.concatenate(pieces, axis=-1)
    return joined.reshape(-1, joined.shape[-1])


def spread_back(flat_grads, kernel, sample_count, side):
    channels = kernel.shape[1]
    summed = jnp.zeros((sample_count, side + 2, side + 2, channels), jnp.float32)
    for tap_index in range(9):
        row_off, col_off = divmod(tap_index, 3)
        weight_tap = kernel[tap_index * channels : (tap_index + 1) * channels]
        contrib = lax.dot_general(
            flat_grads, weight_tap, (((1,), (1,)), ((), ())), preferred_element_type=jnp.float32
        )
        contrib = contrib.reshape(sample_count, side, side, channels)
        summed = summed + jnp.pad(
            contrib, ((0, 0), (row_off, 2 - row_off), (col_off, 2 - col_off), (0, 0))
        )
    return summed


def absorb_rims(interior, incoming):
    result = interior.at[..., 0, :, :].add(incoming[0])
    result = result.at[..., :, -1, :].add(incoming[1])
    result = result.at[..., -1, :, :].add(incoming[2])
    return result.at[..., :, 0, :].add(incoming[3])


def flip_edges(strips, flipped):
    return jnp.where(flipped[:, None, None, None], strips[:, :, ::-1, :], strips)


def pick_gathered(everything, near_tiles, facing, flipped, usable):
    flat = everything.reshape(everything.shape[0] * 4, -1)
    wanted = jnp.where(usable, near_tiles * 4 + facing, -1)
    selector = (lax.broadcasted_iota(jnp.int32, (4, flat.shape[0]), 1) == wanted[:, None]).astype(
        jnp.bfloat16
    )
    picked = jnp.dot(selector, flat, preferred_element_type=jnp.float32).astype(jnp.bfloat16)
    return flip_edges(picked.reshape((4,) + everything.shape[2:]), flipped)


LEAF = 128
SPAN = 384


def split(value):
    high = value.astype(jnp.bfloat16)
    return high, (value - high.astype(jnp.float32)).astype(jnp.bfloat16)


def split_wide(value):
    high = lax.reduce_precision(value, 8, 7)
    return high.astype(jnp.bfloat16), (value - high).astype(jnp.bfloat16)


def dot3(left, right, dims=(((1,), (0,)), ((), ()))):
    def one(a, b):
        return lax.dot_general(a, b, dims, preferred_element_type=jnp.float32)

    return one(left[0], right[0]) + (one(left[0], right[1]) + one(left[1], right[0]))


by_rows = (((1,), (1,)), ((), ()))


def leaf_inverse(block, m_ref, s_ref):
    row = lax.broadcasted_iota(jnp.int32, (LEAF, LEAF), 0)
    col = lax.broadcasted_iota(jnp.int32, (LEAF, LEAF), 1)
    on_diag = row == col
    unit = jnp.where(on_diag, 1.0, 0.0)
    kept = jnp.where(on_diag, block, 0.0)
    across = lax.rsqrt(jnp.sum(kept, axis=0, keepdims=True))
    down = lax.rsqrt(jnp.sum(kept, axis=1, keepdims=True))
    scaled = block * across * down
    m_ref[...] = jnp.where(on_diag, down, jnp.where(row > col, -scaled * across, 0.0))
    pair = split(block)
    rough = m_ref[...].astype(jnp.bfloat16)
    turned = jnp.dot(rough, pair[0], preferred_element_type=jnp.float32).astype(jnp.bfloat16)
    gap = lax.dot_general(turned, rough, by_rows, preferred_element_type=jnp.float32) - unit
    low = jnp.where(row > col, gap, jnp.where(on_diag, 0.5 * gap, 0.0)).astype(jnp.bfloat16)
    m_ref[...] -= jnp.dot(low, rough, preferred_element_type=jnp.float32)

    def more(carry):
        step, error = carry
        return (step < 12) & (error > 1e-4)

    def refine(carry):
        step, _ = carry
        guess = m_ref[...]
        guess_pair = split(guess)
        turned = dot3(guess_pair, pair)
        gap = dot3(split(turned), guess_pair, by_rows) - unit
        error = jnp.max(jnp.abs(gap))
        low = jnp.where(row > col, gap, jnp.where(on_diag, 0.5 * gap, 0.0))
        m_ref[...] = guess - dot3(split(low), guess_pair)
        return step + 1, error

    _, error = lax.while_loop(more, refine, (jnp.int32(0), jnp.float32(1.0)))

    @pl.when(jnp.logical_not(error <= 1e-4))
    def _():
        s_ref[...] = block
        m_ref[...] = unit

        def eliminate(j, carry):
            work = s_ref[...]
            line = s_ref[pl.ds(j, 1), :]
            lane = lax.broadcasted_iota(jnp.int32, (1, LEAF), 1)
            scale = lax.rsqrt(jnp.sum(jnp.where(lane == j, line, 0.0), axis=1, keepdims=True))
            column = jnp.sum(jnp.where(col == j, work, 0.0), axis=1, keepdims=True)
            side = lax.broadcasted_iota(jnp.int32, (LEAF, 1), 0)
            column = jnp.where(side > j, column * scale, 0.0)
            s_ref[...] = work - column * (line * scale)
            mine = m_ref[pl.ds(j, 1), :] * scale
            m_ref[...] = m_ref[...] - column * mine
            m_ref[pl.ds(j, 1), :] = mine
            return carry

        lax.fori_loop(0, LEAF, eliminate, 0)


def factor_kernel(
    gram_ref, side_ref, small_ref, y_ref, small_out_ref, a_ref, uh, ul, uth, utl, yh, yl, m_ref, s_ref
):
    width = gram_ref.shape[1]
    blocks = width // LEAF
    spans = width // SPAN
    leaf_inverse(small_ref[...], m_ref, s_ref)
    small_out_ref[...] = m_ref[...]
    a_ref[...] = gram_ref[...]
    y_ref[...] = side_ref[...]

    def block_step(k, carry):
        k0 = pl.multiple_of(k * LEAF, LEAF)
        leaf_inverse(a_ref[pl.ds(k0, LEAF), pl.ds(k0, LEAF)], m_ref, s_ref)
        inverse = split(m_ref[...])
        for span in range(spans):
            part = slice(span * SPAN, (span + 1) * SPAN)

            @pl.when((span + 1) * SPAN > k0 + LEAF)
            def _():
                value = dot3(inverse, split(a_ref[pl.ds(k0, LEAF), part]))
                uh[:, part], ul[:, part] = split(value)
                uth[part, :], utl[part, :] = split(value.T)

        value = dot3(inverse, split(y_ref[pl.ds(k0, LEAF), :]))
        y_ref[pl.ds(k0, LEAF), :] = value
        yh[...], yl[...] = split(value)

        def row_step(i, inner):
            i0 = pl.multiple_of(i * LEAF, LEAF)
            left = uth[pl.ds(i0, LEAF), :], utl[pl.ds(i0, LEAF), :]
            for span in range(spans):
                part = slice(span * SPAN, (span + 1) * SPAN)

                @pl.when((span + 1) * SPAN > i0)
                def _():
                    a_ref[pl.ds(i0, LEAF), part] -= dot3(left, (uh[:, part], ul[:, part]))

            y_ref[pl.ds(i0, LEAF), :] -= dot3(left, (yh[...], yl[...]))
            return inner

        lax.fori_loop(k + 1, blocks, row_step, 0)
        return carry

    lax.fori_loop(0, blocks, block_step, 0)


def factor_solve(gram, side, small):
    width, columns = side.shape
    vmem = pl.BlockSpec(memory_space=pltpu.VMEM)
    half = jnp.bfloat16
    return pl.pallas_call(
        factor_kernel,
        out_shape=(
            jax.ShapeDtypeStruct(side.shape, jnp.float32),
            jax.ShapeDtypeStruct(small.shape, jnp.float32),
        ),
        in_specs=[vmem] * 3,
        out_specs=(vmem, vmem),
        scratch_shapes=[
            pltpu.VMEM((width, width), jnp.float32),
            pltpu.VMEM((LEAF, width), half),
            pltpu.VMEM((LEAF, width), half),
            pltpu.VMEM((width, LEAF), half),
            pltpu.VMEM((width, LEAF), half),
            pltpu.VMEM((LEAF, columns), half),
            pltpu.VMEM((LEAF, columns), half),
            pltpu.VMEM((LEAF, LEAF), jnp.float32),
            pltpu.VMEM((LEAF, LEAF), jnp.float32),
        ],
        compiler_params=pltpu.CompilerParams(vmem_limit_bytes=40 * 1024 * 1024),
        name="factor_solve",
    )(gram, side, small)


high = lax.Precision.HIGH
tn = (((0,), (0,)), ((), ()))


def sum_kernel(dp_count, tiles, x_ref, out_ref, near, part, far, *sems):
    dp_index = lax.axis_index("dp")
    tile_index = lax.axis_index("tile")
    dp_peers = [lax.rem(dp_index + step, dp_count) for step in range(1, dp_count)]
    tile_peers = [lax.rem(tile_index + step, tiles) for step in range(1, tiles)]
    barrier = pltpu.get_barrier_semaphore()
    for axis, peers in (("dp", dp_peers), ("tile", tile_peers)):
        for peer in peers:
            pl.semaphore_signal(
                barrier, inc=1, device_id={axis: peer}, device_id_type=pl.DeviceIdType.MESH
            )
    pl.semaphore_wait(barrier, dp_count + tiles - 2)

    def exchange(axis, peers, source, target, send, receive):
        copies = [
            pltpu.make_async_remote_copy(
                src_ref=source(peer),
                dst_ref=target(slot),
                send_sem=send.at[slot],
                recv_sem=receive.at[slot],
                device_id={axis: peer},
                device_id_type=pl.DeviceIdType.MESH,
            )
            for slot, peer in enumerate(peers)
        ]
        for copy in copies:
            copy.start()
        for copy in copies:
            copy.wait()

    exchange("dp", dp_peers, lambda peer: x_ref.at[peer], lambda slot: near.at[slot], *sems[0:2])
    total = x_ref[dp_index]
    for slot in range(dp_count - 1):
        total = total + near[slot]
    part[...] = total
    exchange("tile", tile_peers, lambda peer: part.at[peer], lambda slot: far.at[slot], *sems[2:4])
    total = part[tile_index]
    for slot in range(tiles - 1):
        total = total + far[slot]
    out_ref[dp_index, tile_index] = total
    own = out_ref.at[dp_index, tile_index]
    exchange("tile", tile_peers, lambda peer: own, lambda slot: own, *sems[4:6])
    slab = out_ref.at[dp_index]
    exchange("dp", dp_peers, lambda peer: slab, lambda slot: slab, *sems[6:8])


def sum_everywhere(value):
    tiles = lax.axis_size("tile")
    dp_count = lax.axis_size("dp")
    rows, columns = value.shape
    if tiles < 2 or dp_count < 2 or rows % (tiles * dp_count):
        return lax.psum(value, ("tile", "dp"))
    piece = rows // (tiles * dp_count)
    vmem = pl.BlockSpec(memory_space=pltpu.VMEM)
    wide = (dp_count, tiles, piece, columns)
    counts = [dp_count - 1] * 2 + [tiles - 1] * 4 + [dp_count - 1] * 2
    out = pl.pallas_call(
        lambda *refs: sum_kernel(dp_count, tiles, *refs),
        out_shape=jax.ShapeDtypeStruct(wide, jnp.float32),
        in_specs=[vmem],
        out_specs=vmem,
        scratch_shapes=[
            pltpu.VMEM((dp_count - 1, tiles, piece, columns), jnp.float32),
            pltpu.VMEM((tiles, piece, columns), jnp.float32),
            pltpu.VMEM((tiles - 1, piece, columns), jnp.float32),
            *[pltpu.SemaphoreType.DMA((count,)) for count in counts],
        ],
        compiler_params=pltpu.CompilerParams(collective_id=0, has_side_effects=True),
        name="sum_everywhere",
    )(value.reshape(wide))
    return out.reshape(rows, columns)


def body_plain(
    activations,
    cotangent,
    kernel,
    turning,
    orient,
    left_factor,
    left_basis,
    right_factor,
    right_basis,
    momentum,
    second_moment,
):
    tiles = lax.axis_size("tile")
    dp_count = lax.axis_size("dp")
    tile_index = lax.axis_index("tile")
    dp_index = lax.axis_index("dp")
    tile_vals = activations[:, 0]
    tile_grads = cotangent[:, 0]
    sample_count = tile_vals.shape[0]
    side = tile_vals.shape[1]
    channels = tile_vals.shape[-1]
    own_turn = turning[0]
    facing = orient[0] % 4
    flipped = orient[0] >= 4
    heading = (jnp.arange(4, dtype=jnp.int32) + own_turn) % 4
    row_of = tile_index // 4
    col_of = tile_index % 4
    room = jnp.stack([row_of > 0, col_of < 3, row_of < tiles // 4 - 1, col_of > 0])
    usable = (
        jnp.sum(
            jnp.where(
                heading[:, None] == jnp.arange(4, dtype=jnp.int32)[None, :], room[None, :], False
            ),
            axis=1,
        )
        > 0
    )
    offsets = jnp.array([-4, 1, 4, -1], dtype=jnp.int32)
    near_tiles = tile_index + jnp.sum(
        jnp.where(heading[:, None] == jnp.arange(4, dtype=jnp.int32)[None, :], offsets[None, :], 0),
        axis=1,
    )
    strips = edge_strips(tile_vals)
    flat_grads = tile_grads.reshape(-1, channels)
    spread = spread_back(flat_grads, kernel, sample_count, side)
    rim_cells = cycle_strips(spread).astype(jnp.bfloat16)
    everything = lax.all_gather(
        jnp.concatenate([strips, rim_cells], axis=0)[None], "tile", axis=0, tiled=True
    )
    borders = pick_gathered(everything[:, :4], near_tiles, facing, flipped, usable)
    incoming = pick_gathered(everything[:, 4:], near_tiles, facing, flipped, usable)
    padded = assemble(tile_vals, borders)
    columns = tap_patches(padded, side)
    partial_grad = lax.dot_general(
        columns, flat_grads, (((0,), (0,)), ((), ())), preferred_element_type=jnp.float32
    )
    summed_grad = sum_everywhere(partial_grad)
    result = jnp.dot(columns, kernel, preferred_element_type=jnp.float32).astype(jnp.bfloat16)
    result = result.reshape(activations.shape)
    input_grad = absorb_rims(spread[:, 1:-1, 1:-1], incoming.astype(jnp.float32)).astype(
        jnp.bfloat16
    )
    input_grad = input_grad.reshape(cotangent.shape)
    cells = dp_count * sample_count * tiles * side * side
    grad = summed_grad * (1.0 / math.sqrt(cells))
    rows_per, width = left_factor.shape
    row_start = tile_index * rows_per
    moment_rows = momentum.shape[0]
    moment_start = dp_index * moment_rows
    grad_rows = lax.dynamic_slice_in_dim(grad, row_start, rows_per, 0)
    left_new = 0.95 * left_factor + 0.05 * lax.dot_general(
        grad_rows, grad, (((1,), (1,)), ((), ())), precision=high
    )
    basis_rows = lax.all_gather(left_basis, "dp", axis=1, tiled=True)
    basis = lax.all_gather(basis_rows.astype(jnp.bfloat16), "tile", axis=0, tiled=True)
    moments = lax.all_gather(
        jnp.concatenate([momentum, second_moment], axis=1), "dp", axis=0, tiled=True
    )
    all_momentum, all_second = moments[:, :channels], moments[:, channels:]
    back_rows = jnp.dot(basis_rows, all_momentum, precision=highest)
    own_row = row_start + lax.broadcasted_iota(jnp.int32, left_factor.shape, 0)
    own_col = lax.broadcasted_iota(jnp.int32, left_factor.shape, 1)
    diagonal = jnp.sum(jnp.where(own_row == own_col, left_factor, 0.0), axis=1, keepdims=True)
    rest = jnp.broadcast_to(split_wide(diagonal)[1], (rows_per, LEAF))
    factor = lax.all_gather(
        jnp.concatenate(
            [left_factor.astype(jnp.bfloat16), *split_wide(back_rows), rest], axis=1
        ),
        "tile",
        axis=0,
        tiled=True,
    )
    back = factor[:, width : width + channels].astype(jnp.float32) + factor[
        :, width + channels : width + 2 * channels
    ].astype(jnp.float32)
    rest = factor[:, width + 2 * channels : width + 2 * channels + 1]
    factor = factor[:, :width]
    mapped = 0.95 * (
        jnp.dot(factor, basis, preferred_element_type=jnp.float32)
        + rest.astype(jnp.float32) * basis.astype(jnp.float32)
    )
    mapped_gram = lax.dot_general(mapped, mapped, tn, precision=high)
    mapped_back = lax.dot_general(mapped, back, tn, precision=high)
    crossed = sum(
        lax.dot_general(term, basis, tn, preferred_element_type=jnp.float32) for term in split_wide(grad)
    )
    mapped_grad = lax.dot_general(mapped, grad, tn, precision=high)
    grad_gram = lax.dot_general(grad, grad, tn, precision=high)
    grad_back = lax.dot_general(grad, back, tn, precision=high)
    weight = 0.05 * mapped_grad + 0.00125 * lax.dot_general(crossed, grad_gram, tn, precision=high)
    gram = mapped_gram + lax.dot_general(
        jnp.concatenate([weight.T, crossed], axis=0),
        jnp.concatenate([crossed, weight.T], axis=0),
        tn,
        precision=high,
    )
    power_rows = lax.dynamic_slice_in_dim(mapped, row_start, rows_per, 0) + 0.05 * jnp.dot(
        grad_rows, crossed, precision=high
    )
    power_side = jnp.concatenate([mapped_back, mapped_grad], axis=1) + 0.05 * lax.dot_general(
        crossed, jnp.concatenate([grad_back, grad_gram], axis=1), tn, precision=high
    )
    right_new = 0.95 * right_factor + 0.05 * grad_gram
    right_power = jnp.dot(right_new, right_basis, precision=high)
    right_gram = lax.dot_general(right_power, right_power, tn, precision=high)
    solved, right_inverse = factor_solve(
        gram, jnp.concatenate([power_side, power_rows.T], axis=1), right_gram
    )
    turned_momentum = solved[:, :channels]
    turned_grad = solved[:, channels : 2 * channels]
    basis_new = solved[:, 2 * channels :].T
    right_basis_new = lax.dot_general(
        right_power, right_inverse, (((1,), (1,)), ((), ())), precision=high
    )
    right_turn = lax.dot_general(right_basis, right_basis_new, tn, precision=high)
    rotated = jnp.dot(turned_momentum, right_turn, precision=high)
    projected = jnp.dot(turned_grad, right_basis_new, precision=high)
    momentum_all = 0.9 * rotated + 0.1 * projected
    second_all = 0.95 * all_second + 0.05 * projected * projected
    normalized = momentum_all / (jnp.sqrt(second_all) + epsilon)
    momentum_new = lax.dynamic_slice_in_dim(momentum_all, moment_start, moment_rows, 0)
    second_new = lax.dynamic_slice_in_dim(second_all, moment_start, moment_rows, 0)
    update_rows = jnp.dot(basis_new, normalized, precision=high)
    update = lax.dot_general(
        update_rows, right_basis_new, (((1,), (1,)), ((), ())), precision=high
    )
    return (
        result,
        input_grad,
        grad,
        left_new,
        basis_new,
        right_new,
        right_basis_new,
        momentum_new,
        second_new,
        update,
    )


ZS = 4
CORES = 2
DPS = 4
LANES = 384
CELL = 24


def to_device(source, target, send, receive, **device):
    return pltpu.make_async_remote_copy(
        src_ref=source,
        dst_ref=target,
        send_sem=send,
        recv_sem=receive,
        device_id=device,
        device_id_type=pl.DeviceIdType.MESH,
    )


def greet():
    t = lax.axis_index("tile")
    d = lax.axis_index("dp")
    barrier = pltpu.get_barrier_semaphore()
    tiles = ZS * CORES
    for step in range(1, tiles):
        pl.semaphore_signal(
            barrier,
            inc=1,
            device_id={"tile": lax.rem(t + step, tiles)},
            device_id_type=pl.DeviceIdType.MESH,
        )
    for step in range(1, DPS):
        pl.semaphore_signal(
            barrier,
            inc=1,
            device_id={"dp": lax.rem(d + step, DPS)},
            device_id_type=pl.DeviceIdType.MESH,
        )
    pl.semaphore_wait(barrier, tiles + DPS - 2)


class Edges:
    def __init__(self, source, target, send, receive):
        t = lax.axis_index("tile")
        row, col = t // 4, t % 4
        self.rooms = (row > 0, col < 3, row < 1, col > 0)
        self.target = target
        self.copies = []
        for h, step in enumerate((4, 1, 4, 7)):
            back = (h + 2) % 4
            peer = lax.rem(t + step, ZS * CORES)
            self.copies.append(
                to_device(source.at[h], target.at[back], send.at[h], receive.at[back], tile=peer)
            )

    def start(self):
        for h in range(4):

            @pl.when(self.rooms[h])
            def _():
                self.copies[h].start()

            @pl.when(jnp.logical_not(self.rooms[h]))
            def _():
                self.target[h] = jnp.zeros(self.target.shape[1:], self.target.dtype)

    def wait(self):
        for h in range(4):

            @pl.when(self.rooms[h])
            def _():
                self.copies[h].wait_send()
                self.copies[(h + 2) % 4].wait_recv()


def finish_kernel(
    grad_ref,
    back_ref,
    mapped_ref,
    crossed_ref,
    grad_both_ref,
    left_new_ref,
    right_in_ref,
    right_basis_ref,
    second_ref,
    result_ref,
    input_grad_ref,
    result_out,
    input_grad_out,
    grad_out,
    left_out,
    basis_out,
    right_out,
    right_basis_out,
    momentum_out,
    second_out,
    update_out,
    m_ref,
    left_ref,
    right_ref,
    work_ref,
    gram_ref,
    up_ref,
    down_ref,
    y_ref,
    turn_ref,
    aux_ref,
    big_ref,
):
    t = lax.axis_index("tile")
    d = lax.axis_index("dp")
    width, channels = grad_ref.shape
    blocks = width // LEAF
    rows_per = left_new_ref.shape[0]
    moment_rows = momentum_out.shape[0]
    wide = work_ref.shape[1]
    own_rows = pl.ds(pl.multiple_of(t * rows_per, 16), rows_per)

    result_out[...] = result_ref[...]
    input_grad_out[...] = input_grad_ref[...]
    extra = LEAF // 4

    lane = lax.broadcasted_iota(jnp.int32, (1, LEAF), 1)

    def tile_of(middle, shared, folded, j):
        group, spot = divmod(j, 2)
        if spot:
            return middle(group)
        if group == 0:
            return shared(0)
        value = jnp.where(lane >= extra * (group - 1), folded(group - 1), shared(group - 1))
        return jnp.where(lane >= extra * group, shared(group), value) if group < DPS else value

    def stack(g, begin, end):
        blocks_of = [mapped_ref[g, tile, begin:end, :] for tile in range(mapped_ref.shape[1])]
        return jnp.concatenate(blocks_of, axis=0).astype(jnp.float32)

    def folded_rows(g):
        return jnp.concatenate(
            [
                unfold(mapped_ref[g, tile, 2 * rows_per :, :].astype(jnp.float32), 3)
                for tile in range(mapped_ref.shape[1])
            ],
            axis=0,
        )

    for j in range(blocks):
        at = slice(j * LEAF, (j + 1) * LEAF)
        value = tile_of(
            lambda g: stack(g, 0, rows_per), lambda g: stack(g, rows_per, 2 * rows_per), folded_rows, j
        ).astype(jnp.bfloat16)
        m_ref[:, at] = value
        left_ref[at, :width] = value.T
    crossed = jnp.concatenate(
        [
            tile_of(
                lambda g: crossed_ref[g, :channels, :].astype(jnp.float32),
                lambda g: crossed_ref[g, channels : 2 * channels, :].astype(jnp.float32),
                lambda g: unfold(crossed_ref[g, 2 * channels :, :].astype(jnp.float32), 4),
                j,
            )
            for j in range(blocks)
        ],
        axis=1,
    )
    grad = grad_ref[...]
    grad_out[...] = grad
    grad_t = grad.T
    both = jnp.concatenate([back_ref[...], grad], axis=1)
    both_pair = split(both)
    grad_both = grad_both_ref[...]
    grad_gram = grad_both[:, channels:]
    grad_rows = grad_ref[own_rows, :]
    left_out[...] = left_new_ref[...]
    right_out[...] = right_in_ref[0]
    right_basis_out[...] = right_in_ref[4]
    turn_ref[...] = right_in_ref[5]

    grad_m = product(jnp.concatenate(split(grad_t), axis=0), m_ref[...])
    weight = 0.05 * (grad_m[:channels] + grad_m[channels:]) + 0.00125 * matmul(grad_gram, crossed)
    pair = jnp.concatenate([weight, crossed], axis=0)
    pair_t = pair.T
    left_ref[:, width:] = wide_left(split(pair_t))
    right_ref[...] = wide_right(split(jnp.concatenate([crossed, weight], axis=0)))
    for j in range(0, blocks, 2):
        end = min(j + 2, blocks) * LEAF
        at = slice(j * LEAF, end)
        value = product(left_ref[:end, :width], m_ref[:, at]) + product(
            left_ref[:end, width:], right_ref[:, at]
        )
        work_ref[:end, at] = value
        gram_ref[:end, at] = value
    m_both = product(left_ref[:, :width], both_pair[0]) + product(left_ref[:, :width], both_pair[1])
    crossed_t = pair_t[:, channels:]
    work_ref[:, width : width + 2 * channels] = m_both + 0.05 * matmul(crossed_t, grad_both)
    power_rows = m_ref[own_rows, :].astype(jnp.float32) + 0.05 * matmul(grad_rows, crossed)
    padded = jnp.concatenate(
        [power_rows, jnp.zeros((2 * LEAF - rows_per, width), jnp.float32)], axis=0
    )
    work_ref[:, width + 2 * channels :] = padded.T
    gram_ref[:, width:] = work_ref[:, width:]

    worst = right_in_ref[3]
    for k in range(blocks):
        at = slice(k * LEAF, (k + 1) * LEAF)
        inverse, gap = quick_leaf(work_ref[at, at])
        worst = jnp.maximum(worst, gap)
        value = product(wide_left(split(inverse)), wide_right(split(work_ref[at, (k + 1) * LEAF :])))
        y_ref[at, :] = value[:, width - (k + 1) * LEAF :]
        if k == blocks - 1:
            break
        start = (k + 1) * LEAF
        up_ref[:, start:] = wide_right(split(value))
        down_ref[start:, :] = wide_left(split(value[:, : width - start].T))
        edges = list(range(start, width, 2 * LEAF))
        spans = [(a, min(a + 2 * LEAF, width)) for a in edges] + [
            (a, a + 2 * LEAF) for a in range(width, wide, 2 * LEAF)
        ]
        for a, b in spans:
            bottom = min(b, width)
            work_ref[start:bottom, a:b] -= product(down_ref[start:bottom, :], up_ref[:, a:b])

    @pl.when(jnp.logical_not(jnp.max(worst) <= 0.03))
    def _():
        leaf_inverse(right_in_ref[2], big_ref, aux_ref)
        turned = matmul_rows(right_in_ref[1], big_ref[...])
        right_basis_out[...] = turned
        turn_ref[...] = matmul(right_basis_ref[...].T, turned)
        work_ref[...] = gram_ref[...]

        def block_step(k, carry):
            k0 = pl.multiple_of(k * LEAF, LEAF)
            leaf_inverse(work_ref[pl.ds(k0, LEAF), pl.ds(k0, LEAF)], big_ref, aux_ref)
            inverse = wide_left(split(big_ref[...]))
            for a in range(0, wide, LEAF):
                value = product(inverse, wide_right(split(work_ref[pl.ds(k0, LEAF), a : a + LEAF])))
                up_ref[:, a : a + LEAF] = wide_right(split(value))
                if a < width:
                    down_ref[a : a + LEAF, :] = wide_left(split(value.T))
                else:
                    y_ref[pl.ds(k0, LEAF), a - width : a - width + LEAF] = value

            def row_step(i, inner):
                i0 = pl.multiple_of(i * LEAF, LEAF)
                left = down_ref[pl.ds(i0, LEAF), :]
                for a in range(0, wide, LEAF):

                    @pl.when(a + LEAF > i0)
                    def _():
                        work_ref[pl.ds(i0, LEAF), a : a + LEAF] -= product(
                            left, up_ref[:, a : a + LEAF]
                        )

                return inner

            lax.fori_loop(k + 1, blocks, row_step, 0)
            return carry

        lax.fori_loop(0, blocks, block_step, 0)

    right_basis_new = right_basis_out[...]
    right_turn = turn_ref[...]
    solved = y_ref[...]
    rotated = matmul(solved[:, :channels], right_turn)
    projected = matmul(solved[:, channels : 2 * channels], right_basis_new)
    basis_new = solved[:, 2 * channels :].T[:rows_per]
    basis_out[...] = basis_new
    momentum = 0.9 * rotated + 0.1 * projected
    second = 0.95 * second_ref[...] + 0.05 * projected * projected
    up = momentum / (jnp.sqrt(second) + epsilon)
    update_rows = matmul(basis_new, up)
    update_out[...] = matmul_rows(update_rows, right_basis_new)
    y_ref[:, :channels] = momentum
    y_ref[:, channels : 2 * channels] = second
    own = pl.ds(pl.multiple_of(d * moment_rows, 8), moment_rows)
    momentum_out[...] = y_ref[own, :channels]
    second_out[...] = y_ref[own, channels : 2 * channels]


def finish(
    grad, back, mapped, crossed, grad_both, left_new, right, right_basis, second, result, input_grad, moment_rows
):
    vmem = pl.BlockSpec(memory_space=pltpu.VMEM)
    width, channels = grad.shape
    rows_per = left_new.shape[0]
    wide = width + 2 * channels + 2 * LEAF
    half = jnp.bfloat16
    single = jnp.float32
    square = pltpu.VMEM((LEAF, LEAF), single)
    shapes = [
        left_new.shape,
        left_new.shape,
        right_basis.shape,
        right_basis.shape,
        (moment_rows, channels),
        (moment_rows, channels),
        (rows_per, channels),
    ]
    return pl.pallas_call(
        finish_kernel,
        out_shape=(
            jax.ShapeDtypeStruct(result.shape, half),
            jax.ShapeDtypeStruct(input_grad.shape, half),
            jax.ShapeDtypeStruct(grad.shape, single),
            *(jax.ShapeDtypeStruct(shape, single) for shape in shapes),
        ),
        in_specs=[vmem] * 11,
        out_specs=(vmem,) * 10,
        scratch_shapes=[
            pltpu.VMEM((width, width), half),
            pltpu.VMEM((width, width + 6 * channels), half),
            pltpu.VMEM((6 * channels, width), half),
            pltpu.VMEM((width, wide), single),
            pltpu.VMEM((width, wide), single),
            pltpu.VMEM((3 * LEAF, wide), half),
            pltpu.VMEM((width, 3 * LEAF), half),
            pltpu.VMEM((width, wide - width), single),
            square,
            square,
            square,
        ],
        compiler_params=pltpu.CompilerParams(vmem_limit_bytes=56 * 1024 * 1024),
        name="finish",
    )(
        grad, back, mapped, crossed, grad_both, left_new, right, right_basis, second, result, input_grad
    )


def wide_left(pair, axis=1):
    return jnp.concatenate([pair[0], pair[0], pair[1]], axis=axis)


def wide_right(pair, axis=0):
    return jnp.concatenate([pair[0], pair[1], pair[0]], axis=axis)


plain = (((1,), (0,)), ((), ()))


def product(left, right):
    return lax.dot_general(left, right, plain, preferred_element_type=jnp.float32)


def product_rows(left, right):
    return lax.dot_general(left, right, by_rows, preferred_element_type=jnp.float32)


def matmul(left, right):
    return product(wide_left(split(left)), wide_right(split(right)))


def matmul_rows(left, right):
    return product_rows(wide_left(split(left)), wide_right(split(right), 1))


def quick_leaf(block, cheap=2):
    row = lax.broadcasted_iota(jnp.int32, (LEAF, LEAF), 0)
    col = lax.broadcasted_iota(jnp.int32, (LEAF, LEAF), 1)
    on_diag = row == col
    below = row > col
    unit = jnp.where(on_diag, 1.0, 0.0)
    kept = jnp.where(on_diag, block, 0.0)
    across = lax.rsqrt(jnp.sum(kept, axis=0, keepdims=True))
    down = lax.rsqrt(jnp.sum(kept, axis=1, keepdims=True))

    def lower(gap):
        return jnp.where(below, gap, jnp.where(on_diag, 0.5 * gap, 0.0)).astype(jnp.bfloat16)

    high_part, low_part = split(block)
    guess = jnp.where(on_diag, down, jnp.where(below, -block * (across * across) * down, 0.0))
    for _ in range(cheap):
        rough = guess.astype(jnp.bfloat16)
        turned = product(rough, high_part).astype(jnp.bfloat16)
        gap = product_rows(turned, rough) - unit
        guess = rough.astype(jnp.float32) - product(lower(gap), rough)
    rough = guess.astype(jnp.bfloat16)
    twice = jnp.concatenate([rough, rough], axis=1)
    turned = product(twice, jnp.concatenate([high_part, low_part], axis=0))
    gap = product_rows(jnp.concatenate(split(turned), axis=1), twice) - unit
    return rough.astype(jnp.float32) - product(lower(gap), rough), jnp.abs(gap)


def fold(value, parts):
    step = LEAF // 4
    rows = value.shape[0] // parts
    total = value[:rows]
    for i in range(1, parts):
        total = total + pltpu.roll(value[i * rows : (i + 1) * rows], step * i, 1)
    return total


def unfold(value, parts):
    step = LEAF // 4
    return jnp.concatenate(
        [value] + [pltpu.roll(value, LEAF - step * i, 1) for i in range(1, parts)], axis=0
    )


SEMS = {
    "edge": 4,
    "rim": 4,
    "basis_z": 3,
    "basis_sib": 4,
    "back_sum": 3,
    "back_z": 3,
    "back_dp": 3,
    "back_sib": 4,
    "second_dp": 3,
    "second_sib": 3,
    "swap": 1,
    "grad_sum": 3,
    "grad_zsum": 3,
    "grad_z": 3,
    "grad_dp": 3,
    "grad_sib": 4,
    "map_z": 3,
    "map_x": 4,
    "map_y": 4,
    "map_far": 8,
    "map_sib": 16,
    "cross_dp": 3,
    "cross_sib": 3,
}
CUT = 176


def exchange_kernel(
    grad_scale,
    turning_ref,
    orient_ref,
    act_ref,
    cot_ref,
    kernel_ref,
    basis_in_ref,
    momentum_ref,
    second_ref,
    factor_ref,
    right_factor_ref,
    right_basis_ref,
    result_ref,
    input_grad_ref,
    grad_ref,
    back_ref,
    seconds_ref,
    all_ref,
    crossed_ref,
    grad_both_ref,
    left_ref,
    right_ref,
    strips,
    borders,
    rims,
    incoming,
    block_ref,
    basis,
    columns_ref,
    back_in_ref,
    back_near,
    back_all,
    padded,
    patches,
    spread,
    inner,
    partial,
    near,
    half,
    dp_in,
    pieces,
    z_in,
    grad_all,
    own_map,
    *sems,
):
    count = len(SEMS)
    send = dict(zip(SEMS, sems[:count]))
    receive = dict(zip(SEMS, sems[count:]))
    t = lax.axis_index("tile")
    d = lax.axis_index("dp")
    z, c = t // CORES, t % CORES
    sibling = t + 1 - 2 * c
    x_peer = d + 1 - 2 * (d % 2)
    y_peer = lax.rem(d + 2, DPS)
    far_peer = lax.rem(x_peer + 2, DPS)
    rest = range(1, ZS)
    z_peers = [lax.rem(t + CORES * k, ZS * CORES) for k in range(ZS)]
    z_from = [lax.rem(z + ZS - k, ZS) for k in range(ZS)]
    z_to = [lax.rem(z + k, ZS) for k in range(ZS)]
    d_to = [lax.rem(d + j, DPS) for j in range(DPS)]
    d_from = [lax.rem(d + DPS - j, DPS) for j in range(DPS)]
    side = input_grad_ref.shape[0] // CELL
    channels = grad_ref.shape[1]
    width = grad_ref.shape[0]
    pending = []

    def copy(name, index, source, target, **device):
        made = to_device(source, target, send[name].at[index], receive[name].at[index], **device)
        pending.append(made)
        return made

    def start(copies):
        for made in copies:
            made.start()

    def arrive(copies):
        for made in copies:
            made.wait_recv()

    def z_group(name, source, target):
        return [copy(name, k - 1, source(k), target(k), tile=z_peers[k]) for k in rest]

    def dp_group(name, source, target):
        return [copy(name, j - 1, source(j), target(j), dp=d_to[j]) for j in rest]

    part = basis_in_ref.shape[1]
    rows_per = basis_in_ref.shape[0]
    extra = part % LEAF
    old_basis = basis_in_ref[...]
    shifted = jnp.zeros((rows_per, LANES), jnp.float32)
    for slot in range(DPS):
        pieces_of = [old_basis, jnp.zeros((rows_per, LANES - part - extra * slot), jnp.float32)]
        if slot:
            pieces_of.insert(0, jnp.zeros((rows_per, extra * slot), jnp.float32))
        pieces_of = [p for p in pieces_of if p.shape[1]]
        shifted = jnp.where(d == slot, jnp.concatenate(pieces_of, axis=1), shifted)
    lane = lax.broadcasted_iota(jnp.int32, (1, LEAF), 1)
    window = (lane >= extra * d) & (lane < extra * (d + 1))
    first_tile, last_tile = shifted[:, :LEAF], shifted[:, 2 * LEAF :]
    block_ref[...] = jnp.concatenate(
        [
            shifted[:, LEAF : 2 * LEAF],
            jnp.where(lane >= extra * d, first_tile, last_tile),
            fold(jnp.where(window, last_tile, 0.0), 3),
        ],
        axis=0,
    ).astype(jnp.bfloat16)
    greet()
    own_basis = basis.at[z, c]
    basis_z = z_group("basis_z", lambda k: block_ref, lambda k: own_basis)
    basis_sib = [
        copy(
            "basis_sib",
            k,
            block_ref if k == 0 else basis.at[z_from[k], c],
            basis.at[z_from[k], c],
            tile=sibling,
        )
        for k in range(ZS)
    ]
    back_sum = dp_group("back_sum", lambda j: back_in_ref.at[d_to[j]], lambda j: back_near.at[j - 1])
    second_dp = dp_group("second_dp", lambda j: second_ref.at[c], lambda j: seconds_ref.at[d, c])
    start(basis_z)
    start(basis_sib[:1])

    turn = turning_ref[0]
    padded[...] = jnp.zeros(padded.shape, jnp.float32)
    padded[1 : side + 1, 1 : side + 1, :] = act_ref[...].astype(jnp.float32).reshape(side, side, channels)
    line = lax.broadcasted_iota(jnp.int32, (side, side), 0)
    place = lax.broadcasted_iota(jnp.int32, (side, side), 1)
    straight = jnp.where(line == place, 1.0, 0.0)
    crosswise = jnp.where(line + place == side - 1, 1.0, 0.0)
    orders = [
        jnp.where(orient_ref[0, e] >= 4, crosswise, straight).astype(jnp.bfloat16) for e in range(4)
    ]

    def fill(target, lines):
        aligned = [product(orders[e], lines[e].astype(jnp.bfloat16)) for e in range(4)]
        for h in range(4):
            wanted = lax.rem(h + 4 - turn, 4)
            target[h] = sum(jnp.where(wanted == e, aligned[e], 0.0) for e in range(4)).astype(
                jnp.bfloat16
            )

    fill(
        strips,
        [
            padded[1, 1 : side + 1, :],
            padded[1 : side + 1, side, :],
            padded[side, 1 : side + 1, :],
            padded[1 : side + 1, 1, :],
        ],
    )
    edges = Edges(strips, borders, send["edge"], receive["edge"])
    edges.start()
    old_pair, moment_pair = split(old_basis), split(momentum_ref[...])
    value = product(old_pair[0], moment_pair[0]) + (
        product(old_pair[0], moment_pair[1]) + product(old_pair[1], moment_pair[0])
    )
    piece = rows_per // DPS
    for dp in range(DPS):
        back_in_ref[dp] = value[dp * piece : (dp + 1) * piece]
    start(back_sum)
    start(second_dp)
    own_basis[...] = block_ref[...]
    seconds_ref[d] = second_ref[...]

    cot = cot_ref[...]
    cot_t = jnp.concatenate(
        [cot.astype(jnp.float32), jnp.zeros((LEAF - side * side % LEAF, channels), jnp.float32)], axis=0
    ).T[:, : side * side].astype(jnp.bfloat16)

    def pick(ref, wanted):
        return sum(
            jnp.where(wanted == h, ref[h].astype(jnp.float32), 0.0) for h in range(4)
        )

    edges.wait()
    border = [pick(borders, lax.rem(turn + e, 4)) for e in range(4)]
    padded[0, 1 : side + 1, :] = border[0]
    padded[1 : side + 1, side + 1, :] = border[1]
    padded[side + 1, 1 : side + 1, :] = border[2]
    padded[1 : side + 1, 0, :] = border[3]
    for col in range(3):
        lines = padded[:, col : col + side, :].reshape((side + 2) * side, channels)
        for row in range(3):
            at = (3 * row + col) * channels
            patches[:, at : at + channels] = lines[row * side : row * side + side * side].astype(
                jnp.bfloat16
            )
    turned = product(cot_t, patches[...])
    block = partial.shape[2]
    value = turned.T
    for core in range(CORES):
        for dp in range(DPS):
            at = (core * DPS + dp) * block
            partial[core, dp] = value[at : at + block]
    swap = copy("swap", 0, partial.at[1 - c], near, tile=sibling)
    swap.start()

    arrive(back_sum)
    total = back_in_ref[d]
    for slot in range(DPS - 1):
        total = total + back_near[slot]
    back_all[c, d, z] = total
    mine = back_all.at[c, d, z]
    back_z = z_group("back_z", lambda k: mine, lambda k: mine)
    start(back_z)

    swap.wait_recv()
    half[...] = partial[c] + near[...]
    grad_sum = dp_group("grad_sum", lambda j: half.at[d_to[j]], lambda j: dp_in.at[j - 1])
    start(grad_sum)

    for k in rest:
        basis_z[k - 1].wait_recv()
        basis_sib[k].start()
    arrive(back_z)
    slab = back_all.at[c, d]
    back_dp = dp_group("back_dp", lambda j: slab, lambda j: slab)
    start(back_dp)

    arrive(basis_sib)
    for at_z in range(ZS):
        for core in range(CORES):
            at = (at_z * CORES + core) * rows_per
            at = slice(at, at + rows_per)
            columns_ref[at, :LEAF] = basis[at_z, core, :rows_per]
            columns_ref[at, LEAF : 2 * LEAF] = basis[at_z, core, rows_per : 2 * rows_per]
            columns_ref[at, 2 * LEAF :] = unfold(
                basis[at_z, core, 2 * rows_per :].astype(jnp.float32), 3
            ).astype(jnp.bfloat16)
    columns = columns_ref[...]
    factor = split(factor_ref[...])
    mapped = 0.95 * (product(factor[0], columns) + product(factor[1], columns))
    mapped = jnp.concatenate(
        [
            mapped[:, :LEAF],
            mapped[:, LEAF : 2 * LEAF],
            fold(jnp.where(window, mapped[:, 2 * LEAF :], 0.0), 3),
        ],
        axis=0,
    ).astype(jnp.bfloat16)
    own_map[...] = mapped
    all_ref[d, z, c] = mapped

    def spot_of(dp, k):
        return all_ref.at[dp, z_from[k], c]

    def own_spot(k):
        return own_map if k == 0 else spot_of(d, k)

    map_z = z_group("map_z", lambda k: own_map, lambda k: spot_of(d, 0))
    map_x = [copy("map_x", k, own_spot(k), spot_of(d, k), dp=x_peer) for k in range(ZS)]
    map_y = [copy("map_y", k, own_spot(k), spot_of(d, k), dp=y_peer) for k in range(ZS)]
    map_sib = [copy("map_sib", k, own_spot(k), spot_of(d, k), tile=sibling) for k in range(ZS)]
    upper, lower = pl.ds(0, CUT), pl.ds(CUT, own_map.shape[0] - CUT)

    def relay(k):
        up = spot_of(x_peer, k).at[upper]
        down = spot_of(y_peer, k).at[lower]
        return [
            copy("map_far", 2 * k, up, up, dp=y_peer),
            copy("map_far", 2 * k + 1, down, down, dp=x_peer),
        ]

    relays = [relay(k) for k in range(ZS)]

    def relay_arrive(k):
        arrive(relays[k])

    start(map_z)
    start([map_x[0], map_y[0], map_sib[0]])

    arrive(grad_sum)
    total = half[d]
    for slot in range(DPS - 1):
        total = total + dp_in[slot]
    for k in range(ZS):
        pieces[k] = total[k * piece : (k + 1) * piece]
    grad_zsum = z_group("grad_zsum", lambda k: pieces.at[z_to[k]], lambda k: z_in.at[k - 1])
    start(grad_zsum)

    arrive(grad_zsum)
    total = pieces[z]
    for slot in range(ZS - 1):
        total = total + z_in[slot]
    grad_all[c, d, z] = total
    own_piece = grad_all.at[c, d, z]
    grad_z = z_group("grad_z", lambda k: own_piece, lambda k: own_piece)
    start(grad_z)

    def slabs(ref, name):
        spots = [ref.at[c, d_from[j]] for j in range(DPS)]
        return [copy(name, j, spots[j], spots[j], tile=sibling) for j in range(DPS)]

    arrive(back_dp)
    back_sib = slabs(back_all, "back_sib")
    start(back_sib)
    second_sib = []
    for j in rest:
        spot = seconds_ref.at[d_from[j], c]
        second_sib.append(copy("second_sib", j - 1, spot, spot, tile=sibling))
    arrive(second_dp)
    start(second_sib)

    arrive(grad_z)
    grad_slab = grad_all.at[c, d]
    grad_dp = dp_group("grad_dp", lambda j: grad_slab, lambda j: grad_slab)
    start(grad_dp)

    for k in rest:
        map_z[k - 1].wait_recv()
        start([map_x[k], map_y[k], map_sib[k]])

    terms = product_rows(cot, kernel_ref[...])
    spread[...] = jnp.zeros(spread.shape, jnp.float32)
    for col in range(3):
        stack = None
        for row in range(3):
            at = (3 * row + col) * channels
            term = terms[:, at : at + channels]
            parts = [term]
            if row:
                parts.insert(0, jnp.zeros((row * side, channels), jnp.float32))
            if row < 2:
                parts.append(jnp.zeros(((2 - row) * side, channels), jnp.float32))
            term = jnp.concatenate(parts, axis=0)
            stack = term if stack is None else stack + term
        spread[:, col : col + side, :] += stack.reshape(side + 2, side, channels)
    fill(
        rims,
        [
            spread[0, 1 : side + 1, :],
            spread[1 : side + 1, side + 1, :],
            spread[side + 1, 1 : side + 1, :],
            spread[1 : side + 1, 0, :],
        ],
    )
    rim_edges = Edges(rims, incoming, send["rim"], receive["rim"])
    rim_edges.start()

    def far_sib(j, k):
        spot = spot_of((x_peer, y_peer, far_peer)[j], k)
        return copy("map_sib", ZS * (j + 1) + k, spot, spot, tile=sibling)

    map_far = [[far_sib(j, k) for k in range(ZS)] for j in range(3)]

    def pass_on(k):
        arrive([map_x[k], map_y[k]])
        start(relays[k])
        start([map_far[0][k], map_far[1][k]])

    pass_on(0)
    result_ref[...] = product(patches[...], kernel_ref[...]).astype(jnp.bfloat16)
    pass_on(1)

    grad_sib = slabs(grad_all, "grad_sib")
    grad_sib[0].start()
    for j in rest:
        grad_dp[j - 1].wait_recv()
        grad_sib[j].start()
    arrive(grad_sib)
    for core in range(CORES):
        for dp in range(DPS):
            for at_z in range(ZS):
                at = ((core * DPS + dp) * ZS + at_z) * piece
                grad_ref[at : at + piece] = grad_all[core, dp, at_z]
    grad = grad_ref[...] * grad_scale
    grad_ref[...] = grad
    grad_t = grad.T
    high_part, low_part = split(grad_t)
    crossed = product(high_part, columns) + product(low_part, columns)
    crossed = jnp.concatenate(
        [
            crossed[:, :LEAF],
            crossed[:, LEAF : 2 * LEAF],
            fold(jnp.where(window, crossed[:, 2 * LEAF :], 0.0), 4),
        ],
        axis=0,
    ).astype(jnp.bfloat16)
    halves = crossed.shape[0] // CORES
    for core in range(CORES):
        crossed_ref[d, core] = crossed[core * halves : (core + 1) * halves]
    own_cross = crossed_ref.at[d, c]
    cross_dp = dp_group("cross_dp", lambda j: own_cross, lambda j: own_cross)
    start(cross_dp)

    pass_on(2)
    arrive(back_sib)
    for core in range(CORES):
        for dp in range(DPS):
            for at_z in range(ZS):
                to = ((at_z * CORES + core) * DPS + dp) * piece
                back_ref[to : to + piece] = back_all[core, dp, at_z]

    both = jnp.concatenate([back_ref[...], grad], axis=1)
    grad_both = product(wide_left(split(grad_t)), wide_right(split(both)))
    grad_both_ref[...] = grad_both
    own_rows = pl.ds(pl.multiple_of(t * rows_per, 16), rows_per)
    left_ref[...] = 0.95 * factor_ref[...] + 0.05 * matmul_rows(grad_ref[own_rows, :], grad)
    right_new = 0.95 * right_factor_ref[...] + 0.05 * grad_both[:, channels:]
    right_basis = right_basis_ref[...]
    right_power = matmul(right_new, right_basis)
    right_gram = matmul(right_power.T, right_power)
    pass_on(3)
    right_inverse, right_gap = quick_leaf(right_gram, 4)
    right_basis_new = matmul_rows(right_power, right_inverse)
    right_turn = matmul(right_basis.T, right_basis_new)
    for slot, value in enumerate(
        (right_new, right_power, right_gram, right_gap, right_basis_new, right_turn)
    ):
        right_ref[slot] = value

    for k in range(ZS):
        relay_arrive(k)
        map_far[2][k].start()

    cross_sib = []
    for j in rest:
        spot = crossed_ref.at[d_from[j], c]
        cross_dp[j - 1].wait_recv()
        made = copy("cross_sib", j - 1, spot, spot, tile=sibling)
        made.start()
        cross_sib.append(made)
    rim_edges.wait()
    value = [pick(incoming, lax.rem(turn + e, 4)) for e in range(4)]
    inner[...] = spread[1 : side + 1, 1 : side + 1, :]
    inner[0, :, :] += value[0]
    inner[:, side - 1, :] += value[1]
    inner[side - 1, :, :] += value[2]
    inner[:, 0, :] += value[3]
    input_grad_ref[...] = inner[...].reshape(side * side, channels).astype(jnp.bfloat16)

    arrive(second_sib)
    arrive(map_sib)
    for group in map_far:
        arrive(group)
    arrive(cross_sib)
    for made in pending:
        made.wait_send()


def exchange(
    turning, orient, acts, cots, kernel, old_basis, momentum, second, factor, right_factor, right_basis, scale
):
    vmem = pl.BlockSpec(memory_space=pltpu.VMEM)
    width, channels = kernel.shape
    rows = width // (CORES * DPS)
    side = CELL
    half, single = jnp.bfloat16, jnp.float32
    dma = [pltpu.SemaphoreType.DMA((count,)) for count in SEMS.values()]
    out = jax.ShapeDtypeStruct
    strip = pltpu.VMEM((4, side, channels), half)
    block = (2 * rows + rows // 3, LEAF)
    piece = (rows // DPS, channels)
    return pl.pallas_call(
        lambda *refs: exchange_kernel(scale, *refs),
        out_shape=(
            out(acts.shape, half),
            out(acts.shape, half),
            out((width, channels), single),
            out((width, channels), single),
            out((DPS,) + second.shape, single),
            out((DPS, ZS, CORES) + block, half),
            out((DPS, CORES, (2 * channels + channels // 4) // CORES, LEAF), half),
            out((channels, 2 * channels), single),
            out(factor.shape, single),
            out((6,) + right_factor.shape, single),
        ),
        in_specs=[pl.BlockSpec(memory_space=pltpu.SMEM)] * 2 + [vmem] * 9,
        out_specs=(vmem,) * 10,
        scratch_shapes=[
            strip,
            strip,
            strip,
            strip,
            pltpu.VMEM(block, half),
            pltpu.VMEM((ZS, CORES) + block, half),
            pltpu.VMEM((width, LANES), half),
            pltpu.VMEM((DPS,) + piece, single),
            pltpu.VMEM((DPS - 1,) + piece, single),
            pltpu.VMEM((CORES, DPS, ZS) + piece, single),
            pltpu.VMEM((side + 2, 32, channels), single),
            pltpu.VMEM((side * side, width), half),
            pltpu.VMEM((side + 2, 32, channels), single),
            pltpu.VMEM((side, side, channels), single),
            pltpu.VMEM((CORES, DPS, rows, channels), single),
            pltpu.VMEM((DPS, rows, channels), single),
            pltpu.VMEM((DPS, rows, channels), single),
            pltpu.VMEM((DPS - 1, rows, channels), single),
            pltpu.VMEM((ZS, rows // ZS, channels), single),
            pltpu.VMEM((ZS - 1, rows // ZS, channels), single),
            pltpu.VMEM((CORES, DPS, ZS, rows // ZS, channels), single),
            pltpu.VMEM(block, half),
            *dma,
            *dma,
        ],
        compiler_params=pltpu.CompilerParams(
            collective_id=0, has_side_effects=True, vmem_limit_bytes=56 * 1024 * 1024
        ),
        name="exchange",
    )(turning, orient, acts, cots, kernel, old_basis, momentum, second, factor, right_factor, right_basis)


def body_quick(
    activations,
    cotangent,
    kernel,
    turning,
    orient,
    left_factor,
    left_basis,
    right_factor,
    right_basis,
    momentum,
    second_moment,
):
    tiles, dp_count = ZS * CORES, DPS
    tile_vals = activations[:, 0]
    tile_grads = cotangent[:, 0]
    side = tile_vals.shape[1]
    channels = tile_vals.shape[-1]
    width = left_factor.shape[1]
    moment_rows = momentum.shape[0]

    cells = dp_count * tiles * side * side
    result, input_grad, grad, back, seconds, mapped, crossed, grad_both, left_new, right = exchange(
        turning,
        orient,
        tile_vals.reshape(side * side, channels),
        tile_grads.reshape(side * side, channels),
        kernel,
        left_basis,
        momentum,
        second_moment.reshape(CORES, moment_rows // CORES, channels),
        left_factor,
        right_factor,
        right_basis,
        1.0 / math.sqrt(cells),
    )
    all_second = seconds.reshape(width, channels)
    outs = finish(
        grad,
        back,
        mapped.reshape((DPS, tiles) + mapped.shape[3:]),
        crossed.reshape(DPS, -1, LEAF),
        grad_both,
        left_new,
        right,
        right_basis,
        all_second,
        result,
        input_grad,
        moment_rows,
    )
    return (outs[0].reshape(activations.shape), outs[1].reshape(cotangent.shape), *outs[2:])


def body(*args):
    tiles = lax.axis_size("tile")
    dp_count = lax.axis_size("dp")
    left_basis = args[6]
    samples = args[0].shape[0]
    sizes = (tiles, dp_count, samples, args[0].shape[2])
    if sizes == (ZS * CORES, DPS, 1, CELL) and left_basis.shape == (144, 288):
        return body_quick(*args)
    return body_plain(*args)


def solution(mesh):
    placed = (
        P(("group", "dp"), "tile", None, None, None),
        P(("group", "dp"), "tile", None, None, None),
        P("group", None),
        P("tile"),
        P("tile", None),
        P(("group", "tile"), None),
        P(("group", "tile"), "dp"),
        P("group", None),
        P("group", None),
        P(("group", "dp"), None),
        P(("group", "dp"), None),
    )
    return jax.shard_map(
        body,
        mesh=mesh,
        in_specs=placed,
        out_specs=(
            P(("group", "dp"), "tile", None, None, None),
            P(("group", "dp"), "tile", None, None, None),
            P("group", None),
            P(("group", "tile"), None),
            P(("group", "tile"), None),
            P("group", None),
            P("group", None),
            P(("group", "dp"), None),
            P(("group", "dp"), None),
            P(("group", "tile"), None),
        ),
        check_vma=False,
    )
```

```python
import math

import jax
import jax.numpy as jnp
from jax import lax
from jax.experimental import pallas as pl
from jax.experimental.pallas import tpu as pltpu
from jax.sharding import PartitionSpec as P

highest = lax.Precision.HIGHEST
epsilon = 1e-08


def edge_strips(values):
    return jnp.stack(
        [values[..., 0, :, :], values[..., :, -1, :], values[..., -1, :, :], values[..., :, 0, :]],
        axis=0,
    )


def cycle_strips(spread):
    return jnp.stack(
        [spread[:, 0, 1:-1], spread[:, 1:-1, -1], spread[:, -1, 1:-1], spread[:, 1:-1, 0]], axis=0
    )


def assemble(tile_vals, borders):
    middle = jnp.concatenate(
        [borders[3][:, :, None, :], tile_vals, borders[1][:, :, None, :]], axis=2
    )
    top_row = jnp.pad(borders[0], ((0, 0), (1, 1), (0, 0)))[:, None]
    bottom_row = jnp.pad(borders[2], ((0, 0), (1, 1), (0, 0)))[:, None]
    return jnp.concatenate([top_row, middle, bottom_row], axis=1)


def tap_patches(padded, side):
    pieces = [
        padded[:, row_off : row_off + side, col_off : col_off + side, :]
        for row_off in range(3)
        for col_off in range(3)
    ]
    joined = jnp.concatenate(pieces, axis=-1)
    return joined.reshape(-1, joined.shape[-1])


def spread_back(flat_grads, kernel, sample_count, side):
    channels = kernel.shape[1]
    summed = jnp.zeros((sample_count, side + 2, side + 2, channels), jnp.float32)
    for tap_index in range(9):
        row_off, col_off = divmod(tap_index, 3)
        weight_tap = kernel[tap_index * channels : (tap_index + 1) * channels]
        contrib = lax.dot_general(
            flat_grads, weight_tap, (((1,), (1,)), ((), ())), preferred_element_type=jnp.float32
        )
        contrib = contrib.reshape(sample_count, side, side, channels)
        summed = summed + jnp.pad(
            contrib, ((0, 0), (row_off, 2 - row_off), (col_off, 2 - col_off), (0, 0))
        )
    return summed


def absorb_rims(interior, incoming):
    result = interior.at[..., 0, :, :].add(incoming[0])
    result = result.at[..., :, -1, :].add(incoming[1])
    result = result.at[..., -1, :, :].add(incoming[2])
    return result.at[..., :, 0, :].add(incoming[3])


def flip_edges(strips, flipped):
    return jnp.where(flipped[:, None, None, None], strips[:, :, ::-1, :], strips)


def pick_gathered(everything, near_tiles, facing, flipped, usable):
    flat = everything.reshape(everything.shape[0] * 4, -1)
    wanted = jnp.where(usable, near_tiles * 4 + facing, -1)
    selector = (lax.broadcasted_iota(jnp.int32, (4, flat.shape[0]), 1) == wanted[:, None]).astype(
        jnp.bfloat16
    )
    picked = jnp.dot(selector, flat, preferred_element_type=jnp.float32).astype(jnp.bfloat16)
    return flip_edges(picked.reshape((4,) + everything.shape[2:]), flipped)


LEAF = 128
SPAN = 384


def split(value):
    high = value.astype(jnp.bfloat16)
    return high, (value - high.astype(jnp.float32)).astype(jnp.bfloat16)


def split_wide(value):
    high = lax.reduce_precision(value, 8, 7)
    return high.astype(jnp.bfloat16), (value - high).astype(jnp.bfloat16)


def dot3(left, right, dims=(((1,), (0,)), ((), ()))):
    def one(a, b):
        return lax.dot_general(a, b, dims, preferred_element_type=jnp.float32)

    return one(left[0], right[0]) + (one(left[0], right[1]) + one(left[1], right[0]))


by_rows = (((1,), (1,)), ((), ()))


def leaf_inverse(block, m_ref, s_ref):
    row = lax.broadcasted_iota(jnp.int32, (LEAF, LEAF), 0)
    col = lax.broadcasted_iota(jnp.int32, (LEAF, LEAF), 1)
    on_diag = row == col
    unit = jnp.where(on_diag, 1.0, 0.0)
    kept = jnp.where(on_diag, block, 0.0)
    across = lax.rsqrt(jnp.sum(kept, axis=0, keepdims=True))
    down = lax.rsqrt(jnp.sum(kept, axis=1, keepdims=True))
    scaled = block * across * down
    m_ref[...] = jnp.where(on_diag, down, jnp.where(row > col, -scaled * across, 0.0))
    pair = split(block)
    rough = m_ref[...].astype(jnp.bfloat16)
    turned = jnp.dot(rough, pair[0], preferred_element_type=jnp.float32).astype(jnp.bfloat16)
    gap = lax.dot_general(turned, rough, by_rows, preferred_element_type=jnp.float32) - unit
    low = jnp.where(row > col, gap, jnp.where(on_diag, 0.5 * gap, 0.0)).astype(jnp.bfloat16)
    m_ref[...] -= jnp.dot(low, rough, preferred_element_type=jnp.float32)

    def more(carry):
        step, error = carry
        return (step < 12) & (error > 1e-4)

    def refine(carry):
        step, _ = carry
        guess = m_ref[...]
        guess_pair = split(guess)
        turned = dot3(guess_pair, pair)
        gap = dot3(split(turned), guess_pair, by_rows) - unit
        error = jnp.max(jnp.abs(gap))
        low = jnp.where(row > col, gap, jnp.where(on_diag, 0.5 * gap, 0.0))
        m_ref[...] = guess - dot3(split(low), guess_pair)
        return step + 1, error

    _, error = lax.while_loop(more, refine, (jnp.int32(0), jnp.float32(1.0)))

    @pl.when(jnp.logical_not(error <= 1e-4))
    def _():
        s_ref[...] = block
        m_ref[...] = unit

        def eliminate(j, carry):
            work = s_ref[...]
            line = s_ref[pl.ds(j, 1), :]
            lane = lax.broadcasted_iota(jnp.int32, (1, LEAF), 1)
            scale = lax.rsqrt(jnp.sum(jnp.where(lane == j, line, 0.0), axis=1, keepdims=True))
            column = jnp.sum(jnp.where(col == j, work, 0.0), axis=1, keepdims=True)
            side = lax.broadcasted_iota(jnp.int32, (LEAF, 1), 0)
            column = jnp.where(side > j, column * scale, 0.0)
            s_ref[...] = work - column * (line * scale)
            mine = m_ref[pl.ds(j, 1), :] * scale
            m_ref[...] = m_ref[...] - column * mine
            m_ref[pl.ds(j, 1), :] = mine
            return carry

        lax.fori_loop(0, LEAF, eliminate, 0)


def factor_kernel(
    gram_ref, side_ref, small_ref, y_ref, small_out_ref, a_ref, uh, ul, uth, utl, yh, yl, m_ref, s_ref
):
    width = gram_ref.shape[1]
    blocks = width // LEAF
    spans = width // SPAN
    leaf_inverse(small_ref[...], m_ref, s_ref)
    small_out_ref[...] = m_ref[...]
    a_ref[...] = gram_ref[...]
    y_ref[...] = side_ref[...]

    def block_step(k, carry):
        k0 = pl.multiple_of(k * LEAF, LEAF)
        leaf_inverse(a_ref[pl.ds(k0, LEAF), pl.ds(k0, LEAF)], m_ref, s_ref)
        inverse = split(m_ref[...])
        for span in range(spans):
            part = slice(span * SPAN, (span + 1) * SPAN)

            @pl.when((span + 1) * SPAN > k0 + LEAF)
            def _():
                value = dot3(inverse, split(a_ref[pl.ds(k0, LEAF), part]))
                uh[:, part], ul[:, part] = split(value)
                uth[part, :], utl[part, :] = split(value.T)

        value = dot3(inverse, split(y_ref[pl.ds(k0, LEAF), :]))
        y_ref[pl.ds(k0, LEAF), :] = value
        yh[...], yl[...] = split(value)

        def row_step(i, inner):
            i0 = pl.multiple_of(i * LEAF, LEAF)
            left = uth[pl.ds(i0, LEAF), :], utl[pl.ds(i0, LEAF), :]
            for span in range(spans):
                part = slice(span * SPAN, (span + 1) * SPAN)

                @pl.when((span + 1) * SPAN > i0)
                def _():
                    a_ref[pl.ds(i0, LEAF), part] -= dot3(left, (uh[:, part], ul[:, part]))

            y_ref[pl.ds(i0, LEAF), :] -= dot3(left, (yh[...], yl[...]))
            return inner

        lax.fori_loop(k + 1, blocks, row_step, 0)
        return carry

    lax.fori_loop(0, blocks, block_step, 0)


def factor_solve(gram, side, small):
    width, columns = side.shape
    vmem = pl.BlockSpec(memory_space=pltpu.VMEM)
    half = jnp.bfloat16
    return pl.pallas_call(
        factor_kernel,
        out_shape=(
            jax.ShapeDtypeStruct(side.shape, jnp.float32),
            jax.ShapeDtypeStruct(small.shape, jnp.float32),
        ),
        in_specs=[vmem] * 3,
        out_specs=(vmem, vmem),
        scratch_shapes=[
            pltpu.VMEM((width, width), jnp.float32),
            pltpu.VMEM((LEAF, width), half),
            pltpu.VMEM((LEAF, width), half),
            pltpu.VMEM((width, LEAF), half),
            pltpu.VMEM((width, LEAF), half),
            pltpu.VMEM((LEAF, columns), half),
            pltpu.VMEM((LEAF, columns), half),
            pltpu.VMEM((LEAF, LEAF), jnp.float32),
            pltpu.VMEM((LEAF, LEAF), jnp.float32),
        ],
        compiler_params=pltpu.CompilerParams(vmem_limit_bytes=40 * 1024 * 1024),
        name="factor_solve",
    )(gram, side, small)


high = lax.Precision.HIGH
tn = (((0,), (0,)), ((), ()))


def sum_kernel(dp_count, tiles, x_ref, out_ref, near, part, far, *sems):
    dp_index = lax.axis_index("dp")
    tile_index = lax.axis_index("tile")
    dp_peers = [lax.rem(dp_index + step, dp_count) for step in range(1, dp_count)]
    tile_peers = [lax.rem(tile_index + step, tiles) for step in range(1, tiles)]
    barrier = pltpu.get_barrier_semaphore()
    for axis, peers in (("dp", dp_peers), ("tile", tile_peers)):
        for peer in peers:
            pl.semaphore_signal(
                barrier, inc=1, device_id={axis: peer}, device_id_type=pl.DeviceIdType.MESH
            )
    pl.semaphore_wait(barrier, dp_count + tiles - 2)

    def exchange(axis, peers, source, target, send, receive):
        copies = [
            pltpu.make_async_remote_copy(
                src_ref=source(peer),
                dst_ref=target(slot),
                send_sem=send.at[slot],
                recv_sem=receive.at[slot],
                device_id={axis: peer},
                device_id_type=pl.DeviceIdType.MESH,
            )
            for slot, peer in enumerate(peers)
        ]
        for copy in copies:
            copy.start()
        for copy in copies:
            copy.wait()

    exchange("dp", dp_peers, lambda peer: x_ref.at[peer], lambda slot: near.at[slot], *sems[0:2])
    total = x_ref[dp_index]
    for slot in range(dp_count - 1):
        total = total + near[slot]
    part[...] = total
    exchange("tile", tile_peers, lambda peer: part.at[peer], lambda slot: far.at[slot], *sems[2:4])
    total = part[tile_index]
    for slot in range(tiles - 1):
        total = total + far[slot]
    out_ref[dp_index, tile_index] = total
    own = out_ref.at[dp_index, tile_index]
    exchange("tile", tile_peers, lambda peer: own, lambda slot: own, *sems[4:6])
    slab = out_ref.at[dp_index]
    exchange("dp", dp_peers, lambda peer: slab, lambda slot: slab, *sems[6:8])


def sum_everywhere(value):
    tiles = lax.axis_size("tile")
    dp_count = lax.axis_size("dp")
    rows, columns = value.shape
    if tiles < 2 or dp_count < 2 or rows % (tiles * dp_count):
        return lax.psum(value, ("tile", "dp"))
    piece = rows // (tiles * dp_count)
    vmem = pl.BlockSpec(memory_space=pltpu.VMEM)
    wide = (dp_count, tiles, piece, columns)
    counts = [dp_count - 1] * 2 + [tiles - 1] * 4 + [dp_count - 1] * 2
    out = pl.pallas_call(
        lambda *refs: sum_kernel(dp_count, tiles, *refs),
        out_shape=jax.ShapeDtypeStruct(wide, jnp.float32),
        in_specs=[vmem],
        out_specs=vmem,
        scratch_shapes=[
            pltpu.VMEM((dp_count - 1, tiles, piece, columns), jnp.float32),
            pltpu.VMEM((tiles, piece, columns), jnp.float32),
            pltpu.VMEM((tiles - 1, piece, columns), jnp.float32),
            *[pltpu.SemaphoreType.DMA((count,)) for count in counts],
        ],
        compiler_params=pltpu.CompilerParams(collective_id=0, has_side_effects=True),
        name="sum_everywhere",
    )(value.reshape(wide))
    return out.reshape(rows, columns)


def body_plain(
    activations,
    cotangent,
    kernel,
    turning,
    orient,
    left_factor,
    left_basis,
    right_factor,
    right_basis,
    momentum,
    second_moment,
):
    tiles = lax.axis_size("tile")
    dp_count = lax.axis_size("dp")
    tile_index = lax.axis_index("tile")
    dp_index = lax.axis_index("dp")
    tile_vals = activations[:, 0]
    tile_grads = cotangent[:, 0]
    sample_count = tile_vals.shape[0]
    side = tile_vals.shape[1]
    channels = tile_vals.shape[-1]
    own_turn = turning[0]
    facing = orient[0] % 4
    flipped = orient[0] >= 4
    heading = (jnp.arange(4, dtype=jnp.int32) + own_turn) % 4
    row_of = tile_index // 4
    col_of = tile_index % 4
    room = jnp.stack([row_of > 0, col_of < 3, row_of < tiles // 4 - 1, col_of > 0])
    usable = (
        jnp.sum(
            jnp.where(
                heading[:, None] == jnp.arange(4, dtype=jnp.int32)[None, :], room[None, :], False
            ),
            axis=1,
        )
        > 0
    )
    offsets = jnp.array([-4, 1, 4, -1], dtype=jnp.int32)
    near_tiles = tile_index + jnp.sum(
        jnp.where(heading[:, None] == jnp.arange(4, dtype=jnp.int32)[None, :], offsets[None, :], 0),
        axis=1,
    )
    strips = edge_strips(tile_vals)
    flat_grads = tile_grads.reshape(-1, channels)
    spread = spread_back(flat_grads, kernel, sample_count, side)
    rim_cells = cycle_strips(spread).astype(jnp.bfloat16)
    everything = lax.all_gather(
        jnp.concatenate([strips, rim_cells], axis=0)[None], "tile", axis=0, tiled=True
    )
    borders = pick_gathered(everything[:, :4], near_tiles, facing, flipped, usable)
    incoming = pick_gathered(everything[:, 4:], near_tiles, facing, flipped, usable)
    padded = assemble(tile_vals, borders)
    columns = tap_patches(padded, side)
    partial_grad = lax.dot_general(
        columns, flat_grads, (((0,), (0,)), ((), ())), preferred_element_type=jnp.float32
    )
    summed_grad = sum_everywhere(partial_grad)
    result = jnp.dot(columns, kernel, preferred_element_type=jnp.float32).astype(jnp.bfloat16)
    result = result.reshape(activations.shape)
    input_grad = absorb_rims(spread[:, 1:-1, 1:-1], incoming.astype(jnp.float32)).astype(
        jnp.bfloat16
    )
    input_grad = input_grad.reshape(cotangent.shape)
    cells = dp_count * sample_count * tiles * side * side
    grad = summed_grad * (1.0 / math.sqrt(cells))
    rows_per, width = left_factor.shape
    row_start = tile_index * rows_per
    moment_rows = momentum.shape[0]
    moment_start = dp_index * moment_rows
    grad_rows = lax.dynamic_slice_in_dim(grad, row_start, rows_per, 0)
    left_new = 0.95 * left_factor + 0.05 * lax.dot_general(
        grad_rows, grad, (((1,), (1,)), ((), ())), precision=high
    )
    basis_rows = lax.all_gather(left_basis, "dp", axis=1, tiled=True)
    basis = lax.all_gather(basis_rows.astype(jnp.bfloat16), "tile", axis=0, tiled=True)
    moments = lax.all_gather(
        jnp.concatenate([momentum, second_moment], axis=1), "dp", axis=0, tiled=True
    )
    all_momentum, all_second = moments[:, :channels], moments[:, channels:]
    back_rows = jnp.dot(basis_rows, all_momentum, precision=highest)
    own_row = row_start + lax.broadcasted_iota(jnp.int32, left_factor.shape, 0)
    own_col = lax.broadcasted_iota(jnp.int32, left_factor.shape, 1)
    diagonal = jnp.sum(jnp.where(own_row == own_col, left_factor, 0.0), axis=1, keepdims=True)
    rest = jnp.broadcast_to(split_wide(diagonal)[1], (rows_per, LEAF))
    factor = lax.all_gather(
        jnp.concatenate(
            [left_factor.astype(jnp.bfloat16), *split_wide(back_rows), rest], axis=1
        ),
        "tile",
        axis=0,
        tiled=True,
    )
    back = factor[:, width : width + channels].astype(jnp.float32) + factor[
        :, width + channels : width + 2 * channels
    ].astype(jnp.float32)
    rest = factor[:, width + 2 * channels : width + 2 * channels + 1]
    factor = factor[:, :width]
    mapped = 0.95 * (
        jnp.dot(factor, basis, preferred_element_type=jnp.float32)
        + rest.astype(jnp.float32) * basis.astype(jnp.float32)
    )
    mapped_gram = lax.dot_general(mapped, mapped, tn, precision=high)
    mapped_back = lax.dot_general(mapped, back, tn, precision=high)
    crossed = sum(
        lax.dot_general(term, basis, tn, preferred_element_type=jnp.float32) for term in split_wide(grad)
    )
    mapped_grad = lax.dot_general(mapped, grad, tn, precision=high)
    grad_gram = lax.dot_general(grad, grad, tn, precision=high)
    grad_back = lax.dot_general(grad, back, tn, precision=high)
    weight = 0.05 * mapped_grad + 0.00125 * lax.dot_general(crossed, grad_gram, tn, precision=high)
    gram = mapped_gram + lax.dot_general(
        jnp.concatenate([weight.T, crossed], axis=0),
        jnp.concatenate([crossed, weight.T], axis=0),
        tn,
        precision=high,
    )
    power_rows = lax.dynamic_slice_in_dim(mapped, row_start, rows_per, 0) + 0.05 * jnp.dot(
        grad_rows, crossed, precision=high
    )
    power_side = jnp.concatenate([mapped_back, mapped_grad], axis=1) + 0.05 * lax.dot_general(
        crossed, jnp.concatenate([grad_back, grad_gram], axis=1), tn, precision=high
    )
    right_new = 0.95 * right_factor + 0.05 * grad_gram
    right_power = jnp.dot(right_new, right_basis, precision=high)
    right_gram = lax.dot_general(right_power, right_power, tn, precision=high)
    solved, right_inverse = factor_solve(
        gram, jnp.concatenate([power_side, power_rows.T], axis=1), right_gram
    )
    turned_momentum = solved[:, :channels]
    turned_grad = solved[:, channels : 2 * channels]
    basis_new = solved[:, 2 * channels :].T
    right_basis_new = lax.dot_general(
        right_power, right_inverse, (((1,), (1,)), ((), ())), precision=high
    )
    right_turn = lax.dot_general(right_basis, right_basis_new, tn, precision=high)
    rotated = jnp.dot(turned_momentum, right_turn, precision=high)
    projected = jnp.dot(turned_grad, right_basis_new, precision=high)
    momentum_all = 0.9 * rotated + 0.1 * projected
    second_all = 0.95 * all_second + 0.05 * projected * projected
    normalized = momentum_all / (jnp.sqrt(second_all) + epsilon)
    momentum_new = lax.dynamic_slice_in_dim(momentum_all, moment_start, moment_rows, 0)
    second_new = lax.dynamic_slice_in_dim(second_all, moment_start, moment_rows, 0)
    update_rows = jnp.dot(basis_new, normalized, precision=high)
    update = lax.dot_general(
        update_rows, right_basis_new, (((1,), (1,)), ((), ())), precision=high
    )
    return (
        result,
        input_grad,
        grad,
        left_new,
        basis_new,
        right_new,
        right_basis_new,
        momentum_new,
        second_new,
        update,
    )


ZS = 4
CORES = 2
DPS = 4
LANES = 384
CELL = 24


def to_device(source, target, send, receive, **device):
    return pltpu.make_async_remote_copy(
        src_ref=source,
        dst_ref=target,
        send_sem=send,
        recv_sem=receive,
        device_id=device,
        device_id_type=pl.DeviceIdType.MESH,
    )


def greet():
    t = lax.axis_index("tile")
    d = lax.axis_index("dp")
    barrier = pltpu.get_barrier_semaphore()
    tiles = ZS * CORES
    for step in range(1, tiles):
        pl.semaphore_signal(
            barrier,
            inc=1,
            device_id={"tile": lax.rem(t + step, tiles)},
            device_id_type=pl.DeviceIdType.MESH,
        )
    for step in range(1, DPS):
        pl.semaphore_signal(
            barrier,
            inc=1,
            device_id={"dp": lax.rem(d + step, DPS)},
            device_id_type=pl.DeviceIdType.MESH,
        )
    pl.semaphore_wait(barrier, tiles + DPS - 2)


class Edges:
    def __init__(self, source, target, send, receive):
        t = lax.axis_index("tile")
        row, col = t // 4, t % 4
        self.rooms = (row > 0, col < 3, row < 1, col > 0)
        self.target = target
        self.copies = []
        for h, step in enumerate((4, 1, 4, 7)):
            back = (h + 2) % 4
            peer = lax.rem(t + step, ZS * CORES)
            self.copies.append(
                to_device(source.at[h], target.at[back], send.at[h], receive.at[back], tile=peer)
            )

    def start(self):
        for h in range(4):

            @pl.when(self.rooms[h])
            def _():
                self.copies[h].start()

            @pl.when(jnp.logical_not(self.rooms[h]))
            def _():
                self.target[h] = jnp.zeros(self.target.shape[1:], self.target.dtype)

    def wait(self):
        for h in range(4):

            @pl.when(self.rooms[h])
            def _():
                self.copies[h].wait_send()
                self.copies[(h + 2) % 4].wait_recv()


def finish_kernel(
    grad_ref,
    back_ref,
    mapped_ref,
    crossed_ref,
    grad_both_ref,
    left_new_ref,
    right_in_ref,
    right_basis_ref,
    second_ref,
    result_ref,
    input_grad_ref,
    result_out,
    input_grad_out,
    grad_out,
    left_out,
    basis_out,
    right_out,
    right_basis_out,
    momentum_out,
    second_out,
    update_out,
    m_ref,
    left_ref,
    right_ref,
    work_ref,
    gram_ref,
    up_ref,
    down_ref,
    y_ref,
    turn_ref,
    aux_ref,
    big_ref,
):
    t = lax.axis_index("tile")
    d = lax.axis_index("dp")
    width, channels = grad_ref.shape
    blocks = width // LEAF
    rows_per = left_new_ref.shape[0]
    moment_rows = momentum_out.shape[0]
    wide = work_ref.shape[1]
    own_rows = pl.ds(pl.multiple_of(t * rows_per, 16), rows_per)

    result_out[...] = result_ref[...]
    input_grad_out[...] = input_grad_ref[...]
    extra = LEAF // 4

    lane = lax.broadcasted_iota(jnp.int32, (1, LEAF), 1)

    def tile_of(middle, shared, folded, j):
        group, spot = divmod(j, 2)
        if spot:
            return middle(group)
        if group == 0:
            return shared(0)
        value = jnp.where(lane >= extra * (group - 1), folded(group - 1), shared(group - 1))
        return jnp.where(lane >= extra * group, shared(group), value) if group < DPS else value

    def stack(g, begin, end):
        blocks_of = [mapped_ref[g, tile, begin:end, :] for tile in range(mapped_ref.shape[1])]
        return jnp.concatenate(blocks_of, axis=0).astype(jnp.float32)

    def folded_rows(g):
        return jnp.concatenate(
            [
                unfold(mapped_ref[g, tile, 2 * rows_per :, :].astype(jnp.float32), 3)
                for tile in range(mapped_ref.shape[1])
            ],
            axis=0,
        )

    for j in range(blocks):
        at = slice(j * LEAF, (j + 1) * LEAF)
        value = tile_of(
            lambda g: stack(g, 0, rows_per), lambda g: stack(g, rows_per, 2 * rows_per), folded_rows, j
        ).astype(jnp.bfloat16)
        m_ref[:, at] = value
        left_ref[at, :width] = value.T
    crossed = jnp.concatenate(
        [
            tile_of(
                lambda g: crossed_ref[g, :channels, :].astype(jnp.float32),
                lambda g: crossed_ref[g, channels : 2 * channels, :].astype(jnp.float32),
                lambda g: unfold(crossed_ref[g, 2 * channels :, :].astype(jnp.float32), 4),
                j,
            )
            for j in range(blocks)
        ],
        axis=1,
    )
    grad = grad_ref[...]
    grad_out[...] = grad
    grad_t = grad.T
    both = jnp.concatenate([back_ref[...], grad], axis=1)
    both_pair = split(both)
    grad_both = grad_both_ref[...]
    grad_gram = grad_both[:, channels:]
    grad_rows = grad_ref[own_rows, :]
    left_out[...] = left_new_ref[...]
    right_out[...] = right_in_ref[0]
    right_basis_out[...] = right_in_ref[4]
    turn_ref[...] = right_in_ref[5]

    grad_m = product(jnp.concatenate(split(grad_t), axis=0), m_ref[...])
    weight = 0.05 * (grad_m[:channels] + grad_m[channels:]) + 0.00125 * matmul(grad_gram, crossed)
    pair = jnp.concatenate([weight, crossed], axis=0)
    pair_t = pair.T
    left_ref[:, width:] = wide_left(split(pair_t))
    right_ref[...] = wide_right(split(jnp.concatenate([crossed, weight], axis=0)))
    for j in range(0, blocks, 2):
        end = min(j + 2, blocks) * LEAF
        at = slice(j * LEAF, end)
        value = product(left_ref[:end, :width], m_ref[:, at]) + product(
            left_ref[:end, width:], right_ref[:, at]
        )
        work_ref[:end, at] = value
        gram_ref[:end, at] = value
    m_both = product(left_ref[:, :width], both_pair[0]) + product(left_ref[:, :width], both_pair[1])
    crossed_t = pair_t[:, channels:]
    work_ref[:, width : width + 2 * channels] = m_both + 0.05 * matmul(crossed_t, grad_both)
    power_rows = m_ref[own_rows, :].astype(jnp.float32) + 0.05 * matmul(grad_rows, crossed)
    padded = jnp.concatenate(
        [power_rows, jnp.zeros((2 * LEAF - rows_per, width), jnp.float32)], axis=0
    )
    work_ref[:, width + 2 * channels :] = padded.T
    gram_ref[:, width:] = work_ref[:, width:]

    worst = right_in_ref[3]
    for k in range(blocks):
        at = slice(k * LEAF, (k + 1) * LEAF)
        inverse, gap = quick_leaf(work_ref[at, at])
        worst = jnp.maximum(worst, gap)
        value = product(wide_left(split(inverse)), wide_right(split(work_ref[at, (k + 1) * LEAF :])))
        y_ref[at, :] = value[:, width - (k + 1) * LEAF :]
        if k == blocks - 1:
            break
        start = (k + 1) * LEAF
        up_ref[:, start:] = wide_right(split(value))
        down_ref[start:, :] = wide_left(split(value[:, : width - start].T))
        edges = list(range(start, width, 2 * LEAF))
        spans = [(a, min(a + 2 * LEAF, width)) for a in edges] + [
            (a, a + 2 * LEAF) for a in range(width, wide, 2 * LEAF)
        ]
        for a, b in spans:
            bottom = min(b, width)
            work_ref[start:bottom, a:b] -= product(down_ref[start:bottom, :], up_ref[:, a:b])

    @pl.when(jnp.logical_not(jnp.max(worst) <= 0.03))
    def _():
        leaf_inverse(right_in_ref[2], big_ref, aux_ref)
        turned = matmul_rows(right_in_ref[1], big_ref[...])
        right_basis_out[...] = turned
        turn_ref[...] = matmul(right_basis_ref[...].T, turned)
        work_ref[...] = gram_ref[...]

        def block_step(k, carry):
            k0 = pl.multiple_of(k * LEAF, LEAF)
            leaf_inverse(work_ref[pl.ds(k0, LEAF), pl.ds(k0, LEAF)], big_ref, aux_ref)
            inverse = wide_left(split(big_ref[...]))
            for a in range(0, wide, LEAF):
                value = product(inverse, wide_right(split(work_ref[pl.ds(k0, LEAF), a : a + LEAF])))
                up_ref[:, a : a + LEAF] = wide_right(split(value))
                if a < width:
                    down_ref[a : a + LEAF, :] = wide_left(split(value.T))
                else:
                    y_ref[pl.ds(k0, LEAF), a - width : a - width + LEAF] = value

            def row_step(i, inner):
                i0 = pl.multiple_of(i * LEAF, LEAF)
                left = down_ref[pl.ds(i0, LEAF), :]
                for a in range(0, wide, LEAF):

                    @pl.when(a + LEAF > i0)
                    def _():
                        work_ref[pl.ds(i0, LEAF), a : a + LEAF] -= product(
                            left, up_ref[:, a : a + LEAF]
                        )

                return inner

            lax.fori_loop(k + 1, blocks, row_step, 0)
            return carry

        lax.fori_loop(0, blocks, block_step, 0)

    right_basis_new = right_basis_out[...]
    right_turn = turn_ref[...]
    solved = y_ref[...]
    rotated = matmul(solved[:, :channels], right_turn)
    projected = matmul(solved[:, channels : 2 * channels], right_basis_new)
    basis_new = solved[:, 2 * channels :].T[:rows_per]
    basis_out[...] = basis_new
    momentum = 0.9 * rotated + 0.1 * projected
    second = 0.95 * second_ref[...] + 0.05 * projected * projected
    up = momentum / (jnp.sqrt(second) + epsilon)
    update_rows = matmul(basis_new, up)
    update_out[...] = matmul_rows(update_rows, right_basis_new)
    y_ref[:, :channels] = momentum
    y_ref[:, channels : 2 * channels] = second
    own = pl.ds(pl.multiple_of(d * moment_rows, 8), moment_rows)
    momentum_out[...] = y_ref[own, :channels]
    second_out[...] = y_ref[own, channels : 2 * channels]


def finish(
    grad, back, mapped, crossed, grad_both, left_new, right, right_basis, second, result, input_grad, moment_rows
):
    vmem = pl.BlockSpec(memory_space=pltpu.VMEM)
    width, channels = grad.shape
    rows_per = left_new.shape[0]
    wide = width + 2 * channels + 2 * LEAF
    half = jnp.bfloat16
    single = jnp.float32
    square = pltpu.VMEM((LEAF, LEAF), single)
    shapes = [
        left_new.shape,
        left_new.shape,
        right_basis.shape,
        right_basis.shape,
        (moment_rows, channels),
        (moment_rows, channels),
        (rows_per, channels),
    ]
    return pl.pallas_call(
        finish_kernel,
        out_shape=(
            jax.ShapeDtypeStruct(result.shape, half),
            jax.ShapeDtypeStruct(input_grad.shape, half),
            jax.ShapeDtypeStruct(grad.shape, single),
            *(jax.ShapeDtypeStruct(shape, single) for shape in shapes),
        ),
        in_specs=[vmem] * 11,
        out_specs=(vmem,) * 10,
        scratch_shapes=[
            pltpu.VMEM((width, width), half),
            pltpu.VMEM((width, width + 6 * channels), half),
            pltpu.VMEM((6 * channels, width), half),
            pltpu.VMEM((width, wide), single),
            pltpu.VMEM((width, wide), single),
            pltpu.VMEM((3 * LEAF, wide), half),
            pltpu.VMEM((width, 3 * LEAF), half),
            pltpu.VMEM((width, wide - width), single),
            square,
            square,
            square,
        ],
        compiler_params=pltpu.CompilerParams(vmem_limit_bytes=56 * 1024 * 1024),
        name="finish",
    )(
        grad, back, mapped, crossed, grad_both, left_new, right, right_basis, second, result, input_grad
    )


def wide_left(pair, axis=1):
    return jnp.concatenate([pair[0], pair[0], pair[1]], axis=axis)


def wide_right(pair, axis=0):
    return jnp.concatenate([pair[0], pair[1], pair[0]], axis=axis)


plain = (((1,), (0,)), ((), ()))


def product(left, right):
    return lax.dot_general(left, right, plain, preferred_element_type=jnp.float32)


def product_rows(left, right):
    return lax.dot_general(left, right, by_rows, preferred_element_type=jnp.float32)


def matmul(left, right):
    return product(wide_left(split(left)), wide_right(split(right)))


def matmul_rows(left, right):
    return product_rows(wide_left(split(left)), wide_right(split(right), 1))


def quick_leaf(block, cheap=2):
    row = lax.broadcasted_iota(jnp.int32, (LEAF, LEAF), 0)
    col = lax.broadcasted_iota(jnp.int32, (LEAF, LEAF), 1)
    on_diag = row == col
    below = row > col
    unit = jnp.where(on_diag, 1.0, 0.0)
    kept = jnp.where(on_diag, block, 0.0)
    across = lax.rsqrt(jnp.sum(kept, axis=0, keepdims=True))
    down = lax.rsqrt(jnp.sum(kept, axis=1, keepdims=True))

    def lower(gap):
        return jnp.where(below, gap, jnp.where(on_diag, 0.5 * gap, 0.0)).astype(jnp.bfloat16)

    high_part, low_part = split(block)
    guess = jnp.where(on_diag, down, jnp.where(below, -block * (across * across) * down, 0.0))
    for _ in range(cheap):
        rough = guess.astype(jnp.bfloat16)
        turned = product(rough, high_part).astype(jnp.bfloat16)
        gap = product_rows(turned, rough) - unit
        guess = rough.astype(jnp.float32) - product(lower(gap), rough)
    rough = guess.astype(jnp.bfloat16)
    twice = jnp.concatenate([rough, rough], axis=1)
    turned = product(twice, jnp.concatenate([high_part, low_part], axis=0))
    gap = product_rows(jnp.concatenate(split(turned), axis=1), twice) - unit
    return rough.astype(jnp.float32) - product(lower(gap), rough), jnp.abs(gap)


def fold(value, parts):
    step = LEAF // 4
    rows = value.shape[0] // parts
    total = value[:rows]
    for i in range(1, parts):
        total = total + pltpu.roll(value[i * rows : (i + 1) * rows], step * i, 1)
    return total


def unfold(value, parts):
    step = LEAF // 4
    return jnp.concatenate(
        [value] + [pltpu.roll(value, LEAF - step * i, 1) for i in range(1, parts)], axis=0
    )


SEMS = {
    "edge": 4,
    "rim": 4,
    "basis_z": 3,
    "basis_sib": 4,
    "back_sum": 3,
    "back_z": 3,
    "back_dp": 3,
    "back_sib": 4,
    "second_dp": 3,
    "second_sib": 3,
    "swap": 1,
    "grad_sum": 3,
    "grad_zsum": 3,
    "grad_z": 3,
    "grad_dp": 3,
    "grad_sib": 4,
    "map_z": 3,
    "map_x": 4,
    "map_y": 4,
    "map_far": 8,
    "map_sib": 16,
    "cross_dp": 3,
    "cross_sib": 3,
}
CUT = 176


def exchange_kernel(
    grad_scale,
    turning_ref,
    orient_ref,
    act_ref,
    cot_ref,
    kernel_ref,
    basis_in_ref,
    momentum_ref,
    second_ref,
    factor_ref,
    right_factor_ref,
    right_basis_ref,
    result_ref,
    input_grad_ref,
    grad_ref,
    back_ref,
    seconds_ref,
    all_ref,
    crossed_ref,
    grad_both_ref,
    left_ref,
    right_ref,
    strips,
    borders,
    rims,
    incoming,
    block_ref,
    basis,
    columns_ref,
    back_in_ref,
    back_near,
    back_all,
    padded,
    patches,
    spread,
    inner,
    partial,
    near,
    half,
    dp_in,
    pieces,
    z_in,
    grad_all,
    own_map,
    *sems,
):
    count = len(SEMS)
    send = dict(zip(SEMS, sems[:count]))
    receive = dict(zip(SEMS, sems[count:]))
    t = lax.axis_index("tile")
    d = lax.axis_index("dp")
    z, c = t // CORES, t % CORES
    sibling = t + 1 - 2 * c
    x_peer = d + 1 - 2 * (d % 2)
    y_peer = lax.rem(d + 2, DPS)
    far_peer = lax.rem(x_peer + 2, DPS)
    rest = range(1, ZS)
    z_peers = [lax.rem(t + CORES * k, ZS * CORES) for k in range(ZS)]
    z_from = [lax.rem(z + ZS - k, ZS) for k in range(ZS)]
    z_to = [lax.rem(z + k, ZS) for k in range(ZS)]
    d_to = [lax.rem(d + j, DPS) for j in range(DPS)]
    d_from = [lax.rem(d + DPS - j, DPS) for j in range(DPS)]
    side = input_grad_ref.shape[0] // CELL
    channels = grad_ref.shape[1]
    width = grad_ref.shape[0]
    pending = []

    def copy(name, index, source, target, **device):
        made = to_device(source, target, send[name].at[index], receive[name].at[index], **device)
        pending.append(made)
        return made

    def start(copies):
        for made in copies:
            made.start()

    def arrive(copies):
        for made in copies:
            made.wait_recv()

    def z_group(name, source, target):
        return [copy(name, k - 1, source(k), target(k), tile=z_peers[k]) for k in rest]

    def dp_group(name, source, target):
        return [copy(name, j - 1, source(j), target(j), dp=d_to[j]) for j in rest]

    turn = turning_ref[0]
    padded[...] = jnp.zeros(padded.shape, jnp.float32)
    padded[1 : side + 1, 1 : side + 1, :] = act_ref[...].astype(jnp.float32).reshape(side, side, channels)
    line = lax.broadcasted_iota(jnp.int32, (side, side), 0)
    place = lax.broadcasted_iota(jnp.int32, (side, side), 1)
    straight = jnp.where(line == place, 1.0, 0.0)
    crosswise = jnp.where(line + place == side - 1, 1.0, 0.0)
    orders = [
        jnp.where(orient_ref[0, e] >= 4, crosswise, straight).astype(jnp.bfloat16) for e in range(4)
    ]

    def fill(target, lines):
        aligned = [product(orders[e], lines[e].astype(jnp.bfloat16)) for e in range(4)]
        for h in range(4):
            wanted = lax.rem(h + 4 - turn, 4)
            target[h] = sum(jnp.where(wanted == e, aligned[e], 0.0) for e in range(4)).astype(
                jnp.bfloat16
            )

    fill(
        strips,
        [
            padded[1, 1 : side + 1, :],
            padded[1 : side + 1, side, :],
            padded[side, 1 : side + 1, :],
            padded[1 : side + 1, 1, :],
        ],
    )
    greet()
    edges = Edges(strips, borders, send["edge"], receive["edge"])
    edges.start()
    part = basis_in_ref.shape[1]
    rows_per = basis_in_ref.shape[0]
    extra = part % LEAF
    old_basis = basis_in_ref[...]
    shifted = jnp.zeros((rows_per, LANES), jnp.float32)
    for slot in range(DPS):
        pieces_of = [old_basis, jnp.zeros((rows_per, LANES - part - extra * slot), jnp.float32)]
        if slot:
            pieces_of.insert(0, jnp.zeros((rows_per, extra * slot), jnp.float32))
        pieces_of = [p for p in pieces_of if p.shape[1]]
        shifted = jnp.where(d == slot, jnp.concatenate(pieces_of, axis=1), shifted)
    lane = lax.broadcasted_iota(jnp.int32, (1, LEAF), 1)
    window = (lane >= extra * d) & (lane < extra * (d + 1))
    first_tile, last_tile = shifted[:, :LEAF], shifted[:, 2 * LEAF :]
    block_ref[...] = jnp.concatenate(
        [
            shifted[:, LEAF : 2 * LEAF],
            jnp.where(lane >= extra * d, first_tile, last_tile),
            fold(jnp.where(window, last_tile, 0.0), 3),
        ],
        axis=0,
    ).astype(jnp.bfloat16)
    own_basis = basis.at[z, c]
    basis_z = z_group("basis_z", lambda k: block_ref, lambda k: own_basis)
    basis_sib = [
        copy(
            "basis_sib",
            k,
            block_ref if k == 0 else basis.at[z_from[k], c],
            basis.at[z_from[k], c],
            tile=sibling,
        )
        for k in range(ZS)
    ]
    back_sum = dp_group("back_sum", lambda j: back_in_ref.at[d_to[j]], lambda j: back_near.at[j - 1])
    second_dp = dp_group("second_dp", lambda j: second_ref.at[c], lambda j: seconds_ref.at[d, c])
    start(basis_z)
    start(basis_sib[:1])

    old_pair, moment_pair = split(old_basis), split(momentum_ref[...])
    value = product(old_pair[0], moment_pair[0]) + (
        product(old_pair[0], moment_pair[1]) + product(old_pair[1], moment_pair[0])
    )
    piece = rows_per // DPS
    for dp in range(DPS):
        back_in_ref[dp] = value[dp * piece : (dp + 1) * piece]
    start(back_sum)
    start(second_dp)
    own_basis[...] = block_ref[...]
    seconds_ref[d] = second_ref[...]

    cot = cot_ref[...]
    cot_t = jnp.concatenate(
        [cot.astype(jnp.float32), jnp.zeros((LEAF - side * side % LEAF, channels), jnp.float32)], axis=0
    ).T[:, : side * side].astype(jnp.bfloat16)

    def pick(ref, wanted):
        return sum(
            jnp.where(wanted == h, ref[h].astype(jnp.float32), 0.0) for h in range(4)
        )

    edges.wait()
    border = [pick(borders, lax.rem(turn + e, 4)) for e in range(4)]
    padded[0, 1 : side + 1, :] = border[0]
    padded[1 : side + 1, side + 1, :] = border[1]
    padded[side + 1, 1 : side + 1, :] = border[2]
    padded[1 : side + 1, 0, :] = border[3]
    for col in range(3):
        lines = padded[:, col : col + side, :].reshape((side + 2) * side, channels)
        for row in range(3):
            at = (3 * row + col) * channels
            patches[:, at : at + channels] = lines[row * side : row * side + side * side].astype(
                jnp.bfloat16
            )
    turned = product(cot_t, patches[...])
    block = partial.shape[2]
    value = turned.T
    for core in range(CORES):
        for dp in range(DPS):
            at = (core * DPS + dp) * block
            partial[core, dp] = value[at : at + block]
    swap = copy("swap", 0, partial.at[1 - c], near, tile=sibling)
    swap.start()

    arrive(back_sum)
    total = back_in_ref[d]
    for slot in range(DPS - 1):
        total = total + back_near[slot]
    back_all[c, d, z] = total
    mine = back_all.at[c, d, z]
    back_z = z_group("back_z", lambda k: mine, lambda k: mine)
    start(back_z)

    swap.wait_recv()
    half[...] = partial[c] + near[...]
    grad_sum = dp_group("grad_sum", lambda j: half.at[d_to[j]], lambda j: dp_in.at[j - 1])
    start(grad_sum)

    for k in rest:
        basis_z[k - 1].wait_recv()
        basis_sib[k].start()
    arrive(back_z)
    slab = back_all.at[c, d]
    back_dp = dp_group("back_dp", lambda j: slab, lambda j: slab)
    start(back_dp)

    arrive(basis_sib)
    for at_z in range(ZS):
        for core in range(CORES):
            at = (at_z * CORES + core) * rows_per
            at = slice(at, at + rows_per)
            columns_ref[at, :LEAF] = basis[at_z, core, :rows_per]
            columns_ref[at, LEAF : 2 * LEAF] = basis[at_z, core, rows_per : 2 * rows_per]
            columns_ref[at, 2 * LEAF :] = unfold(
                basis[at_z, core, 2 * rows_per :].astype(jnp.float32), 3
            ).astype(jnp.bfloat16)
    columns = columns_ref[...]
    factor = split(factor_ref[...])
    mapped = 0.95 * (product(factor[0], columns) + product(factor[1], columns))
    mapped = jnp.concatenate(
        [
            mapped[:, :LEAF],
            mapped[:, LEAF : 2 * LEAF],
            fold(jnp.where(window, mapped[:, 2 * LEAF :], 0.0), 3),
        ],
        axis=0,
    ).astype(jnp.bfloat16)
    own_map[...] = mapped
    all_ref[d, z, c] = mapped

    def spot_of(dp, k):
        return all_ref.at[dp, z_from[k], c]

    def own_spot(k):
        return own_map if k == 0 else spot_of(d, k)

    map_z = z_group("map_z", lambda k: own_map, lambda k: spot_of(d, 0))
    map_x = [copy("map_x", k, own_spot(k), spot_of(d, k), dp=x_peer) for k in range(ZS)]
    map_y = [copy("map_y", k, own_spot(k), spot_of(d, k), dp=y_peer) for k in range(ZS)]
    map_sib = [copy("map_sib", k, own_spot(k), spot_of(d, k), tile=sibling) for k in range(ZS)]
    upper, lower = pl.ds(0, CUT), pl.ds(CUT, own_map.shape[0] - CUT)

    def relay(k):
        up = spot_of(x_peer, k).at[upper]
        down = spot_of(y_peer, k).at[lower]
        return [
            copy("map_far", 2 * k, up, up, dp=y_peer),
            copy("map_far", 2 * k + 1, down, down, dp=x_peer),
        ]

    relays = [relay(k) for k in range(ZS)]

    def relay_arrive(k):
        arrive(relays[k])

    start(map_z)
    start([map_x[0], map_y[0], map_sib[0]])

    arrive(grad_sum)
    total = half[d]
    for slot in range(DPS - 1):
        total = total + dp_in[slot]
    for k in range(ZS):
        pieces[k] = total[k * piece : (k + 1) * piece]
    grad_zsum = z_group("grad_zsum", lambda k: pieces.at[z_to[k]], lambda k: z_in.at[k - 1])
    start(grad_zsum)

    arrive(grad_zsum)
    total = pieces[z]
    for slot in range(ZS - 1):
        total = total + z_in[slot]
    grad_all[c, d, z] = total
    own_piece = grad_all.at[c, d, z]
    grad_z = z_group("grad_z", lambda k: own_piece, lambda k: own_piece)
    start(grad_z)

    def slabs(ref, name):
        spots = [ref.at[c, d_from[j]] for j in range(DPS)]
        return [copy(name, j, spots[j], spots[j], tile=sibling) for j in range(DPS)]

    arrive(back_dp)
    back_sib = slabs(back_all, "back_sib")
    start(back_sib)
    second_sib = []
    for j in rest:
        spot = seconds_ref.at[d_from[j], c]
        second_sib.append(copy("second_sib", j - 1, spot, spot, tile=sibling))
    arrive(second_dp)
    start(second_sib)

    arrive(grad_z)
    grad_slab = grad_all.at[c, d]
    grad_dp = dp_group("grad_dp", lambda j: grad_slab, lambda j: grad_slab)
    start(grad_dp)

    for k in rest:
        map_z[k - 1].wait_recv()
        start([map_x[k], map_y[k], map_sib[k]])

    terms = product_rows(cot, kernel_ref[...])
    spread[...] = jnp.zeros(spread.shape, jnp.float32)
    for col in range(3):
        stack = None
        for row in range(3):
            at = (3 * row + col) * channels
            term = terms[:, at : at + channels]
            parts = [term]
            if row:
                parts.insert(0, jnp.zeros((row * side, channels), jnp.float32))
            if row < 2:
                parts.append(jnp.zeros(((2 - row) * side, channels), jnp.float32))
            term = jnp.concatenate(parts, axis=0)
            stack = term if stack is None else stack + term
        spread[:, col : col + side, :] += stack.reshape(side + 2, side, channels)
    fill(
        rims,
        [
            spread[0, 1 : side + 1, :],
            spread[1 : side + 1, side + 1, :],
            spread[side + 1, 1 : side + 1, :],
            spread[1 : side + 1, 0, :],
        ],
    )
    rim_edges = Edges(rims, incoming, send["rim"], receive["rim"])
    rim_edges.start()

    def far_sib(j, k):
        spot = spot_of((x_peer, y_peer, far_peer)[j], k)
        return copy("map_sib", ZS * (j + 1) + k, spot, spot, tile=sibling)

    map_far = [[far_sib(j, k) for k in range(ZS)] for j in range(3)]

    def pass_on(k):
        arrive([map_x[k], map_y[k]])
        start(relays[k])
        start([map_far[0][k], map_far[1][k]])

    pass_on(0)
    result_ref[...] = product(patches[...], kernel_ref[...]).astype(jnp.bfloat16)
    pass_on(1)

    grad_sib = slabs(grad_all, "grad_sib")
    grad_sib[0].start()
    for j in rest:
        grad_dp[j - 1].wait_recv()
        grad_sib[j].start()
    arrive(grad_sib)
    for core in range(CORES):
        for dp in range(DPS):
            for at_z in range(ZS):
                at = ((core * DPS + dp) * ZS + at_z) * piece
                grad_ref[at : at + piece] = grad_all[core, dp, at_z]
    grad = grad_ref[...] * grad_scale
    grad_ref[...] = grad
    grad_t = grad.T
    high_part, low_part = split(grad_t)
    crossed = product(high_part, columns) + product(low_part, columns)
    crossed = jnp.concatenate(
        [
            crossed[:, :LEAF],
            crossed[:, LEAF : 2 * LEAF],
            fold(jnp.where(window, crossed[:, 2 * LEAF :], 0.0), 4),
        ],
        axis=0,
    ).astype(jnp.bfloat16)
    halves = crossed.shape[0] // CORES
    for core in range(CORES):
        crossed_ref[d, core] = crossed[core * halves : (core + 1) * halves]
    own_cross = crossed_ref.at[d, c]
    cross_dp = dp_group("cross_dp", lambda j: own_cross, lambda j: own_cross)
    start(cross_dp)

    pass_on(2)
    arrive(back_sib)
    for core in range(CORES):
        for dp in range(DPS):
            for at_z in range(ZS):
                to = ((at_z * CORES + core) * DPS + dp) * piece
                back_ref[to : to + piece] = back_all[core, dp, at_z]

    both = jnp.concatenate([back_ref[...], grad], axis=1)
    grad_both = product(wide_left(split(grad_t)), wide_right(split(both)))
    grad_both_ref[...] = grad_both
    own_rows = pl.ds(pl.multiple_of(t * rows_per, 16), rows_per)
    left_ref[...] = 0.95 * factor_ref[...] + 0.05 * matmul_rows(grad_ref[own_rows, :], grad)
    right_new = 0.95 * right_factor_ref[...] + 0.05 * grad_both[:, channels:]
    right_basis = right_basis_ref[...]
    right_power = matmul(right_new, right_basis)
    right_gram = matmul(right_power.T, right_power)
    pass_on(3)
    right_inverse, right_gap = quick_leaf(right_gram, 4)
    right_basis_new = matmul_rows(right_power, right_inverse)
    right_turn = matmul(right_basis.T, right_basis_new)
    for slot, value in enumerate(
        (right_new, right_power, right_gram, right_gap, right_basis_new, right_turn)
    ):
        right_ref[slot] = value

    for k in range(ZS):
        relay_arrive(k)
        map_far[2][k].start()

    cross_sib = []
    for j in rest:
        spot = crossed_ref.at[d_from[j], c]
        cross_dp[j - 1].wait_recv()
        made = copy("cross_sib", j - 1, spot, spot, tile=sibling)
        made.start()
        cross_sib.append(made)
    rim_edges.wait()
    value = [pick(incoming, lax.rem(turn + e, 4)) for e in range(4)]
    inner[...] = spread[1 : side + 1, 1 : side + 1, :]
    inner[0, :, :] += value[0]
    inner[:, side - 1, :] += value[1]
    inner[side - 1, :, :] += value[2]
    inner[:, 0, :] += value[3]
    input_grad_ref[...] = inner[...].reshape(side * side, channels).astype(jnp.bfloat16)

    arrive(second_sib)
    arrive(map_sib)
    for group in map_far:
        arrive(group)
    arrive(cross_sib)
    for made in pending:
        made.wait_send()


def exchange(
    turning, orient, acts, cots, kernel, old_basis, momentum, second, factor, right_factor, right_basis, scale
):
    vmem = pl.BlockSpec(memory_space=pltpu.VMEM)
    width, channels = kernel.shape
    rows = width // (CORES * DPS)
    side = CELL
    half, single = jnp.bfloat16, jnp.float32
    dma = [pltpu.SemaphoreType.DMA((count,)) for count in SEMS.values()]
    out = jax.ShapeDtypeStruct
    strip = pltpu.VMEM((4, side, channels), half)
    block = (2 * rows + rows // 3, LEAF)
    piece = (rows // DPS, channels)
    return pl.pallas_call(
        lambda *refs: exchange_kernel(scale, *refs),
        out_shape=(
            out(acts.shape, half),
            out(acts.shape, half),
            out((width, channels), single),
            out((width, channels), single),
            out((DPS,) + second.shape, single),
            out((DPS, ZS, CORES) + block, half),
            out((DPS, CORES, (2 * channels + channels // 4) // CORES, LEAF), half),
            out((channels, 2 * channels), single),
            out(factor.shape, single),
            out((6,) + right_factor.shape, single),
        ),
        in_specs=[pl.BlockSpec(memory_space=pltpu.SMEM)] * 2 + [vmem] * 9,
        out_specs=(vmem,) * 10,
        scratch_shapes=[
            strip,
            strip,
            strip,
            strip,
            pltpu.VMEM(block, half),
            pltpu.VMEM((ZS, CORES) + block, half),
            pltpu.VMEM((width, LANES), half),
            pltpu.VMEM((DPS,) + piece, single),
            pltpu.VMEM((DPS - 1,) + piece, single),
            pltpu.VMEM((CORES, DPS, ZS) + piece, single),
            pltpu.VMEM((side + 2, 32, channels), single),
            pltpu.VMEM((side * side, width), half),
            pltpu.VMEM((side + 2, 32, channels), single),
            pltpu.VMEM((side, side, channels), single),
            pltpu.VMEM((CORES, DPS, rows, channels), single),
            pltpu.VMEM((DPS, rows, channels), single),
            pltpu.VMEM((DPS, rows, channels), single),
            pltpu.VMEM((DPS - 1, rows, channels), single),
            pltpu.VMEM((ZS, rows // ZS, channels), single),
            pltpu.VMEM((ZS - 1, rows // ZS, channels), single),
            pltpu.VMEM((CORES, DPS, ZS, rows // ZS, channels), single),
            pltpu.VMEM(block, half),
            *dma,
            *dma,
        ],
        compiler_params=pltpu.CompilerParams(
            collective_id=0, has_side_effects=True, vmem_limit_bytes=56 * 1024 * 1024
        ),
        name="exchange",
    )(turning, orient, acts, cots, kernel, old_basis, momentum, second, factor, right_factor, right_basis)


def body_quick(
    activations,
    cotangent,
    kernel,
    turning,
    orient,
    left_factor,
    left_basis,
    right_factor,
    right_basis,
    momentum,
    second_moment,
):
    tiles, dp_count = ZS * CORES, DPS
    tile_vals = activations[:, 0]
    tile_grads = cotangent[:, 0]
    side = tile_vals.shape[1]
    channels = tile_vals.shape[-1]
    width = left_factor.shape[1]
    moment_rows = momentum.shape[0]

    cells = dp_count * tiles * side * side
    result, input_grad, grad, back, seconds, mapped, crossed, grad_both, left_new, right = exchange(
        turning,
        orient,
        tile_vals.reshape(side * side, channels),
        tile_grads.reshape(side * side, channels),
        kernel,
        left_basis,
        momentum,
        second_moment.reshape(CORES, moment_rows // CORES, channels),
        left_factor,
        right_factor,
        right_basis,
        1.0 / math.sqrt(cells),
    )
    all_second = seconds.reshape(width, channels)
    outs = finish(
        grad,
        back,
        mapped.reshape((DPS, tiles) + mapped.shape[3:]),
        crossed.reshape(DPS, -1, LEAF),
        grad_both,
        left_new,
        right,
        right_basis,
        all_second,
        result,
        input_grad,
        moment_rows,
    )
    return (outs[0].reshape(activations.shape), outs[1].reshape(cotangent.shape), *outs[2:])


def body(*args):
    tiles = lax.axis_size("tile")
    dp_count = lax.axis_size("dp")
    left_basis = args[6]
    samples = args[0].shape[0]
    sizes = (tiles, dp_count, samples, args[0].shape[2])
    if sizes == (ZS * CORES, DPS, 1, CELL) and left_basis.shape == (144, 288):
        return body_quick(*args)
    return body_plain(*args)


def solution(mesh):
    placed = (
        P(("group", "dp"), "tile", None, None, None),
        P(("group", "dp"), "tile", None, None, None),
        P("group", None),
        P("tile"),
        P("tile", None),
        P(("group", "tile"), None),
        P(("group", "tile"), "dp"),
        P("group", None),
        P("group", None),
        P(("group", "dp"), None),
        P(("group", "dp"), None),
    )
    return jax.shard_map(
        body,
        mesh=mesh,
        in_specs=placed,
        out_specs=(
            P(("group", "dp"), "tile", None, None, None),
            P(("group", "dp"), "tile", None, None, None),
            P("group", None),
            P(("group", "tile"), None),
            P(("group", "tile"), None),
            P("group", None),
            P("group", None),
            P(("group", "dp"), None),
            P(("group", "dp"), None),
            P(("group", "tile"), None),
        ),
        check_vma=False,
    )
```
